32 devices in a mesh: seq: 8 (over z, y), head: 4 (over x, core).
Axes of the slice: x: 2, y: 2, z: 4, core: 2. Of those that a mesh axis runs over, the one named last changes fastest.
Arguments:
- queries: bfloat16 [4096, 2048], P('seq', 'head'), may hold values from -8 to 8
- keys: bfloat16 [4096, 1024], P('seq', 'head'), may hold values from -8 to 8
- values: bfloat16 [4096, 1024], P('seq', 'head'), may hold values from -6 to 6
- output_gradient: bfloat16 [4096, 2048], P('seq', 'head'), may hold values from -6 to 6
- key_exponents: int32 [32, 8], P('seq', 'head'), may hold values from -1 to 1
- value_exponents: int32 [32, 8], P('seq', 'head'), may hold values from -1 to 1
- key_matrix: bfloat16 [5376, 1024], P(None, 'head'), may hold values from -0.1875 to 0.1875
- value_matrix: bfloat16 [5376, 1024], P(None, 'head'), may hold values from -0.1875 to 0.1875
Outputs:
- query_grad: bfloat16 [4096, 2048], P('seq', 'head')
- input_grad: bfloat16 [5376, 4096], P('head', 'seq')
The draws below stay inside these ranges and needn't reach their ends.
All inputs are finite; a program needn't handle non-finite values.
Results may differ from the reference program's by a relative error of at most 0.015.
Values may be sent and summed in bfloat16 or wider, within the bound.
A program may use at most 64 MiB of HBM per device.

```python
import math
import jax
import jax.numpy as jnp
from jax import lax

MODEL_WIDTH = 5376
QUERY_HEADS = 16
KEY_VALUE_HEADS = 8
HEAD_SIZE = 128
QUERY_SCALE = 168
ATTEND_WINDOW = 1024
SCALE_BLOCK = 128
SEQUENCE_TOKENS = 4096
N_HEAD = 4


def draw_queries(key, part):
    window_entries = jax.random.normal(jax.random.fold_in(key, 5), (SEQUENCE_TOKENS, QUERY_HEADS, HEAD_SIZE), jnp.float32)
    return jnp.clip(window_entries, -8.0, 8.0).reshape(SEQUENCE_TOKENS, QUERY_HEADS * HEAD_SIZE).astype(jnp.bfloat16)


def draw_keys(key, part):
    window_offsets = jax.random.normal(jax.random.fold_in(key, 7), (SEQUENCE_TOKENS // SCALE_BLOCK, KEY_VALUE_HEADS, HEAD_SIZE), jnp.float32)
    window_offsets = jnp.repeat(window_offsets, SCALE_BLOCK, axis=0)
    window_entries = jax.random.normal(jax.random.fold_in(key, 6), (SEQUENCE_TOKENS, KEY_VALUE_HEADS, HEAD_SIZE), jnp.float32) + window_offsets
    return jnp.clip(window_entries, -8.0, 8.0).reshape(SEQUENCE_TOKENS, KEY_VALUE_HEADS * HEAD_SIZE).astype(jnp.bfloat16)


def place_ends(values, stream_key, low, top_value):
    longest = values.shape.index(max(values.shape))
    spots = []
    for shift in (0, 1):
        where = [jax.random.randint(jax.random.fold_in(stream_key, axis), (), 0, length) for axis, length in enumerate(values.shape)]
        where[longest] = (where[longest] + shift) % values.shape[longest]
        spots.append(tuple(where))
    return values.at[spots[0]].set(low).at[spots[1]].set(top_value)


def level_of(key, dims, shards, low, top_value):
    def one(axis_at, shards_of):
        heights = jax.random.uniform(jax.random.fold_in(jax.random.fold_in(key, 6), axis_at), (shards_of,), jnp.float32, low / len(shards), top_value / len(shards))
        return jnp.repeat(jnp.exp(heights), dims[axis_at] // shards_of).reshape((-1,) + (1,) * (len(dims) - axis_at - 1))

    gain = one(*shards[0])
    for cut in shards[1:]:
        gain = gain * one(*cut)
    return gain


def centred(key, extent, scale, most, cuts=(), kind=jnp.bfloat16):
    entries = jax.random.normal(key, extent, jnp.float32) * scale
    if len(cuts) > 0:
        entries = level_of(key, extent, cuts, -0.22, 0.18) * entries
    return jnp.clip(entries, min=-most, max=most).astype(kind)


def setup_inputs(seed: int = 0) -> dict:
    arg_keys = jax.random.split(jax.random.key(seed), 9)
    return {
        "queries": draw_queries(jax.random.fold_in(arg_keys[8], 71), 0),
        "keys": draw_keys(jax.random.fold_in(arg_keys[8], 71), 0),
        "values": centred(arg_keys[2], (SEQUENCE_TOKENS, KEY_VALUE_HEADS * HEAD_SIZE), 1.0, 6.0, ((0, 8), (1, 4))),
        "output_gradient": centred(arg_keys[3], (SEQUENCE_TOKENS, QUERY_HEADS * HEAD_SIZE), 1.0, 6.0, ((0, 8), (1, 4))),
        "key_exponents": place_ends(jax.random.randint(arg_keys[4], (SEQUENCE_TOKENS // SCALE_BLOCK, KEY_VALUE_HEADS), -1, 2), jax.random.fold_in(arg_keys[4], 1), -1, 1).astype(jnp.int32),
        "value_exponents": place_ends(jax.random.randint(arg_keys[5], (SEQUENCE_TOKENS // SCALE_BLOCK, KEY_VALUE_HEADS), -1, 2), jax.random.fold_in(arg_keys[5], 1), -1, 1).astype(jnp.int32),
        "key_matrix": centred(arg_keys[6], (MODEL_WIDTH, KEY_VALUE_HEADS * HEAD_SIZE), (KEY_VALUE_HEADS * HEAD_SIZE) ** -0.5, 0.1875, ((1, 4),)),
        "value_matrix": centred(arg_keys[7], (MODEL_WIDTH, KEY_VALUE_HEADS * HEAD_SIZE), (KEY_VALUE_HEADS * HEAD_SIZE) ** -0.5, 0.1875, ((1, 4),)),
    }


def power_of_two(exponents):
    return jnp.where(exponents > 0, 2.0, jnp.where(exponents < 0, 0.5, 1.0)).astype(jnp.float32)


def reference(queries, keys, values, output_gradient, key_exponents, value_exponents, key_matrix, value_matrix):
    score_scale = QUERY_SCALE ** -0.5
    group_width = QUERY_HEADS // KEY_VALUE_HEADS
    key_multiplier = jnp.repeat(power_of_two(key_exponents), SCALE_BLOCK, axis=0)[:, :, None]
    value_multiplier = jnp.repeat(power_of_two(value_exponents), SCALE_BLOCK, axis=0)[:, :, None]
    exact_keys = (keys.astype(jnp.float32).reshape(SEQUENCE_TOKENS, KEY_VALUE_HEADS, HEAD_SIZE) * key_multiplier).astype(jnp.bfloat16)
    exact_values = (values.astype(jnp.float32).reshape(SEQUENCE_TOKENS, KEY_VALUE_HEADS, HEAD_SIZE) * value_multiplier).astype(jnp.bfloat16)
    running_sum = jnp.cumsum(exact_keys.astype(jnp.float32), axis=0)
    preceding = jnp.concatenate([jnp.zeros((ATTEND_WINDOW, KEY_VALUE_HEADS, HEAD_SIZE), jnp.float32), running_sum], 0)[:SEQUENCE_TOKENS]
    places = jnp.arange(SEQUENCE_TOKENS, dtype=jnp.int32)
    counts = jnp.minimum(places + 1, ATTEND_WINDOW).astype(jnp.float32)
    key_mean = (running_sum - preceding) / counts[:, None, None]
    smoothed_keys = (exact_keys.astype(jnp.float32) - key_mean).astype(jnp.bfloat16)

    block_rows = math.gcd(SEQUENCE_TOKENS, 512)
    key_padding = jnp.concatenate([jnp.zeros((ATTEND_WINDOW, KEY_VALUE_HEADS, HEAD_SIZE), jnp.bfloat16), smoothed_keys], 0)
    value_padding = jnp.concatenate([jnp.zeros((ATTEND_WINDOW, KEY_VALUE_HEADS, HEAD_SIZE), jnp.bfloat16), exact_values], 0)
    query_head_count = queries.reshape(SEQUENCE_TOKENS, KEY_VALUE_HEADS, group_width, HEAD_SIZE)
    gradient_heads = output_gradient.reshape(SEQUENCE_TOKENS, KEY_VALUE_HEADS, group_width, HEAD_SIZE)

    def one_block(block_index):
        begin_row = block_index * block_rows
        query_rows = lax.dynamic_slice_in_dim(query_head_count, begin_row, block_rows, 0).astype(jnp.float32)
        grad_rows = lax.dynamic_slice_in_dim(gradient_heads, begin_row, block_rows, 0).astype(jnp.float32)
        key_rows = lax.dynamic_slice_in_dim(key_padding, begin_row, block_rows + ATTEND_WINDOW, 0).astype(jnp.float32)
        value_rows = lax.dynamic_slice_in_dim(value_padding, begin_row, block_rows + ATTEND_WINDOW, 0).astype(jnp.float32)
        query_at = begin_row + jnp.arange(block_rows, dtype=jnp.int32)
        key_at = begin_row - ATTEND_WINDOW + jnp.arange(block_rows + ATTEND_WINDOW, dtype=jnp.int32)
        distance = query_at[:, None] - key_at[None, :]
        allowed = (distance >= 0) & (distance < ATTEND_WINDOW) & (key_at[None, :] >= 0)
        scores = jnp.einsum("qhgd,khd->hgqk", query_rows, key_rows) * score_scale
        scores = jnp.where(allowed, scores, -jnp.inf)
        highest = jnp.max(scores, axis=-1, keepdims=True)
        weights = jnp.exp(scores - highest)
        shares = weights / jnp.sum(weights, axis=-1, keepdims=True)
        rounded = lax.optimization_barrier(shares.astype(jnp.bfloat16)).astype(jnp.float32)
        attended = jnp.einsum("hgqk,khd->hgqd", rounded, value_rows)
        row_dot = jnp.einsum("hgqd,qhgd->hgq", attended, grad_rows)[..., None]
        share_grad = jnp.einsum("qhgd,khd->hgqk", grad_rows, value_rows)
        score_grad = lax.optimization_barrier((shares * (share_grad - row_dot)).astype(jnp.bfloat16)).astype(jnp.float32)
        query_part = (score_scale * jnp.einsum("hgqk,khd->qhgd", score_grad, key_rows)).astype(jnp.bfloat16)
        key_part = score_scale * jnp.einsum("hgqk,qhgd->khd", score_grad, query_rows)
        value_part = jnp.einsum("hgqk,qhgd->khd", rounded, grad_rows)
        return query_part, key_part, value_part

    def advance(carried, block_index):
        key_gradient_sum, value_gradient_sum = carried
        query_part, key_part, value_part = one_block(block_index)
        begin_row = block_index * block_rows
        key_gradient_sum = lax.dynamic_update_slice_in_dim(
            key_gradient_sum, lax.dynamic_slice_in_dim(key_gradient_sum, begin_row, block_rows + ATTEND_WINDOW, 0) + key_part, begin_row, 0)
        value_gradient_sum = lax.dynamic_update_slice_in_dim(
            value_gradient_sum, lax.dynamic_slice_in_dim(value_gradient_sum, begin_row, block_rows + ATTEND_WINDOW, 0) + value_part, begin_row, 0)
        return (key_gradient_sum, value_gradient_sum), query_part

    blank_rows = jnp.zeros((SEQUENCE_TOKENS + ATTEND_WINDOW, KEY_VALUE_HEADS, HEAD_SIZE), jnp.float32)
    (key_gradient_sum, value_gradient_sum), query_parts = lax.scan(
        advance, (blank_rows, blank_rows), jnp.arange(SEQUENCE_TOKENS // block_rows, dtype=jnp.int32))
    query_grad = query_parts.reshape(SEQUENCE_TOKENS, QUERY_HEADS * HEAD_SIZE)
    scaled_keys = (key_gradient_sum[ATTEND_WINDOW:] * key_multiplier).astype(jnp.bfloat16).reshape(SEQUENCE_TOKENS, KEY_VALUE_HEADS * HEAD_SIZE)
    scaled_values = (value_gradient_sum[ATTEND_WINDOW:] * value_multiplier).astype(jnp.bfloat16).reshape(SEQUENCE_TOKENS, KEY_VALUE_HEADS * HEAD_SIZE)

    group_members = KEY_VALUE_HEADS * HEAD_SIZE // N_HEAD
    summed = jnp.zeros((MODEL_WIDTH, SEQUENCE_TOKENS), jnp.float32)
    for group_index in range(N_HEAD):
        first_col = group_index * group_members
        last_col = first_col + group_members
        partial_value = jnp.dot(key_matrix[:, first_col:last_col], scaled_keys[:, first_col:last_col].T,
                          preferred_element_type=jnp.float32)
        partial_value = partial_value + jnp.dot(value_matrix[:, first_col:last_col], scaled_values[:, first_col:last_col].T,
                                    preferred_element_type=jnp.float32)
        summed = summed + lax.optimization_barrier(partial_value.astype(jnp.bfloat16)).astype(jnp.float32)
    return query_grad, summed.astype(jnp.bfloat16)
```

```python
import functools

import jax
import jax.numpy as jnp
from jax import lax
from jax.experimental import pallas as pl
from jax.experimental.pallas import tpu as pltpu
from jax.sharding import PartitionSpec as P

HEAD_SIZE = 128
QUERY_SCALE = 168
ATTEND_WINDOW = 1024
SCALE_BLOCK = 128
LOG2_E = 1.4426950408889634
MESH = pl.DeviceIdType.MESH
F32 = jnp.float32
BF16 = jnp.bfloat16
D = HEAD_SIZE
TILE = SCALE_BLOCK
SPAN = ATTEND_WINDOW + TILE
PIECES = 2
V, S = 0, 1
FAR, NEAR = 0, 1
OVER_Y, OVER_Z = 0, 1


def power_of_two(exponent):
    return jnp.where(exponent > 0, 2.0, jnp.where(exponent < 0, 0.5, 1.0)).astype(F32)


def contract_last(a, b):
    return lax.dot_general(a, b, (((1,), (1,)), ((), ())), preferred_element_type=F32)


def partner(h, t):
    other, bit = h, 1
    while bit <= t:
        if t & bit:
            other = other + bit - 2 * bit * lax.rem(lax.div(h, bit), 2)
        bit *= 2
    return other


def kernel(
    n, nh, q_ref, k_ref, v_ref, do_ref, ke_ref, ve_ref, wk_ref, wv_ref, dq_out, grad_rows,
    k_in, v_in, ke_in, ve_in, q_all, do_all, key_true, raw_far, own_sum, total_own, total_near, smooth, value, smooth_t,
    shares_all, score_all, far_grad, own_grad, grad_out, grad_in, scaled, gathered, weights, acc,
    dq_ref, out_ref, out_sem, in_sem, qd_sem, w_own, kf_send, kf_recv, t_send, t_recv, h_send, h_recv,
    w_send, w_recv, f_down, f_up, f_side, f_recv, c_send, c_recv, g_send, g_recv, s_send, s_recv,
):
    tokens = k_ref.shape[0]
    heads = k_ref.shape[1] // D
    group = q_ref.shape[1] // (heads * D)
    width = group * TILE
    tiles = tokens // TILE
    rows = grad_rows.shape[0]
    own = 2 * tokens
    scale = QUERY_SCALE ** (-0.5)
    b = lax.axis_index("seq")
    h = lax.axis_index("head")
    odd = lax.rem(b, 2) == 1
    even = lax.rem(b, 2) == 0
    colour = lax.rem(lax.rem(b, 2) + lax.div(b, 2), 2)
    crossing = list(range(2, nh))

    def cols(g):
        return slice(g * D, (g + 1) * D)

    loads = [
        pltpu.make_async_copy(k_ref, k_in, in_sem.at[0]),
        pltpu.make_async_copy(v_ref, v_in, in_sem.at[1]),
        pltpu.make_async_copy(ke_ref, ke_in, in_sem.at[2]),
        pltpu.make_async_copy(ve_ref, ve_in, in_sem.at[3]),
    ]
    for copy in loads:
        copy.start()
    head_loads = []
    for g in range(heads):
        for m, (ref, dst) in enumerate(((q_ref, q_all), (do_ref, do_all))):
            for i in range(tiles):
                for u in range(group):
                    head_loads.append(
                        pltpu.make_async_copy(
                            ref.at[i * TILE : (i + 1) * TILE, cols(g * group + u)],
                            dst.at[g, (i * group + u) * TILE : (i * group + u + 1) * TILE, :],
                            qd_sem.at[g, m, i * group + u],
                        )
                    )
    for copy in head_loads:
        copy.start()

    barrier = pltpu.get_barrier_semaphore()

    def greet(step):
        pl.semaphore_signal(
            barrier, inc=1, device_id={"seq": lax.rem(b + n + step, n)}, device_id_type=MESH
        )

    for step in (1, 2):
        pl.when(b + step < n)(lambda: greet(step))
        pl.when(b >= step)(lambda: greet(-step))
    for t in range(1, nh):
        pl.semaphore_signal(barrier, inc=1, device_id={"head": partner(h, t)}, device_id_type=MESH)
    greeted = nh - 1 + jnp.minimum(b, 2) + jnp.minimum(n - 1 - b, 2)

    def when(condition, action):
        pl.when(condition)(action)

    def along(src, dst, send, recv, step):
        return pltpu.make_async_remote_copy(
            src_ref=src, dst_ref=dst, send_sem=send, recv_sem=recv,
            device_id={"seq": lax.rem(b + n + step, n)}, device_id_type=MESH,
        )

    def across(src, dst, send, recv, t):
        return pltpu.make_async_remote_copy(
            src_ref=src, dst_ref=dst, send_sem=send, recv_sem=recv,
            device_id={"head": partner(h, t)}, device_id_type=MESH,
        )

    def when(condition, *steps):
        @pl.when(condition)
        def _():
            for step in steps:
                step()

    half = rows // 2
    part = half // 2
    chunks = [(t, m, q) for q in range(2) for t in crossing for m in range(2)]
    by_down = range(0, len(chunks) // 2)
    by_up = range(len(chunks) // 2, len(chunks) * 3 // 4)
    w_refs = (wk_ref, wv_ref)
    row_0 = b < 2
    row_1 = (b >= 2) & (b < 4)
    top = b + 2 >= n
    below_top = (b + 2 < n) & (b + 4 >= n)

    def held(t, m, q, side):
        return weights.at[t, m, pl.ds(side * half + q * part, part), :]

    def cross_copy(j):
        t, m, q = chunks[j]
        return across(
            w_refs[m].at[pl.ds(partner(h, t) * rows + colour * half + q * part, part), :],
            held(t, m, q, colour), w_send.at[j], w_recv.at[j], t,
        )

    def down_copy(j, side):
        ref = held(*chunks[j], side)
        return along(ref, ref, f_down.at[j], f_recv.at[j], -2)

    def up_copy(j):
        ref = held(*chunks[j], colour)
        return along(ref, ref, f_up.at[j], f_recv.at[j], 2)

    def side_copy(j):
        ref = held(*chunks[j], colour)
        return pltpu.make_async_remote_copy(
            src_ref=ref, dst_ref=ref, send_sem=f_side.at[j], recv_sem=f_recv.at[j],
            device_id={"seq": partner(b, 1)}, device_id_type=MESH,
        )

    def hand(j, action):
        if j in by_down:
            when(b >= 4, lambda: action(down_copy(j, colour)))
            when(below_top, lambda: action(up_copy(j)))
            when(row_0, lambda: action(side_copy(j)))
        elif j in by_up:
            when(b + 2 < n, lambda: action(up_copy(j)))
            when(row_1, lambda: action(down_copy(j, colour)))
        else:
            action(side_copy(j))

    def hand_on(j):
        cross_copy(j).wait_recv()
        hand(j, lambda copy: copy.start())

    core_copies = [
        across(ref.at[pl.ds(partner(h, 1) * rows, rows), :], weights.at[1, m], c_send.at[m], c_recv.at[m], 1)
        for m, ref in enumerate(w_refs)
    ]
    own_copies = [
        pltpu.make_async_copy(ref.at[pl.ds(h * rows, rows), :], weights.at[0, m], w_own.at[m])
        for m, ref in enumerate(w_refs)
    ]

    def key_copy(g):
        return along(key_true.at[g], raw_far.at[g], kf_send.at[g], kf_recv.at[g], 2)

    piece = tokens // PIECES
    halo_refs = (value, smooth)

    def slot(kind, g, base, p):
        return halo_refs[kind].at[g, base + p * piece : base + (p + 1) * piece]

    def far_copy(kind, g, p):
        at = (kind, g, p, FAR)
        return along(slot(kind, g, own, p), slot(kind, g, 0, p), h_send.at[at], h_recv.at[at], 2)

    def near_copy(kind, g, p):
        at = (kind, g, p, NEAR)
        return along(slot(kind, g, own, p), slot(kind, g, tokens, p), h_send.at[at], h_recv.at[at], 1)

    def relay_copy(kind, g, p):
        at = (kind, g, p, NEAR)
        return along(slot(kind, g, 0, p), slot(kind, g, tokens, p), h_send.at[at], h_recv.at[at], -1)

    def send_far(kind, g):
        for p in range(PIECES):
            when(b + 2 < n, lambda: far_copy(kind, g, p).start())

    def send_near(kind, g):
        for p in range(PIECES):
            when(even, lambda: near_copy(kind, g, p).start())

    def relay(kind, g):
        for p in range(PIECES):
            @pl.when(odd & (b >= 2))
            def _():
                far_copy(kind, g, p).wait_recv()
                relay_copy(kind, g, p).start()

    def await_halo(kind, g):
        for p in range(PIECES):
            when(even & (b >= 2), lambda: far_copy(kind, g, p).wait_recv())
            when(b >= 1, lambda: near_copy(kind, g, p).wait_recv())

    def near_sum():
        return along(total_own, total_near, t_send.at[0], t_recv.at[0], 1)

    def rows_of(p, base=0):
        return slice(base + p * piece, base + (p + 1) * piece)

    def grad_copy(m, g, over, p, step):
        at = (m, g, over, rows_of(p))
        return along(grad_out.at[at], grad_in.at[at], g_send.at[m, g, over, p], g_recv.at[m, g, over, p], step)

    def true_keys(g):
        for j in range(tiles):
            at = slice(j * TILE, (j + 1) * TILE)
            key_true[g, at] = (k_in[at, cols(g)].astype(F32) * power_of_two(ke_in[g : g + 1, j : j + 1])).astype(BF16)

    def true_values(g):
        for j in range(tiles):
            at = slice(j * TILE, (j + 1) * TILE)
            value[g, own + j * TILE : own + (j + 1) * TILE] = (
                v_in[at, cols(g)].astype(F32) * power_of_two(ve_in[g : g + 1, j : j + 1])
            ).astype(BF16)

    def sum_keys():
        for g in range(heads):
            total_own[:, cols(g)] = jnp.broadcast_to(
                jnp.sum(key_true[g].astype(F32), axis=0, keepdims=True), (8, D)
            )
        when(b + 1 < n, lambda: near_sum().start())

    def clear():
        @pl.when(b < 1)
        def _():
            total_near[...] = jnp.zeros_like(total_near)
            for g in range(heads):
                value[g, tokens:own, :] = jnp.zeros((tokens, D), BF16)
                smooth[g, tokens:own, :] = jnp.zeros((tokens, D), BF16)

        @pl.when(b < 2)
        def _():
            raw_far[...] = jnp.zeros_like(raw_far)
            for g in range(heads):
                value[g, 0:tokens, :] = jnp.zeros((tokens, D), BF16)
                smooth[g, 0:tokens, :] = jnp.zeros((tokens, D), BF16)
                for m in range(2):
                    grad_in[m, g, OVER_Y] = jnp.zeros((tokens, D), BF16)

        @pl.when(top)
        def _():
            for g in range(heads):
                for m in range(2):
                    grad_in[m, g, OVER_Z] = jnp.zeros((tokens, D), BF16)

        blank = jnp.zeros((TILE, width), BF16)
        for ref in (shares_all, score_all):
            for g in range(heads):
                for i in range(0, tiles, 2):
                    ref[g, i * TILE : (i + 1) * TILE, (i + 1) * width : (i + 2) * width] = blank
                    ref[g, own + (i + 1) * TILE : own + (i + 2) * TILE, i * width : (i + 1) * width] = blank

    row_at = lax.broadcasted_iota(jnp.int32, (tokens, tokens), 0)
    col_at = lax.broadcasted_iota(jnp.int32, (tokens, tokens), 1)
    lower = jnp.where(row_at >= col_at, 1.0, 0.0).astype(BF16)
    place = b * tokens + lax.broadcasted_iota(jnp.int32, (tokens, 1), 0)
    counts = jnp.clip(place + 1, 1, ATTEND_WINDOW).astype(F32)

    def running_keys(g):
        own_sum[g] = jnp.dot(lower, key_true[g], preferred_element_type=F32)

    def smooth_keys(g):
        when(b >= 2, lambda: key_copy(g).wait_recv())
        far = jnp.dot(lower, raw_far[g], preferred_element_type=F32)
        mean = (own_sum[g] - far + far[tokens - 1 :, :] + total_near[0:1, cols(g)]) / counts
        smooth[g, own : own + tokens, :] = (key_true[g].astype(F32) - mean).astype(BF16)
        send_far(S, g)
        send_near(S, g)

    near_row = lax.broadcasted_iota(jnp.int32, (TILE, width), 0)
    lane = lax.rem(lax.broadcasted_iota(jnp.int32, (1, width), 1), TILE)

    def attend(g):
        def one_tile(i, carry):
            begin = pl.multiple_of(i * TILE, TILE)
            window = pl.ds(begin, SPAN)
            lanes = pl.ds(pl.multiple_of(i * width, width), width)
            scores = contract_last(smooth[g, window, :], q_all[g, lanes, :])
            blocks = []
            for j in range(SPAN // TILE):
                block = scores[j * TILE : (j + 1) * TILE]
                if j == 0:
                    block = jnp.where(near_row > lane, block, -jnp.inf)
                if j == ATTEND_WINDOW // TILE:
                    block = jnp.where(near_row <= lane, block, -jnp.inf)
                else:
                    block = jnp.where(i + j >= (2 - b) * tiles, block, -jnp.inf)
                blocks.append(block)
            scores = jnp.concatenate(blocks, 0)
            highest = jnp.max(scores, axis=0, keepdims=True)
            powers = jnp.exp2((scores - highest) * (scale * LOG2_E))
            shares = powers * (1.0 / jnp.sum(powers, axis=0, keepdims=True))
            shares_all[g, window, lanes] = shares.astype(BF16)
            return carry

        lax.fori_loop(0, tiles, one_tile, 0)

    def differentiate(g):
        def one_tile(i, carry):
            begin = pl.multiple_of(i * TILE, TILE)
            window = pl.ds(begin, SPAN)
            lanes = pl.ds(pl.multiple_of(i * width, width), width)
            share_grad = contract_last(value[g, window, :], do_all[g, lanes, :])
            shares = shares_all[g, window, lanes].astype(F32)
            row_dot = jnp.sum(shares * share_grad, axis=0, keepdims=True)
            score_all[g, window, lanes] = (shares * (share_grad - row_dot)).astype(BF16)
            return carry

        lax.fori_loop(0, tiles, one_tile, 0)

    def key_grads(m, g, at, lanes):
        if m == 0:
            return jnp.dot(score_all[g, at, lanes], q_all[g, lanes, :], preferred_element_type=F32) * scale
        return jnp.dot(shares_all[g, at, lanes], do_all[g, lanes, :], preferred_element_type=F32)

    def near_grads(m, g):
        for p in range(PIECES):
            grads = key_grads(m, g, rows_of(p, tokens), slice(0, group * tokens))
            grad_out[m, g, OVER_Y, rows_of(p)] = grads.astype(BF16)

    def send_near_grads(m, g):
        for p in range(PIECES):
            when(even & (b >= 2), lambda: grad_copy(m, g, OVER_Y, p, 1).start())
            when(odd, lambda: grad_copy(m, g, OVER_Y, p, -1).start())

    def far_grads(m, g):
        for p in range(PIECES):
            grads = key_grads(m, g, rows_of(p), slice(0, (p + 1) * group * piece))
            far_grad[m, g, rows_of(p)] = grads

            @pl.when(even & (b >= 2))
            def _():
                grad_out[m, g, OVER_Z, rows_of(p)] = far_grad[m, g, rows_of(p)].astype(BF16)
                grad_copy(m, g, OVER_Z, p, -2).start()

    def join_grads(m, g):
        for p in range(PIECES):
            @pl.when(odd & (b >= 2))
            def _():
                grad_copy(m, g, OVER_Y, p, 1).wait_recv()
                both = far_grad[m, g, rows_of(p)] + grad_in[m, g, OVER_Y, rows_of(p)].astype(F32)
                grad_out[m, g, OVER_Z, rows_of(p)] = both.astype(BF16)
                grad_copy(m, g, OVER_Z, p, -2).start()

    def own_grads(m, g):
        for p in range(PIECES):
            own_grad[m, g, rows_of(p)] = key_grads(
                m, g, rows_of(p, own), slice(p * group * piece, group * tokens)
            )

    def query_grads(g):
        smooth_t[...] = smooth[g].astype(F32).T.astype(BF16)
        for i in range(tiles):
            window = slice(i * TILE, i * TILE + SPAN)
            dq = jnp.dot(
                smooth_t[:, window], score_all[g, window, i * width : (i + 1) * width],
                preferred_element_type=F32,
            ) * scale
            dq = dq.T.astype(BF16)
            for u in range(group):
                dq_ref[i * TILE : (i + 1) * TILE, cols(g * group + u)] = dq[u * TILE : (u + 1) * TILE]

    def share_copy(m, g, p, t):
        return across(
            scaled.at[m, g, rows_of(p)], gathered.at[t - 1, m, g, rows_of(p)],
            s_send.at[t - 1, m, g, p], s_recv.at[t - 1, m, g, p], t,
        )

    def onward_copy(m, g, p, t):
        return across(
            gathered.at[t - 1, m, g, rows_of(p)], gathered.at[t, m, g, rows_of(p)],
            s_send.at[t, m, g, p], s_recv.at[t, m, g, p], 1,
        )

    far_steps = list(range(2, nh, 2))

    def finish(m, g):
        exponent = (ke_in, ve_in)[m]
        for p in range(PIECES):
            when(even, lambda: grad_copy(m, g, OVER_Y, p, -1).wait_recv())
            when(b + 2 < n, lambda: grad_copy(m, g, OVER_Z, p, -2).wait_recv())
            for r in range(p * tiles // PIECES, (p + 1) * tiles // PIECES):
                at = slice(r * TILE, (r + 1) * TILE)
                whole = own_grad[m, g, at] + grad_in[m, g, OVER_Z, at].astype(F32)
                whole = whole + jnp.where(even, grad_in[m, g, OVER_Y, at].astype(F32), 0.0)
                scaled[m, g, at] = (whole * power_of_two(exponent[g : g + 1, r : r + 1])).astype(BF16)
            for t in far_steps + [1]:
                share_copy(m, g, p, t).start()

    def pass_on(m, g):
        for p in range(PIECES):
            for t in far_steps:
                share_copy(m, g, p, t).wait_recv()
                onward_copy(m, g, p, t).start()

    def await_core(g):
        for m in range(2):
            for p in range(PIECES):
                share_copy(m, g, p, 1).wait_recv()

    def await_onward(g):
        for m in range(2):
            for p in range(PIECES):
                for t in far_steps:
                    onward_copy(m, g, p, t).wait_recv()

    chunk = rows // 4

    def row_copy(c):
        at = pl.ds(pl.multiple_of(c * chunk, 16), chunk)
        return pltpu.make_async_copy(out_ref.at[at, :], grad_rows.at[at, :], out_sem.at[c])

    def query_copy():
        return pltpu.make_async_copy(dq_ref, dq_out, out_sem.at[4])

    def product(ts, g, fresh, last):
        def one_chunk(c, carry):
            at = pl.ds(pl.multiple_of(c * chunk, 16), chunk)
            total = None if fresh else acc[at, :]
            for t in ts:
                left = jnp.concatenate([weights[t, 0, at, cols(g)], weights[t, 1, at, cols(g)]], 1)
                if t == 0:
                    right = jnp.concatenate([scaled[0, g], scaled[1, g]], 1)
                else:
                    right = jnp.concatenate([gathered[t - 1, 0, g], gathered[t - 1, 1, g]], 1)
                term = contract_last(left, right)
                total = term if total is None else total + term
            if last:
                out_ref[at, :] = total.astype(BF16)
                row_copy(c).start()
            else:
                acc[at, :] = total
            return carry

        lax.fori_loop(0, 4, one_chunk, 0)

    pl.semaphore_wait(barrier, greeted)
    for copy in loads: copy.wait()
    for j in range(len(chunks)): cross_copy(j).start()
    for g in range(heads): true_keys(g)
    sum_keys()
    for g in range(heads): when(b + 2 < n, lambda: key_copy(g).start())
    for g in range(heads):
        true_values(g)
        send_near(V, g)
    for copy in core_copies + own_copies: copy.start()
    clear()
    for g in range(heads): running_keys(g)
    when(b >= 1, lambda: near_sum().wait_recv())
    smooth_keys(0)
    smooth_keys(1)
    for g in range(heads): send_far(V, g)
    for copy in head_loads: copy.wait()
    hand_on(0)
    relay(S, 0)
    await_halo(S, 0)
    attend(0)
    relay(S, 1)
    hand_on(1)
    await_halo(S, 1)
    attend(1)
    relay(V, 0)
    hand_on(2)
    near_grads(1, 0)
    near_grads(1, 1)
    relay(V, 1)
    send_near_grads(1, 0)
    send_near_grads(1, 1)
    far_grads(1, 0)
    far_grads(1, 1)
    hand_on(3)
    await_halo(V, 0)
    differentiate(0)
    near_grads(0, 0)
    send_near_grads(0, 0)
    far_grads(0, 0)
    hand_on(4)
    await_halo(V, 1)
    differentiate(1)
    near_grads(0, 1)
    send_near_grads(0, 1)
    join_grads(1, 0)
    far_grads(0, 1)
    own_grads(1, 0)
    join_grads(1, 1)
    hand_on(5)
    own_grads(1, 1)
    own_grads(0, 0)
    own_grads(0, 1)
    join_grads(0, 0)
    finish(1, 0)
    hand_on(6)
    query_grads(0)
    join_grads(0, 1)
    finish(1, 1)
    finish(0, 0)
    hand_on(7)
    for copy in own_copies: copy.wait()
    for copy in core_copies: copy.wait_recv()
    await_core(0)
    product((0, 1), 0, True, False)
    finish(0, 1)
    query_grads(1)
    query_copy().start()
    for m in (1, 0): pass_on(m, 0)
    await_core(1)
    product((0, 1), 1, False, False)
    for j in range(len(chunks)): down_copy(j, 1 - colour).wait_recv()
    await_onward(0)
    product(crossing, 0, False, False)
    for m in (1, 0): pass_on(m, 1)
    await_onward(1)
    product(crossing, 1, False, True)

    query_copy().wait()
    for c in range(4):
        row_copy(c).wait()
    when(b + 1 < n, lambda: near_sum().wait_send())
    for g in range(heads):
        when(b + 2 < n, lambda: key_copy(g).wait_send())
        for p in range(PIECES):
            for kind in (V, S):
                when(b + 2 < n, lambda: far_copy(kind, g, p).wait_send())
                when(even | (b >= 2), lambda: near_copy(kind, g, p).wait_send())
            for m in range(2):
                when(odd | (b >= 2), lambda: grad_copy(m, g, OVER_Y, p, 1).wait_send())
                when(b >= 2, lambda: grad_copy(m, g, OVER_Z, p, -2).wait_send())
                for t in far_steps + [1]:
                    share_copy(m, g, p, t).wait_send()
                for t in far_steps:
                    onward_copy(m, g, p, t).wait_send()
    for j in range(len(chunks)):
        cross_copy(j).wait_send()
        hand(j, lambda copy: copy.wait_send())
    for copy in core_copies:
        copy.wait_send()


def solution(mesh):
    n, nh = mesh.shape["seq"], mesh.shape["head"]
    assert n % 2 == 0 and n >= 4

    def local(q, k, v, do, ke, ve, wk, wv):
        tokens, width = k.shape
        heads = width // HEAD_SIZE
        group = q.shape[1] // width
        tiles = tokens // TILE
        assert ATTEND_WINDOW == 2 * tokens
        rows = wk.shape[0] // nh
        n_chunks = 4 * (nh - 2)
        hbm = pl.BlockSpec(memory_space=pltpu.HBM)
        dma = pltpu.SemaphoreType.DMA
        return pl.pallas_call(
            functools.partial(kernel, n, nh),
            out_shape=(
                pltpu.VMEM(q.shape, BF16),
                pltpu.VMEM((rows, tokens), BF16),
            ),
            in_specs=[hbm] * 8,
            out_specs=(pl.BlockSpec(memory_space=pl.ANY),) * 2,
            scratch_shapes=[
                pltpu.VMEM((tokens, width), BF16),
                pltpu.VMEM((tokens, width), BF16),
                pltpu.VMEM((heads, tiles), jnp.int32),
                pltpu.VMEM((heads, tiles), jnp.int32),
                pltpu.VMEM((heads, group * tokens, D), BF16),
                pltpu.VMEM((heads, group * tokens, D), BF16),
                pltpu.VMEM((heads, tokens, D), BF16),
                pltpu.VMEM((heads, tokens, D), BF16),
                pltpu.VMEM((heads, tokens, D), F32),
                pltpu.VMEM((8, width), F32),
                pltpu.VMEM((8, width), F32),
                pltpu.VMEM((heads, 3 * tokens, D), BF16),
                pltpu.VMEM((heads, 3 * tokens, D), BF16),
                pltpu.VMEM((D, 3 * tokens), BF16),
                pltpu.VMEM((heads, 3 * tokens, group * tokens), BF16),
                pltpu.VMEM((heads, 3 * tokens, group * tokens), BF16),
                pltpu.VMEM((2, heads, tokens, D), F32),
                pltpu.VMEM((2, heads, tokens, D), F32),
                pltpu.VMEM((2, heads, 2, tokens, D), BF16),
                pltpu.VMEM((2, heads, 2, tokens, D), BF16),
                pltpu.VMEM((2, heads, tokens, D), BF16),
                pltpu.VMEM((nh - 1, 2, heads, tokens, D), BF16),
                pltpu.VMEM((nh, 2, rows, width), BF16),
                pltpu.VMEM((rows, tokens), F32),
                pltpu.VMEM(q.shape, BF16),
                pltpu.VMEM((rows, tokens), BF16),
                dma((5,)),
                dma((4,)), dma((heads, 2, group * tiles)), dma((2,)),
                dma((heads,)), dma((heads,)), dma((1,)), dma((1,)),
                dma((2, heads, PIECES, 2)), dma((2, heads, PIECES, 2)),
                dma((n_chunks,)), dma((n_chunks,)),
                dma((n_chunks,)), dma((n_chunks,)), dma((n_chunks,)), dma((n_chunks,)),
                dma((2,)), dma((2,)),
                dma((2, heads, 2, PIECES)), dma((2, heads, 2, PIECES)),
                dma((nh - 1, 2, heads, PIECES)), dma((nh - 1, 2, heads, PIECES)),
            ],
            compiler_params=pltpu.CompilerParams(
                collective_id=0, has_side_effects=True, vmem_limit_bytes=48 * 2**20
            ),
        )(*[pltpu.with_memory_space_constraint(x, pltpu.HBM) for x in (q, k, v, do, ke.T, ve.T, wk, wv)])

    in_specs = (P("seq", "head"),) * 6 + (P(None, "head"),) * 2
    out_specs = (P("seq", "head"), P("head", "seq"))
    return jax.shard_map(local, mesh=mesh, in_specs=in_specs, out_specs=out_specs, check_vma=False)
```

```python
import functools

import jax
import jax.numpy as jnp
from jax import lax
from jax.experimental import pallas as pl
from jax.experimental.pallas import tpu as pltpu
from jax.sharding import PartitionSpec as P

HEAD_SIZE = 128
QUERY_SCALE = 168
ATTEND_WINDOW = 1024
SCALE_BLOCK = 128
LOG2_E = 1.4426950408889634
LOWEST = -1e30
MESH = pl.DeviceIdType.MESH
F32 = jnp.float32
BF16 = jnp.bfloat16
D = HEAD_SIZE
TILE = SCALE_BLOCK
SPAN = ATTEND_WINDOW + TILE
PIECES = 2
V, S = 0, 1
FAR, NEAR = 0, 1
OVER_Y, OVER_Z = 0, 1


def power_of_two(exponent):
    return jnp.where(exponent > 0, 2.0, jnp.where(exponent < 0, 0.5, 1.0)).astype(F32)


def contract_last(a, b):
    return lax.dot_general(a, b, (((1,), (1,)), ((), ())), preferred_element_type=F32)


def partner(h, t):
    other, bit = h, 1
    while bit <= t:
        if t & bit:
            other = other + bit - 2 * bit * lax.rem(lax.div(h, bit), 2)
        bit *= 2
    return other


def kernel(
    n, nh, q_ref, k_ref, v_ref, do_ref, ke_ref, ve_ref, wk_ref, wv_ref, dq_out, grad_rows,
    k_in, v_in, ke_in, ve_in, q_all, do_all, key_true, raw_far, own_sum, total_own, total_near, smooth, value, smooth_t,
    shares_all, score_all, stats, do_part, far_grad, own_grad, grad_out, grad_in, scaled, gathered, weights, acc,
    dq_ref, out_ref, out_sem, in_sem, qd_sem, w_own, kf_send, kf_recv, t_send, t_recv, h_send, h_recv,
    w_send, w_recv, f_send, f_recv, c_send, c_recv, g_send, g_recv, s_send, s_recv,
):
    tokens = k_ref.shape[0]
    heads = k_ref.shape[1] // D
    group = q_ref.shape[1] // (heads * D)
    width = group * TILE
    tiles = tokens // TILE
    rows = grad_rows.shape[0]
    own = 2 * tokens
    scale = QUERY_SCALE ** (-0.5)
    b = lax.axis_index("seq")
    h = lax.axis_index("head")
    odd = lax.rem(b, 2) == 1
    even = lax.rem(b, 2) == 0
    colour = lax.rem(lax.rem(b, 2) + lax.div(b, 2), 2)
    crossing = list(range(2, nh))

    def cols(g):
        return slice(g * D, (g + 1) * D)

    loads = [
        pltpu.make_async_copy(k_ref, k_in, in_sem.at[0]),
        pltpu.make_async_copy(v_ref, v_in, in_sem.at[1]),
        pltpu.make_async_copy(ke_ref, ke_in, in_sem.at[2]),
        pltpu.make_async_copy(ve_ref, ve_in, in_sem.at[3]),
    ]
    for copy in loads:
        copy.start()
    head_loads = []
    for g in range(heads):
        for m, (ref, dst) in enumerate(((q_ref, q_all), (do_ref, do_all))):
            for i in range(tiles):
                for u in range(group):
                    head_loads.append(
                        pltpu.make_async_copy(
                            ref.at[i * TILE : (i + 1) * TILE, cols(g * group + u)],
                            dst.at[g, (i * group + u) * TILE : (i * group + u + 1) * TILE, :],
                            qd_sem.at[g, m],
                        )
                    )
    for copy in head_loads:
        copy.start()

    barrier = pltpu.get_barrier_semaphore()

    def greet(step):
        pl.semaphore_signal(
            barrier, inc=1, device_id={"seq": lax.rem(b + n + step, n)}, device_id_type=MESH
        )

    for step in (1, 2):
        pl.when(b + step < n)(lambda: greet(step))
        pl.when(b >= step)(lambda: greet(-step))
    for t in range(1, nh):
        pl.semaphore_signal(barrier, inc=1, device_id={"head": partner(h, t)}, device_id_type=MESH)
    greeted = nh - 1 + jnp.minimum(b, 2) + jnp.minimum(n - 1 - b, 2)

    def when(condition, action):
        pl.when(condition)(action)

    def along(src, dst, send, recv, step):
        return pltpu.make_async_remote_copy(
            src_ref=src, dst_ref=dst, send_sem=send, recv_sem=recv,
            device_id={"seq": lax.rem(b + n + step, n)}, device_id_type=MESH,
        )

    def across(src, dst, send, recv, t):
        return pltpu.make_async_remote_copy(
            src_ref=src, dst_ref=dst, send_sem=send, recv_sem=recv,
            device_id={"head": partner(h, t)}, device_id_type=MESH,
        )

    def when(condition, *steps):
        @pl.when(condition)
        def _():
            for step in steps:
                step()

    half = rows // 2
    part = half // 2
    chunks = [(t, m, q) for q in range(2) for t in crossing for m in range(2)]
    by_down = range(0, len(chunks) // 2)
    by_up = range(len(chunks) // 2, len(chunks) * 3 // 4)
    late = len(chunks) - 2
    w_refs = (wk_ref, wv_ref)
    row_0 = b < 2
    row_1 = (b >= 2) & (b < 4)
    top = b + 2 >= n
    below_top = (b + 2 < n) & (b + 4 >= n)

    def held(t, m, q, side):
        return weights.at[t, m, pl.ds(side * half + q * part, part), :]

    def cross_copy(j):
        t, m, q = chunks[j]
        return across(
            w_refs[m].at[pl.ds(partner(h, t) * rows + colour * half + q * part, part), :],
            held(t, m, q, colour), w_send.at[0], w_recv.at[j], t,
        )

    def down_copy(j, side):
        ref = held(*chunks[j], side)
        return along(ref, ref, f_send.at[j, 0], f_recv.at[j], -2)

    def up_copy(j):
        ref = held(*chunks[j], colour)
        return along(ref, ref, f_send.at[j, 1], f_recv.at[j], 2)

    def side_copy(j):
        ref = held(*chunks[j], colour)
        return pltpu.make_async_remote_copy(
            src_ref=ref, dst_ref=ref, send_sem=f_send.at[j, 0], recv_sem=f_recv.at[j],
            device_id={"seq": partner(b, 1)}, device_id_type=MESH,
        )

    def hand(j, action):
        if j in by_down:
            when(b >= 4, lambda: action(down_copy(j, colour)))
            when(below_top, lambda: action(up_copy(j)))
            when(row_0, lambda: action(side_copy(j)))
        elif j in by_up:
            when(b + 2 < n, lambda: action(up_copy(j)))
            if j == by_up[0]:
                when(row_1, lambda: action(down_copy(j, colour)))
            else:
                when(row_0, lambda: action(side_copy(j)))
        elif j == late:
            when(b >= 2, lambda: action(side_copy(j)))
        else:
            action(side_copy(j))

    def hand_late(action):
        ref = held(*chunks[late], colour)
        when(row_1, lambda: action(along(ref, ref, f_send.at[late, 1], f_recv.at[late], -2)))

    def hand_on(j):
        cross_copy(j).wait_recv()
        hand(j, lambda copy: copy.start())

    core_copies = [
        across(ref.at[pl.ds(partner(h, 1) * rows, rows), :], weights.at[1, m], c_send.at[m], c_recv.at[m], 1)
        for m, ref in enumerate(w_refs)
    ]
    own_copies = [
        pltpu.make_async_copy(ref.at[pl.ds(h * rows, rows), :], weights.at[0, m], w_own.at[m])
        for m, ref in enumerate(w_refs)
    ]

    def key_copy(g):
        return along(key_true.at[g], raw_far.at[g], kf_send.at[g], kf_recv.at[g], 2)

    piece = tokens // PIECES
    halo_refs = (value, smooth)

    def slot(kind, g, base, p):
        return halo_refs[kind].at[g, base + p * piece : base + (p + 1) * piece]

    def far_copy(kind, g, p):
        at = (kind, g, p, FAR)
        return along(slot(kind, g, own, p), slot(kind, g, 0, p), h_send.at[FAR], h_recv.at[at], 2)

    def near_copy(kind, g, p):
        at = (kind, g, p, NEAR)
        return along(slot(kind, g, own, p), slot(kind, g, tokens, p), h_send.at[NEAR], h_recv.at[at], 1)

    def relay_copy(kind, g, p):
        at = (kind, g, p, NEAR)
        return along(slot(kind, g, 0, p), slot(kind, g, tokens, p), h_send.at[NEAR], h_recv.at[at], -1)

    def send_far(kind, g):
        for p in range(PIECES):
            when(b + 2 < n, lambda: far_copy(kind, g, p).start())

    def send_near(kind, g):
        for p in range(PIECES):
            when(even, lambda: near_copy(kind, g, p).start())

    def relay(kind, g):
        for p in range(PIECES):
            @pl.when(odd & (b >= 2))
            def _():
                far_copy(kind, g, p).wait_recv()
                relay_copy(kind, g, p).start()

    def await_far(kind, g):
        for p in range(PIECES):
            when(even & (b >= 2), lambda: far_copy(kind, g, p).wait_recv())

    def await_near(kind, g):
        for p in range(PIECES):
            when(b >= 1, lambda: near_copy(kind, g, p).wait_recv())

    def near_sum():
        return along(total_own, total_near, t_send.at[0], t_recv.at[0], 1)

    def await_heads(g):
        for m, ref in enumerate((q_all, do_all)):
            pltpu.make_async_copy(ref.at[g], ref.at[g], qd_sem.at[g, m]).wait()

    def rows_of(p, base=0):
        return slice(base + p * piece, base + (p + 1) * piece)

    def grad_copy(m, g, over, p, step):
        at = (m, g, over, rows_of(p))
        return along(grad_out.at[at], grad_in.at[at], g_send.at[over], g_recv.at[m, g, over, p], step)

    def true_keys(g):
        for j in range(tiles):
            at = slice(j * TILE, (j + 1) * TILE)
            key_true[g, at] = (k_in[at, cols(g)].astype(F32) * power_of_two(ke_in[g : g + 1, j : j + 1])).astype(BF16)

    def true_values(g):
        for j in range(tiles):
            at = slice(j * TILE, (j + 1) * TILE)
            value[g, own + j * TILE : own + (j + 1) * TILE] = (
                v_in[at, cols(g)].astype(F32) * power_of_two(ve_in[g : g + 1, j : j + 1])
            ).astype(BF16)

    def sum_keys():
        for g in range(heads):
            total_own[:, cols(g)] = jnp.broadcast_to(
                jnp.sum(key_true[g].astype(F32), axis=0, keepdims=True), (8, D)
            )
        when(b + 1 < n, lambda: near_sum().start())

    def clear():
        @pl.when(b < 1)
        def _():
            total_near[...] = jnp.zeros_like(total_near)
            for g in range(heads):
                value[g, tokens:own, :] = jnp.zeros((tokens, D), BF16)
                smooth[g, tokens:own, :] = jnp.zeros((tokens, D), BF16)

        @pl.when(b < 2)
        def _():
            raw_far[...] = jnp.zeros_like(raw_far)
            for g in range(heads):
                value[g, 0:tokens, :] = jnp.zeros((tokens, D), BF16)
                smooth[g, 0:tokens, :] = jnp.zeros((tokens, D), BF16)
                for m in range(2):
                    grad_in[m, g, OVER_Y] = jnp.zeros((tokens, D), BF16)

        @pl.when(top)
        def _():
            for g in range(heads):
                for m in range(2):
                    grad_in[m, g, OVER_Z] = jnp.zeros((tokens, D), BF16)

        blank = jnp.zeros((TILE, width), BF16)
        for ref in (shares_all, score_all):
            for g in range(heads):
                for i in range(0, tiles, 2):
                    ref[g, i * TILE : (i + 1) * TILE, (i + 1) * width : (i + 2) * width] = blank
                    ref[g, own + (i + 1) * TILE : own + (i + 2) * TILE, i * width : (i + 1) * width] = blank

    row_at = lax.broadcasted_iota(jnp.int32, (tokens, tokens), 0)
    col_at = lax.broadcasted_iota(jnp.int32, (tokens, tokens), 1)
    lower = jnp.where(row_at >= col_at, 1.0, 0.0).astype(BF16)
    place = b * tokens + lax.broadcasted_iota(jnp.int32, (tokens, 1), 0)
    counts = jnp.clip(place + 1, 1, ATTEND_WINDOW).astype(F32)

    def running_keys(g):
        own_sum[g] = jnp.dot(lower, key_true[g], preferred_element_type=F32)

    def smooth_keys(g):
        when(b >= 2, lambda: key_copy(g).wait_recv())
        far = jnp.dot(lower, raw_far[g], preferred_element_type=F32)
        mean = (own_sum[g] - far + far[tokens - 1 :, :] + total_near[0:1, cols(g)]) / counts
        smooth[g, own : own + tokens, :] = (key_true[g].astype(F32) - mean).astype(BF16)
        send_far(S, g)
        send_near(S, g)

    row = lax.broadcasted_iota(jnp.int32, (TILE, width), 0)
    lane = lax.rem(lax.broadcasted_iota(jnp.int32, (1, width), 1), TILE)
    unit = jnp.where(
        lax.broadcasted_iota(jnp.int32, (TILE, TILE), 0) == lax.broadcasted_iota(jnp.int32, (TILE, TILE), 1), 1.0, 0.0
    )

    def lanes_of(i):
        return slice(i * width, (i + 1) * width)

    def keys_of(part, i):
        return (slice(i * TILE, tokens), slice(tokens, own), slice(own, own + (i + 1) * TILE))[part]

    def attend(g, part):
        for i in range(tiles):
            at, lanes = keys_of(part, i), lanes_of(i)
            scores = contract_last(smooth[g, at, :], q_all[g, lanes, :])
            if part == 0:
                edge = jnp.where(row > lane, scores[:TILE], -jnp.inf)
                scores = edge if i == tiles - 1 else jnp.concatenate([edge, scores[TILE:]], 0)
            if part == 2:
                edge = jnp.where(row <= lane, scores[i * TILE :], -jnp.inf)
                scores = edge if i == 0 else jnp.concatenate([scores[: i * TILE], edge], 0)
            highest = jnp.maximum(jnp.max(scores, axis=0, keepdims=True), LOWEST)
            powers = jnp.exp2((scores - highest) * (scale * LOG2_E))
            shares_all[g, at, lanes] = powers.astype(BF16)
            stats[g, part, 0:1, lanes] = highest
            stats[g, part, 1:2, lanes] = jnp.sum(powers, axis=0, keepdims=True)

    def combine(g):
        present = (b >= 2, b >= 1, b >= 0)
        tops = [jnp.where(here, stats[g, part, 0:1, :], LOWEST) for part, here in enumerate(present)]
        highest = jnp.maximum(jnp.maximum(tops[0], tops[1]), tops[2])
        powers = [
            jnp.where(here, jnp.exp2((top - highest) * (scale * LOG2_E)), 0.0) for top, here in zip(tops, present)
        ]
        total = sum(power * stats[g, part, 1:2, :] for part, power in enumerate(powers))
        inverse = 1.0 / total
        for part in range(3):
            factor = powers[part] * inverse
            stats[g, part, 0:1, :] = factor.astype(BF16).astype(F32)
            for k in range(group * tiles):
                at = slice(k * TILE, (k + 1) * TILE)
                spread = (unit * factor[:, at]).astype(BF16)
                do_part[g, part, at, :] = jnp.dot(
                    spread, do_all[g, at, :], preferred_element_type=F32
                ).astype(BF16)

    def differentiate(g):
        for i in range(tiles):
            lanes = lanes_of(i)
            row_dot, parts = 0.0, []
            for part in range(3):
                at = keys_of(part, i)
                share_grad = contract_last(value[g, at, :], do_part[g, part, lanes, :])
                shares = shares_all[g, at, lanes].astype(F32)
                row_dot = row_dot + jnp.sum(shares * share_grad, axis=0, keepdims=True)
                parts.append((at, shares, share_grad))
            for part, (at, shares, share_grad) in enumerate(parts):
                shift = row_dot * stats[g, part, 0:1, lanes]
                score_all[g, at, lanes] = (shares * (share_grad - shift)).astype(BF16)

    def key_grads(m, g, part, at, lanes):
        if m == 0:
            return jnp.dot(score_all[g, at, lanes], q_all[g, lanes, :], preferred_element_type=F32) * scale
        return jnp.dot(shares_all[g, at, lanes], do_part[g, part, lanes, :], preferred_element_type=F32)

    def near_grads(m, g):
        for p in range(PIECES):
            grads = key_grads(m, g, 1, rows_of(p, tokens), slice(0, group * tokens))
            grad_out[m, g, OVER_Y, rows_of(p)] = grads.astype(BF16)

    def send_near_grads(m, g):
        for p in range(PIECES):
            when(even & (b >= 2), lambda: grad_copy(m, g, OVER_Y, p, 1).start())
            when(odd, lambda: grad_copy(m, g, OVER_Y, p, -1).start())

    def far_grads(m, g):
        for p in range(PIECES):
            grads = key_grads(m, g, 0, rows_of(p), slice(0, (p + 1) * group * piece))
            far_grad[m, g, rows_of(p)] = grads

            @pl.when(even & (b >= 2))
            def _():
                grad_out[m, g, OVER_Z, rows_of(p)] = far_grad[m, g, rows_of(p)].astype(BF16)
                grad_copy(m, g, OVER_Z, p, -2).start()

    def join_grads(m, g):
        for p in range(PIECES):
            @pl.when(odd & (b >= 2))
            def _():
                grad_copy(m, g, OVER_Y, p, 1).wait_recv()
                both = far_grad[m, g, rows_of(p)] + grad_in[m, g, OVER_Y, rows_of(p)].astype(F32)
                grad_out[m, g, OVER_Z, rows_of(p)] = both.astype(BF16)
                grad_copy(m, g, OVER_Z, p, -2).start()

    def own_grads(m, g):
        for p in range(PIECES):
            own_grad[m, g, rows_of(p)] = key_grads(
                m, g, 2, rows_of(p, own), slice(p * group * piece, group * tokens)
            )

    def query_grads(g):
        smooth_t[...] = smooth[g].astype(F32).T.astype(BF16)
        for i in range(tiles):
            window = slice(i * TILE, i * TILE + SPAN)
            dq = jnp.dot(
                smooth_t[:, window], score_all[g, window, i * width : (i + 1) * width],
                preferred_element_type=F32,
            ) * scale
            dq = dq.T.astype(BF16)
            for u in range(group):
                dq_ref[i * TILE : (i + 1) * TILE, cols(g * group + u)] = dq[u * TILE : (u + 1) * TILE]

    def share_copy(m, g, p, t):
        at = (m, g) if p is None else (m, g, rows_of(p))
        return across(scaled.at[at], gathered.at[(t - 1,) + at], s_send.at[t - 1], s_recv.at[t - 1, m, g], t)

    def onward_copy(m, g, t):
        return across(gathered.at[t - 1, m, g], gathered.at[t, m, g], s_send.at[t], s_recv.at[t, m, g], 1)

    far_steps = list(range(2, nh, 2))

    def finish(m, g):
        exponent = (ke_in, ve_in)[m]
        for p in range(PIECES):
            when(even, lambda: grad_copy(m, g, OVER_Y, p, -1).wait_recv())
            when(b + 2 < n, lambda: grad_copy(m, g, OVER_Z, p, -2).wait_recv())
            for r in range(p * tiles // PIECES, (p + 1) * tiles // PIECES):
                at = slice(r * TILE, (r + 1) * TILE)
                whole = own_grad[m, g, at] + grad_in[m, g, OVER_Z, at].astype(F32)
                whole = whole + jnp.where(even, grad_in[m, g, OVER_Y, at].astype(F32), 0.0)
                scaled[m, g, at] = (whole * power_of_two(exponent[g : g + 1, r : r + 1])).astype(BF16)
            for t in far_steps + [1]:
                share_copy(m, g, p, t).start()

    def pass_on(m, g):
        for t in far_steps:
            share_copy(m, g, None, t).wait_recv()
            onward_copy(m, g, t).start()

    def await_core(g):
        for m in range(2):
            share_copy(m, g, None, 1).wait_recv()

    def await_onward(g):
        for m in range(2):
            for t in far_steps:
                onward_copy(m, g, t).wait_recv()

    chunk = rows // 4

    def row_copy(c):
        at = pl.ds(pl.multiple_of(c * chunk, 16), chunk)
        return pltpu.make_async_copy(out_ref.at[at, :], grad_rows.at[at, :], out_sem.at[c])

    def query_copy():
        return pltpu.make_async_copy(dq_ref, dq_out, out_sem.at[4])

    def product(ts, g, fresh, last):
        def one_chunk(c, carry):
            at = pl.ds(pl.multiple_of(c * chunk, 16), chunk)
            total = None if fresh else acc[at, :]
            for t in ts:
                left = jnp.concatenate([weights[t, 0, at, cols(g)], weights[t, 1, at, cols(g)]], 1)
                if t == 0:
                    right = jnp.concatenate([scaled[0, g], scaled[1, g]], 1)
                else:
                    right = jnp.concatenate([gathered[t - 1, 0, g], gathered[t - 1, 1, g]], 1)
                term = contract_last(left, right)
                total = term if total is None else total + term
            if last:
                out_ref[at, :] = total.astype(BF16)
                row_copy(c).start()
            else:
                acc[at, :] = total
            return carry

        lax.fori_loop(0, 4, one_chunk, 0)

    pl.semaphore_wait(barrier, greeted)
    for copy in loads: copy.wait()
    for j in range(len(chunks)): cross_copy(j).start()
    for g in range(heads): true_keys(g)
    sum_keys()
    for g in range(heads): when(b + 2 < n, lambda: key_copy(g).start())
    for g in range(heads):
        true_values(g)
        send_near(V, g)
    for copy in core_copies + own_copies: copy.start()
    clear()
    for g in range(heads): running_keys(g)
    when(b >= 1, lambda: near_sum().wait_recv())
    smooth_keys(0)
    smooth_keys(1)
    for g in range(heads): send_far(V, g)
    for g in range(heads): await_heads(g)
    hand_on(0)
    attend(0, 2)
    attend(1, 2)
    relay(S, 0)
    hand_on(1)
    await_far(S, 0)
    attend(0, 0)
    relay(S, 1)
    await_far(S, 1)
    attend(1, 0)
    hand_on(2)
    await_near(S, 0)
    attend(0, 1)
    combine(0)
    relay(V, 0)
    near_grads(1, 0)
    when(even, lambda: send_near_grads(1, 0))
    far_grads(1, 0)
    hand_on(3)
    relay(V, 1)
    when(odd, lambda: send_near_grads(1, 0))
    await_near(S, 1)
    attend(1, 1)
    combine(1)
    near_grads(1, 1)
    send_near_grads(1, 1)
    far_grads(1, 1)
    await_far(V, 0)
    await_near(V, 0)
    differentiate(0)
    near_grads(0, 0)
    send_near_grads(0, 0)
    far_grads(0, 0)
    hand_on(4)
    await_far(V, 1)
    await_near(V, 1)
    differentiate(1)
    near_grads(0, 1)
    send_near_grads(0, 1)
    join_grads(1, 0)
    far_grads(0, 1)
    hand_on(5)
    own_grads(1, 0)
    join_grads(1, 1)
    own_grads(1, 1)
    own_grads(0, 0)
    own_grads(0, 1)
    join_grads(0, 0)
    hand_on(6)
    finish(1, 0)
    query_grads(0)
    hand_on(7)
    finish(1, 1)
    join_grads(0, 1)
    hand_late(lambda copy: copy.start())
    finish(0, 0)
    query_grads(1)
    query_copy().start()
    for copy in own_copies: copy.wait()
    for copy in core_copies: copy.wait_recv()
    await_core(0)
    product((0, 1), 0, True, False)
    finish(0, 1)
    for m in (1, 0): pass_on(m, 0)
    await_core(1)
    product((0, 1), 1, False, False)
    for j in range(len(chunks)): down_copy(j, 1 - colour).wait_recv()
    await_onward(0)
    product(crossing, 0, False, False)
    for m in (1, 0): pass_on(m, 1)
    await_onward(1)
    product(crossing, 1, False, True)

    query_copy().wait()
    for c in range(4):
        row_copy(c).wait()
    when(b + 1 < n, lambda: near_sum().wait_send())
    for g in range(heads):
        when(b + 2 < n, lambda: key_copy(g).wait_send())
    halo = value.at[:, 0:own]
    when(b + 2 < n, lambda: along(halo, halo, h_send.at[FAR], h_recv.at[0, 0, 0, FAR], 2).wait_send())
    when(even | (b >= 2), lambda: along(halo, halo, h_send.at[NEAR], h_recv.at[0, 0, 0, FAR], 2).wait_send())
    for over, condition in ((OVER_Y, odd | (b >= 2)), (OVER_Z, b >= 2)):
        ref = grad_out.at[:, :, over]
        when(condition, lambda: along(ref, ref, g_send.at[over], g_recv.at[0, 0, 0, 0], 2).wait_send())
    for t in range(1, nh):
        across(scaled, scaled, s_send.at[t - 1], s_recv.at[0, 0, 0], 1).wait_send()
    crossed = weights.at[pl.ds(2, nh - 2), :, pl.ds(0, half), :]
    across(crossed, crossed, w_send.at[0], w_recv.at[0], 1).wait_send()
    for j in range(len(chunks)):
        hand(j, lambda copy: copy.wait_send())
    hand_late(lambda copy: copy.wait_send())
    for copy in core_copies:
        copy.wait_send()


def solution(mesh):
    n, nh = mesh.shape["seq"], mesh.shape["head"]
    assert n % 2 == 0 and n >= 4

    def local(q, k, v, do, ke, ve, wk, wv):
        tokens, width = k.shape
        heads = width // HEAD_SIZE
        group = q.shape[1] // width
        tiles = tokens // TILE
        assert ATTEND_WINDOW == 2 * tokens
        rows = wk.shape[0] // nh
        n_chunks = 4 * (nh - 2)
        hbm = pl.BlockSpec(memory_space=pltpu.HBM)
        dma = pltpu.SemaphoreType.DMA
        return pl.pallas_call(
            functools.partial(kernel, n, nh),
            out_shape=(
                pltpu.VMEM(q.shape, BF16),
                pltpu.VMEM((rows, tokens), BF16),
            ),
            in_specs=[hbm] * 8,
            out_specs=(pl.BlockSpec(memory_space=pl.ANY),) * 2,
            scratch_shapes=[
                pltpu.VMEM((tokens, width), BF16),
                pltpu.VMEM((tokens, width), BF16),
                pltpu.VMEM((heads, tiles), jnp.int32),
                pltpu.VMEM((heads, tiles), jnp.int32),
                pltpu.VMEM((heads, group * tokens, D), BF16),
                pltpu.VMEM((heads, group * tokens, D), BF16),
                pltpu.VMEM((heads, tokens, D), BF16),
                pltpu.VMEM((heads, tokens, D), BF16),
                pltpu.VMEM((heads, tokens, D), F32),
                pltpu.VMEM((8, width), F32),
                pltpu.VMEM((8, width), F32),
                pltpu.VMEM((heads, 3 * tokens, D), BF16),
                pltpu.VMEM((heads, 3 * tokens, D), BF16),
                pltpu.VMEM((D, 3 * tokens), BF16),
                pltpu.VMEM((heads, 3 * tokens, group * tokens), BF16),
                pltpu.VMEM((heads, 3 * tokens, group * tokens), BF16),
                pltpu.VMEM((heads, 3, 2, group * tokens), F32),
                pltpu.VMEM((heads, 3, group * tokens, D), BF16),
                pltpu.VMEM((2, heads, tokens, D), F32),
                pltpu.VMEM((2, heads, tokens, D), F32),
                pltpu.VMEM((2, heads, 2, tokens, D), BF16),
                pltpu.VMEM((2, heads, 2, tokens, D), BF16),
                pltpu.VMEM((2, heads, tokens, D), BF16),
                pltpu.VMEM((nh - 1, 2, heads, tokens, D), BF16),
                pltpu.VMEM((nh, 2, rows, width), BF16),
                pltpu.VMEM((rows, tokens), F32),
                pltpu.VMEM(q.shape, BF16),
                pltpu.VMEM((rows, tokens), BF16),
                dma((5,)),
                dma((4,)), dma((heads, 2)), dma((2,)),
                dma((heads,)), dma((heads,)), dma((1,)), dma((1,)),
                dma((2,)), dma((2, heads, PIECES, 2)),
                dma((1,)), dma((n_chunks,)), dma((n_chunks, 2)), dma((n_chunks,)),
                dma((2,)), dma((2,)),
                dma((2,)), dma((2, heads, 2, PIECES)),
                dma((nh - 1,)), dma((nh - 1, 2, heads)),
            ],
            compiler_params=pltpu.CompilerParams(
                collective_id=0, has_side_effects=True, vmem_limit_bytes=48 * 2**20
            ),
        )(*[pltpu.with_memory_space_constraint(x, pltpu.HBM) for x in (q, k, v, do, ke.T, ve.T, wk, wv)])

    in_specs = (P("seq", "head"),) * 6 + (P(None, "head"),) * 2
    out_specs = (P("seq", "head"), P("head", "seq"))
    return jax.shard_map(local, mesh=mesh, in_specs=in_specs, out_specs=out_specs, check_vma=False)
```

```python
import functools

import jax
import jax.numpy as jnp
from jax import lax
from jax.experimental import pallas as pl
from jax.experimental.pallas import tpu as pltpu
from jax.sharding import PartitionSpec as P

HEAD_SIZE = 128
QUERY_SCALE = 168
ATTEND_WINDOW = 1024
SCALE_BLOCK = 128
LOG2_E = 1.4426950408889634
LOWEST = -1e30
MESH = pl.DeviceIdType.MESH
F32 = jnp.float32
BF16 = jnp.bfloat16
D = HEAD_SIZE
TILE = SCALE_BLOCK
SPAN = ATTEND_WINDOW + TILE
PIECES = 2
V, S = 0, 1
FAR, NEAR = 0, 1
OVER_Y, OVER_Z = 0, 1


def power_of_two(exponent):
    return jnp.where(exponent > 0, 2.0, jnp.where(exponent < 0, 0.5, 1.0)).astype(F32)


def contract_last(a, b):
    return lax.dot_general(a, b, (((1,), (1,)), ((), ())), preferred_element_type=F32)


def partner(h, t):
    other, bit = h, 1
    while bit <= t:
        if t & bit:
            other = other + bit - 2 * bit * lax.rem(lax.div(h, bit), 2)
        bit *= 2
    return other


def kernel(
    n, nh, q_ref, k_ref, v_ref, do_ref, ke_ref, ve_ref, wk_ref, wv_ref, dq_out, grad_rows,
    k_in, v_in, ke_in, ve_in, q_all, do_all, key_true, raw_far, own_sum, total_own, total_near, smooth, value, smooth_t,
    shares_all, score_all, stats, do_part, far_grad, own_grad, grad_out, grad_in, scaled, gathered, weights, acc,
    dq_ref, out_ref, out_sem, in_sem, qd_sem, w_own, kf_send, kf_recv, t_send, t_recv, h_send, h_recv,
    w_send, w_recv, f_send, f_recv, thin_send, thin_recv, c_send, c_recv, g_send, g_recv, s_send, s_recv,
):
    tokens = k_ref.shape[0]
    heads = k_ref.shape[1] // D
    group = q_ref.shape[1] // (heads * D)
    width = group * TILE
    tiles = tokens // TILE
    rows = grad_rows.shape[0]
    own = 2 * tokens
    scale = QUERY_SCALE ** (-0.5)
    b = lax.axis_index("seq")
    h = lax.axis_index("head")
    odd = lax.rem(b, 2) == 1
    even = lax.rem(b, 2) == 0
    colour = lax.rem(lax.rem(b, 2) + lax.div(b, 2), 2)
    crossing = list(range(2, nh))

    def cols(g):
        return slice(g * D, (g + 1) * D)

    loads = [
        pltpu.make_async_copy(k_ref, k_in, in_sem.at[0]),
        pltpu.make_async_copy(v_ref, v_in, in_sem.at[1]),
        pltpu.make_async_copy(ke_ref, ke_in, in_sem.at[2]),
        pltpu.make_async_copy(ve_ref, ve_in, in_sem.at[3]),
    ]
    for copy in loads:
        copy.start()
    head_loads = []
    for g in range(heads):
        for m, (ref, dst) in enumerate(((q_ref, q_all), (do_ref, do_all))):
            for i in range(tiles):
                for u in range(group):
                    head_loads.append(
                        pltpu.make_async_copy(
                            ref.at[i * TILE : (i + 1) * TILE, cols(g * group + u)],
                            dst.at[g, (i * group + u) * TILE : (i * group + u + 1) * TILE, :],
                            qd_sem.at[g, m],
                        )
                    )
    for copy in head_loads:
        copy.start()

    barrier = pltpu.get_barrier_semaphore()

    def greet(step):
        pl.semaphore_signal(
            barrier, inc=1, device_id={"seq": lax.rem(b + n + step, n)}, device_id_type=MESH
        )

    for step in (1, 2):
        pl.when(b + step < n)(lambda: greet(step))
        pl.when(b >= step)(lambda: greet(-step))
    for t in range(1, nh):
        pl.semaphore_signal(barrier, inc=1, device_id={"head": partner(h, t)}, device_id_type=MESH)
    greeted = nh - 1 + jnp.minimum(b, 2) + jnp.minimum(n - 1 - b, 2)

    def when(condition, action):
        pl.when(condition)(action)

    def along(src, dst, send, recv, step):
        return pltpu.make_async_remote_copy(
            src_ref=src, dst_ref=dst, send_sem=send, recv_sem=recv,
            device_id={"seq": lax.rem(b + n + step, n)}, device_id_type=MESH,
        )

    def across(src, dst, send, recv, t):
        return pltpu.make_async_remote_copy(
            src_ref=src, dst_ref=dst, send_sem=send, recv_sem=recv,
            device_id={"head": partner(h, t)}, device_id_type=MESH,
        )

    def when(condition, *steps):
        @pl.when(condition)
        def _():
            for step in steps:
                step()

    half = rows // 2
    part = half // 2
    chunks = [(t, m, q) for t in crossing for m in range(2) for q in range(2)]
    thin_t, thin_m = chunks[-1][:2]
    chunks = chunks[:-2]
    w_refs = (wk_ref, wv_ref)
    z = lax.div(b, 2)
    upper = lax.rem(z, 2)
    mine = lax.rem(lax.div(lax.rem(z, 4) + 1, 2), 2)
    row_0 = b < 2
    row_1 = (b >= 2) & (b < 4)
    top = b + 2 >= n
    below_top = (b + 2 < n) & (b + 4 >= n)

    def held(t, m, q, side):
        return weights.at[t, m, pl.ds(side * half + q * part, part), :]

    def cross(t, m, q, j):
        return across(
            w_refs[m].at[pl.ds(partner(h, t) * rows + colour * half + q * part, part), :],
            held(t, m, q, colour), w_send.at[j], w_recv.at[j], t,
        )

    def cross_copy(j):
        return cross(*chunks[j], j)

    def cross_thin():
        return cross(thin_t, thin_m, mine, len(chunks))

    def hand_copy(ref, step, sent, received):
        if step:
            return along(ref, ref, sent, received, step)
        return pltpu.make_async_remote_copy(
            src_ref=ref, dst_ref=ref, send_sem=sent, recv_sem=received,
            device_id={"seq": partner(b, 1)}, device_id_type=MESH,
        )

    def chunk_copy(j, step, which):
        return hand_copy(held(*chunks[j], colour), step, f_send.at[j, which], f_recv.at[j])

    def hand(j, action):
        if j < 2:
            when(b >= 2, lambda: action(chunk_copy(j, -2, 0)))
            if j > 0:
                when(below_top, lambda: action(chunk_copy(j, 2, 1)))
        else:
            when(b + 2 < n, lambda: action(chunk_copy(j, 2, 1)))
            if j != 3:
                when(row_0, lambda: action(chunk_copy(j, 0, 0)))

    def hand_on(j):
        cross_copy(j).wait_recv()
        hand(j, lambda copy: copy.start())

    def hand_top(action):
        when(top, lambda: action(chunk_copy(0, 0, 1)))

    def hand_bottom(action):
        when(row_1, lambda: action(chunk_copy(3, -2, 0)))

    def thin_copy(which, step, sent, received, side=colour):
        return hand_copy(held(thin_t, thin_m, which, side), step, sent, received)

    def thin_up():
        return thin_copy(mine, 2, thin_send.at[0], thin_recv.at[0])

    def thin_down():
        return thin_copy(mine, -2, thin_send.at[0], thin_recv.at[0])

    def thin_side(which, at, side=colour):
        return thin_copy(which, 0, thin_send.at[at], thin_recv.at[at], side)

    def hand_thin():
        cross_thin().wait_recv()
        thin_side(mine, 1).start()
        when(upper == 1, lambda: thin_down().start())

    def raise_thin():
        when(upper == 0, lambda: thin_up().start())

    def share_thin():
        thin_copy(1 - mine, 2, thin_send.at[0], thin_recv.at[0], 1 - colour).wait_recv()
        thin_side(1 - mine, 2, 1 - colour).start()

    def await_weights():
        for j in range(len(chunks)):
            hand_copy(held(*chunks[j], 1 - colour), 0, f_send.at[j, 0], f_recv.at[j]).wait_recv()
        thin_side(mine, 1, 1 - colour).wait_recv()
        thin_side(1 - mine, 2).wait_recv()

    core_copies = [
        across(ref.at[pl.ds(partner(h, 1) * rows, rows), :], weights.at[1, m], c_send.at[m], c_recv.at[m], 1)
        for m, ref in enumerate(w_refs)
    ]
    own_copies = [
        pltpu.make_async_copy(ref.at[pl.ds(h * rows, rows), :], weights.at[0, m], w_own.at[m])
        for m, ref in enumerate(w_refs)
    ]

    def key_copy(g):
        return along(key_true.at[g], raw_far.at[g], kf_send.at[g], kf_recv.at[g], 2)

    piece = tokens // PIECES
    halo_refs = (value, smooth)

    def slot(kind, g, base, p):
        return halo_refs[kind].at[g, base + p * piece : base + (p + 1) * piece]

    def far_copy(kind, g, p):
        at = (kind, g, p, FAR)
        return along(slot(kind, g, own, p), slot(kind, g, 0, p), h_send.at[FAR], h_recv.at[at], 2)

    def near_copy(kind, g, p):
        at = (kind, g, p, NEAR)
        return along(slot(kind, g, own, p), slot(kind, g, tokens, p), h_send.at[NEAR], h_recv.at[at], 1)

    def relay_copy(kind, g, p):
        at = (kind, g, p, NEAR)
        return along(slot(kind, g, 0, p), slot(kind, g, tokens, p), h_send.at[NEAR], h_recv.at[at], -1)

    def send_far(kind, g):
        for p in range(PIECES):
            when(b + 2 < n, lambda: far_copy(kind, g, p).start())

    def send_near(kind, g):
        for p in range(PIECES):
            when(even, lambda: near_copy(kind, g, p).start())

    def relay(kind, g):
        for p in range(PIECES):
            @pl.when(odd & (b >= 2))
            def _():
                far_copy(kind, g, p).wait_recv()
                relay_copy(kind, g, p).start()

    def await_far(kind, g):
        for p in range(PIECES):
            when(even & (b >= 2), lambda: far_copy(kind, g, p).wait_recv())

    def await_near(kind, g):
        for p in range(PIECES):
            when(b >= 1, lambda: near_copy(kind, g, p).wait_recv())

    def near_sum():
        return along(total_own, total_near, t_send.at[0], t_recv.at[0], 1)

    def await_heads(g):
        for m, ref in enumerate((q_all, do_all)):
            pltpu.make_async_copy(ref.at[g], ref.at[g], qd_sem.at[g, m]).wait()

    def rows_of(p, base=0):
        return slice(base + p * piece, base + (p + 1) * piece)

    def grad_copy(m, g, over, p, step):
        at = (m, g, over, rows_of(p))
        return along(grad_out.at[at], grad_in.at[at], g_send.at[over], g_recv.at[m, g, over, p], step)

    def true_keys(g):
        for j in range(tiles):
            at = slice(j * TILE, (j + 1) * TILE)
            key_true[g, at] = (k_in[at, cols(g)].astype(F32) * power_of_two(ke_in[g : g + 1, j : j + 1])).astype(BF16)

    def true_values(g):
        for j in range(tiles):
            at = slice(j * TILE, (j + 1) * TILE)
            value[g, own + j * TILE : own + (j + 1) * TILE] = (
                v_in[at, cols(g)].astype(F32) * power_of_two(ve_in[g : g + 1, j : j + 1])
            ).astype(BF16)

    def sum_keys():
        for g in range(heads):
            total_own[:, cols(g)] = jnp.broadcast_to(
                jnp.sum(key_true[g].astype(F32), axis=0, keepdims=True), (8, D)
            )
        when(b + 1 < n, lambda: near_sum().start())

    def clear():
        @pl.when(b < 1)
        def _():
            total_near[...] = jnp.zeros_like(total_near)
            for g in range(heads):
                value[g, tokens:own, :] = jnp.zeros((tokens, D), BF16)
                smooth[g, tokens:own, :] = jnp.zeros((tokens, D), BF16)

        @pl.when(b < 2)
        def _():
            raw_far[...] = jnp.zeros_like(raw_far)
            for g in range(heads):
                value[g, 0:tokens, :] = jnp.zeros((tokens, D), BF16)
                smooth[g, 0:tokens, :] = jnp.zeros((tokens, D), BF16)
                for m in range(2):
                    grad_in[m, g, OVER_Y] = jnp.zeros((tokens, D), BF16)

        @pl.when(top)
        def _():
            for g in range(heads):
                for m in range(2):
                    grad_in[m, g, OVER_Z] = jnp.zeros((tokens, D), BF16)

        blank = jnp.zeros((TILE, width), BF16)
        for ref in (shares_all, score_all):
            for g in range(heads):
                for i in range(0, tiles, 2):
                    ref[g, i * TILE : (i + 1) * TILE, (i + 1) * width : (i + 2) * width] = blank
                    ref[g, own + (i + 1) * TILE : own + (i + 2) * TILE, i * width : (i + 1) * width] = blank

    row_at = lax.broadcasted_iota(jnp.int32, (tokens, tokens), 0)
    col_at = lax.broadcasted_iota(jnp.int32, (tokens, tokens), 1)
    lower = jnp.where(row_at >= col_at, 1.0, 0.0).astype(BF16)
    place = b * tokens + lax.broadcasted_iota(jnp.int32, (tokens, 1), 0)
    counts = jnp.clip(place + 1, 1, ATTEND_WINDOW).astype(F32)

    def running_keys(g):
        own_sum[g] = jnp.dot(lower, key_true[g], preferred_element_type=F32)

    def smooth_keys(g):
        when(b >= 2, lambda: key_copy(g).wait_recv())
        far = jnp.dot(lower, raw_far[g], preferred_element_type=F32)
        mean = (own_sum[g] - far + far[tokens - 1 :, :] + total_near[0:1, cols(g)]) / counts
        smooth[g, own : own + tokens, :] = (key_true[g].astype(F32) - mean).astype(BF16)
        send_far(S, g)
        send_near(S, g)

    row = lax.broadcasted_iota(jnp.int32, (TILE, width), 0)
    lane = lax.rem(lax.broadcasted_iota(jnp.int32, (1, width), 1), TILE)
    unit = jnp.where(
        lax.broadcasted_iota(jnp.int32, (TILE, TILE), 0) == lax.broadcasted_iota(jnp.int32, (TILE, TILE), 1), 1.0, 0.0
    )

    def lanes_of(i):
        return slice(i * width, (i + 1) * width)

    def keys_of(part, i):
        return (slice(i * TILE, tokens), slice(tokens, own), slice(own, own + (i + 1) * TILE))[part]

    def attend(g, part):
        for i in range(tiles):
            at, lanes = keys_of(part, i), lanes_of(i)
            scores = contract_last(smooth[g, at, :], q_all[g, lanes, :])
            if part == 0:
                edge = jnp.where(row > lane, scores[:TILE], -jnp.inf)
                scores = edge if i == tiles - 1 else jnp.concatenate([edge, scores[TILE:]], 0)
            if part == 2:
                edge = jnp.where(row <= lane, scores[i * TILE :], -jnp.inf)
                scores = edge if i == 0 else jnp.concatenate([scores[: i * TILE], edge], 0)
            highest = jnp.maximum(jnp.max(scores, axis=0, keepdims=True), LOWEST)
            powers = jnp.exp2((scores - highest) * (scale * LOG2_E))
            shares_all[g, at, lanes] = powers.astype(BF16)
            stats[g, part, 0:1, lanes] = highest
            stats[g, part, 1:2, lanes] = jnp.sum(powers, axis=0, keepdims=True)

    def combine(g):
        present = (b >= 2, b >= 1, b >= 0)
        tops = [jnp.where(here, stats[g, part, 0:1, :], LOWEST) for part, here in enumerate(present)]
        highest = jnp.maximum(jnp.maximum(tops[0], tops[1]), tops[2])
        powers = [
            jnp.where(here, jnp.exp2((top - highest) * (scale * LOG2_E)), 0.0) for top, here in zip(tops, present)
        ]
        total = sum(power * stats[g, part, 1:2, :] for part, power in enumerate(powers))
        inverse = 1.0 / total
        for part in range(3):
            factor = powers[part] * inverse
            stats[g, part, 0:1, :] = factor.astype(BF16).astype(F32)
            for k in range(group * tiles):
                at = slice(k * TILE, (k + 1) * TILE)
                spread = (unit * factor[:, at]).astype(BF16)
                do_part[g, part, at, :] = jnp.dot(
                    spread, do_all[g, at, :], preferred_element_type=F32
                ).astype(BF16)

    def differentiate(g):
        for i in range(tiles):
            lanes = lanes_of(i)
            row_dot, parts = 0.0, []
            for part in range(3):
                at = keys_of(part, i)
                share_grad = contract_last(value[g, at, :], do_part[g, part, lanes, :])
                shares = shares_all[g, at, lanes].astype(F32)
                row_dot = row_dot + jnp.sum(shares * share_grad, axis=0, keepdims=True)
                parts.append((at, shares, share_grad))
            for part, (at, shares, share_grad) in enumerate(parts):
                shift = row_dot * stats[g, part, 0:1, lanes]
                score_all[g, at, lanes] = (shares * (share_grad - shift)).astype(BF16)

    def key_grads(m, g, part, at, lanes):
        if m == 0:
            return jnp.dot(score_all[g, at, lanes], q_all[g, lanes, :], preferred_element_type=F32) * scale
        return jnp.dot(shares_all[g, at, lanes], do_part[g, part, lanes, :], preferred_element_type=F32)

    def near_grads(m, g):
        for p in range(PIECES):
            grads = key_grads(m, g, 1, rows_of(p, tokens), slice(0, group * tokens))
            grad_out[m, g, OVER_Y, rows_of(p)] = grads.astype(BF16)

    def send_near_grads(m, g):
        for p in range(PIECES):
            when(even & (b >= 2), lambda: grad_copy(m, g, OVER_Y, p, 1).start())
            when(odd, lambda: grad_copy(m, g, OVER_Y, p, -1).start())

    def far_grads(m, g):
        for p in range(PIECES):
            grads = key_grads(m, g, 0, rows_of(p), slice(0, (p + 1) * group * piece))
            far_grad[m, g, rows_of(p)] = grads

            @pl.when(even & (b >= 2))
            def _():
                grad_out[m, g, OVER_Z, rows_of(p)] = far_grad[m, g, rows_of(p)].astype(BF16)
                grad_copy(m, g, OVER_Z, p, -2).start()

    def join_grads(m, g):
        for p in range(PIECES):
            @pl.when(odd & (b >= 2))
            def _():
                grad_copy(m, g, OVER_Y, p, 1).wait_recv()
                both = far_grad[m, g, rows_of(p)] + grad_in[m, g, OVER_Y, rows_of(p)].astype(F32)
                grad_out[m, g, OVER_Z, rows_of(p)] = both.astype(BF16)
                grad_copy(m, g, OVER_Z, p, -2).start()

    def own_grads(m, g):
        for p in range(PIECES):
            own_grad[m, g, rows_of(p)] = key_grads(
                m, g, 2, rows_of(p, own), slice(p * group * piece, group * tokens)
            )

    def query_grads(g):
        smooth_t[...] = smooth[g].astype(F32).T.astype(BF16)
        for i in range(tiles):
            window = slice(i * TILE, i * TILE + SPAN)
            dq = jnp.dot(
                smooth_t[:, window], score_all[g, window, i * width : (i + 1) * width],
                preferred_element_type=F32,
            ) * scale
            dq = dq.T.astype(BF16)
            for u in range(group):
                dq_ref[i * TILE : (i + 1) * TILE, cols(g * group + u)] = dq[u * TILE : (u + 1) * TILE]

    def share_copy(m, g, p, t):
        at = (m, g) if p is None else (m, g, rows_of(p))
        return across(scaled.at[at], gathered.at[(t - 1,) + at], s_send.at[t - 1], s_recv.at[t - 1, m, g], t)

    def onward_copy(m, g, t):
        return across(gathered.at[t - 1, m, g], gathered.at[t, m, g], s_send.at[t], s_recv.at[t, m, g], 1)

    far_steps = list(range(2, nh, 2))

    def finish(m, g):
        exponent = (ke_in, ve_in)[m]
        for p in range(PIECES):
            when(even, lambda: grad_copy(m, g, OVER_Y, p, -1).wait_recv())
            when(b + 2 < n, lambda: grad_copy(m, g, OVER_Z, p, -2).wait_recv())
            for r in range(p * tiles // PIECES, (p + 1) * tiles // PIECES):
                at = slice(r * TILE, (r + 1) * TILE)
                whole = own_grad[m, g, at] + grad_in[m, g, OVER_Z, at].astype(F32)
                whole = whole + jnp.where(even, grad_in[m, g, OVER_Y, at].astype(F32), 0.0)
                scaled[m, g, at] = (whole * power_of_two(exponent[g : g + 1, r : r + 1])).astype(BF16)
            for t in far_steps + [1]:
                share_copy(m, g, p, t).start()

    def pass_on(m, g):
        for t in far_steps:
            share_copy(m, g, None, t).wait_recv()
            onward_copy(m, g, t).start()

    def await_core(g):
        for m in range(2):
            share_copy(m, g, None, 1).wait_recv()

    def await_onward(g):
        for m in range(2):
            for t in far_steps:
                onward_copy(m, g, t).wait_recv()

    chunk = rows // 4

    def row_copy(c):
        at = pl.ds(pl.multiple_of(c * chunk, 16), chunk)
        return pltpu.make_async_copy(out_ref.at[at, :], grad_rows.at[at, :], out_sem.at[c])

    def query_copy():
        return pltpu.make_async_copy(dq_ref, dq_out, out_sem.at[4])

    def product(ts, g, fresh, last):
        def one_chunk(c, carry):
            at = pl.ds(pl.multiple_of(c * chunk, 16), chunk)
            total = None if fresh else acc[at, :]
            for t in ts:
                left = jnp.concatenate([weights[t, 0, at, cols(g)], weights[t, 1, at, cols(g)]], 1)
                if t == 0:
                    right = jnp.concatenate([scaled[0, g], scaled[1, g]], 1)
                else:
                    right = jnp.concatenate([gathered[t - 1, 0, g], gathered[t - 1, 1, g]], 1)
                term = contract_last(left, right)
                total = term if total is None else total + term
            if last:
                out_ref[at, :] = total.astype(BF16)
                row_copy(c).start()
            else:
                acc[at, :] = total
            return carry

        lax.fori_loop(0, 4, one_chunk, 0)

    pl.semaphore_wait(barrier, greeted)
    for copy in loads: copy.wait()
    cross_thin().start()
    for j in range(len(chunks)): cross_copy(j).start()
    for g in range(heads): true_keys(g)
    sum_keys()
    for g in range(heads): when(b + 2 < n, lambda: key_copy(g).start())
    for g in range(heads):
        true_values(g)
        send_near(V, g)
    for copy in core_copies + own_copies: copy.start()
    clear()
    for g in range(heads): running_keys(g)
    when(b >= 1, lambda: near_sum().wait_recv())
    smooth_keys(0)
    hand_thin()
    smooth_keys(1)
    for g in range(heads): send_far(V, g)
    raise_thin()
    for g in range(heads): await_heads(g)
    attend(0, 2)
    attend(1, 2)
    relay(S, 0)
    hand_on(0)
    await_far(S, 0)
    attend(0, 0)
    relay(S, 1)
    await_far(S, 1)
    attend(1, 0)
    hand_on(1)
    when(row_0, share_thin)
    await_near(S, 0)
    attend(0, 1)
    combine(0)
    relay(V, 0)
    near_grads(1, 0)
    when(even, lambda: send_near_grads(1, 0))
    far_grads(1, 0)
    relay(V, 1)
    when(odd, lambda: send_near_grads(1, 0))
    await_near(S, 1)
    attend(1, 1)
    hand_on(2)
    combine(1)
    near_grads(1, 1)
    send_near_grads(1, 1)
    far_grads(1, 1)
    await_far(V, 0)
    await_near(V, 0)
    join_grads(1, 0)
    differentiate(0)
    near_grads(0, 0)
    send_near_grads(0, 0)
    hand_on(3)
    far_grads(0, 0)
    await_far(V, 1)
    await_near(V, 1)
    join_grads(1, 1)
    differentiate(1)
    near_grads(0, 1)
    send_near_grads(0, 1)
    hand_on(4)
    when(b >= 2, share_thin)
    hand_top(lambda copy: copy.start())
    far_grads(0, 1)
    for m in (1, 0): own_grads(m, 0)
    join_grads(0, 0)
    finish(1, 0)
    for m in (1, 0): own_grads(m, 1)
    hand_on(5)
    join_grads(0, 1)
    hand_bottom(lambda copy: copy.start())
    finish(1, 1)
    query_grads(0)
    finish(0, 0)
    query_grads(1)
    query_copy().start()
    for copy in own_copies: copy.wait()
    for copy in core_copies: copy.wait_recv()
    await_core(0)
    product((0, 1), 0, True, False)
    finish(0, 1)
    await_core(1)
    product((0, 1), 1, False, False)
    for m in (1, 0): pass_on(m, 0)
    await_weights()
    await_onward(0)
    product(crossing, 0, False, False)
    for m in (1, 0): pass_on(m, 1)
    await_onward(1)
    product(crossing, 1, False, True)

    query_copy().wait()
    for c in range(4):
        row_copy(c).wait()
    when(b + 1 < n, lambda: near_sum().wait_send())
    for g in range(heads):
        when(b + 2 < n, lambda: key_copy(g).wait_send())
    halo = value.at[:, 0:own]
    when(b + 2 < n, lambda: along(halo, halo, h_send.at[FAR], h_recv.at[0, 0, 0, FAR], 2).wait_send())
    when(even | (b >= 2), lambda: along(halo, halo, h_send.at[NEAR], h_recv.at[0, 0, 0, FAR], 2).wait_send())
    for over, condition in ((OVER_Y, odd | (b >= 2)), (OVER_Z, b >= 2)):
        ref = grad_out.at[:, :, over]
        when(condition, lambda: along(ref, ref, g_send.at[over], g_recv.at[0, 0, 0, 0], 2).wait_send())
    for t in range(1, nh):
        across(scaled, scaled, s_send.at[t - 1], s_recv.at[0, 0, 0], 1).wait_send()
    cross_thin().wait_send()
    thin_up().wait_send()
    thin_side(mine, 1).wait_send()
    thin_side(1 - mine, 2, 1 - colour).wait_send()
    for j in range(len(chunks)):
        cross_copy(j).wait_send()
        hand(j, lambda copy: copy.wait_send())
    hand_top(lambda copy: copy.wait_send())
    hand_bottom(lambda copy: copy.wait_send())
    for copy in core_copies:
        copy.wait_send()


def solution(mesh):
    n, nh = mesh.shape["seq"], mesh.shape["head"]
    assert n % 8 == 0 and nh >= 4

    def local(q, k, v, do, ke, ve, wk, wv):
        tokens, width = k.shape
        heads = width // HEAD_SIZE
        group = q.shape[1] // width
        tiles = tokens // TILE
        assert ATTEND_WINDOW == 2 * tokens
        rows = wk.shape[0] // nh
        n_chunks = 4 * (nh - 2)
        hbm = pl.BlockSpec(memory_space=pltpu.HBM)
        dma = pltpu.SemaphoreType.DMA
        return pl.pallas_call(
            functools.partial(kernel, n, nh),
            out_shape=(
                pltpu.VMEM(q.shape, BF16),
                pltpu.VMEM((rows, tokens), BF16),
            ),
            in_specs=[hbm] * 8,
            out_specs=(pl.BlockSpec(memory_space=pl.ANY),) * 2,
            scratch_shapes=[
                pltpu.VMEM((tokens, width), BF16),
                pltpu.VMEM((tokens, width), BF16),
                pltpu.VMEM((heads, tiles), jnp.int32),
                pltpu.VMEM((heads, tiles), jnp.int32),
                pltpu.VMEM((heads, group * tokens, D), BF16),
                pltpu.VMEM((heads, group * tokens, D), BF16),
                pltpu.VMEM((heads, tokens, D), BF16),
                pltpu.VMEM((heads, tokens, D), BF16),
                pltpu.VMEM((heads, tokens, D), F32),
                pltpu.VMEM((8, width), F32),
                pltpu.VMEM((8, width), F32),
                pltpu.VMEM((heads, 3 * tokens, D), BF16),
                pltpu.VMEM((heads, 3 * tokens, D), BF16),
                pltpu.VMEM((D, 3 * tokens), BF16),
                pltpu.VMEM((heads, 3 * tokens, group * tokens), BF16),
                pltpu.VMEM((heads, 3 * tokens, group * tokens), BF16),
                pltpu.VMEM((heads, 3, 2, group * tokens), F32),
                pltpu.VMEM((heads, 3, group * tokens, D), BF16),
                pltpu.VMEM((2, heads, tokens, D), F32),
                pltpu.VMEM((2, heads, tokens, D), F32),
                pltpu.VMEM((2, heads, 2, tokens, D), BF16),
                pltpu.VMEM((2, heads, 2, tokens, D), BF16),
                pltpu.VMEM((2, heads, tokens, D), BF16),
                pltpu.VMEM((nh - 1, 2, heads, tokens, D), BF16),
                pltpu.VMEM((nh, 2, rows, width), BF16),
                pltpu.VMEM((rows, tokens), F32),
                pltpu.VMEM(q.shape, BF16),
                pltpu.VMEM((rows, tokens), BF16),
                dma((5,)),
                dma((4,)), dma((heads, 2)), dma((2,)),
                dma((heads,)), dma((heads,)), dma((1,)), dma((1,)),
                dma((2,)), dma((2, heads, PIECES, 2)),
                dma((n_chunks - 1,)), dma((n_chunks - 1,)), dma((n_chunks - 2, 2)), dma((n_chunks - 2,)), dma((3,)), dma((3,)),
                dma((2,)), dma((2,)),
                dma((2,)), dma((2, heads, 2, PIECES)),
                dma((nh - 1,)), dma((nh - 1, 2, heads)),
            ],
            compiler_params=pltpu.CompilerParams(
                collective_id=0, has_side_effects=True, vmem_limit_bytes=48 * 2**20
            ),
        )(*[pltpu.with_memory_space_constraint(x, pltpu.HBM) for x in (q, k, v, do, ke.T, ve.T, wk, wv)])

    in_specs = (P("seq", "head"),) * 6 + (P(None, "head"),) * 2
    out_specs = (P("seq", "head"), P("head", "seq"))
    return jax.shard_map(local, mesh=mesh, in_specs=in_specs, out_specs=out_specs, check_vma=False)
```

```python
import functools

import jax
import jax.numpy as jnp
from jax import lax
from jax.experimental import pallas as pl
from jax.experimental.pallas import tpu as pltpu
from jax.sharding import PartitionSpec as P

HEAD_SIZE = 128
QUERY_SCALE = 168
ATTEND_WINDOW = 1024
SCALE_BLOCK = 128
LOG2_E = 1.4426950408889634
LOWEST = -1e30
MESH = pl.DeviceIdType.MESH
F32 = jnp.float32
BF16 = jnp.bfloat16
D = HEAD_SIZE
TILE = SCALE_BLOCK
SPAN = ATTEND_WINDOW + TILE
PIECES = 2
CHUNKS = 4
V, S = 0, 1
FAR, NEAR = 0, 1
OVER_Y, OVER_Z = 0, 1


def power_of_two(exponent):
    return jnp.where(exponent > 0, 2.0, jnp.where(exponent < 0, 0.5, 1.0)).astype(F32)


def contract_last(a, b):
    return lax.dot_general(a, b, (((1,), (1,)), ((), ())), preferred_element_type=F32)


def partner(h, t):
    other, bit = h, 1
    while bit <= t:
        if t & bit:
            other = other + bit - 2 * bit * lax.rem(lax.div(h, bit), 2)
        bit *= 2
    return other


def kernel(
    n, nh, q_ref, k_ref, v_ref, do_ref, ke_ref, ve_ref, wk_ref, wv_ref, dq_ref, gathered, weights, acc,
    k_in, v_in, ke_in, ve_in, q_all, do_all, key_true, raw_far, own_sum, total_own, total_near, smooth, value, smooth_t,
    shares_all, score_all, stats, do_part, far_grad, own_grad, grad_out, grad_in, scaled,
    in_sem, qd_sem, w_own, kf_send, kf_recv, t_send, t_recv, h_send, h_recv,
    w_send, w_recv, f_send, f_recv, thin_send, thin_recv, c_send, c_recv, g_send, g_recv, s_send, s_recv,
):
    tokens = k_ref.shape[0]
    heads = k_ref.shape[1] // D
    group = q_ref.shape[1] // (heads * D)
    width = group * TILE
    tiles = tokens // TILE
    rows = acc.shape[0]
    own = 2 * tokens
    scale = QUERY_SCALE ** (-0.5)
    b = lax.axis_index("seq")
    h = lax.axis_index("head")
    odd = lax.rem(b, 2) == 1
    even = lax.rem(b, 2) == 0
    colour = lax.rem(lax.rem(b, 2) + lax.div(b, 2), 2)
    crossing = list(range(2, nh))

    def cols(g):
        return slice(g * D, (g + 1) * D)

    loads = [
        pltpu.make_async_copy(k_ref, k_in, in_sem.at[0]),
        pltpu.make_async_copy(v_ref, v_in, in_sem.at[1]),
        pltpu.make_async_copy(ke_ref, ke_in, in_sem.at[2]),
        pltpu.make_async_copy(ve_ref, ve_in, in_sem.at[3]),
    ]
    for copy in loads:
        copy.start()
    head_loads = []
    for g in range(heads):
        for m, (ref, dst) in enumerate(((q_ref, q_all), (do_ref, do_all))):
            for i in range(tiles):
                for u in range(group):
                    head_loads.append(
                        pltpu.make_async_copy(
                            ref.at[i * TILE : (i + 1) * TILE, cols(g * group + u)],
                            dst.at[g, (i * group + u) * TILE : (i * group + u + 1) * TILE, :],
                            qd_sem.at[g, m],
                        )
                    )
    for copy in head_loads:
        copy.start()

    barrier = pltpu.get_barrier_semaphore()

    def greet(step):
        pl.semaphore_signal(
            barrier, inc=1, device_id={"seq": lax.rem(b + n + step, n)}, device_id_type=MESH
        )

    for step in (1, 2):
        pl.when(b + step < n)(lambda: greet(step))
        pl.when(b >= step)(lambda: greet(-step))
    for t in range(1, nh):
        pl.semaphore_signal(barrier, inc=1, device_id={"head": partner(h, t)}, device_id_type=MESH)
    greeted = nh - 1 + jnp.minimum(b, 2) + jnp.minimum(n - 1 - b, 2)

    def when(condition, action):
        pl.when(condition)(action)

    def along(src, dst, send, recv, step):
        return pltpu.make_async_remote_copy(
            src_ref=src, dst_ref=dst, send_sem=send, recv_sem=recv,
            device_id={"seq": lax.rem(b + n + step, n)}, device_id_type=MESH,
        )

    def across(src, dst, send, recv, t):
        return pltpu.make_async_remote_copy(
            src_ref=src, dst_ref=dst, send_sem=send, recv_sem=recv,
            device_id={"head": partner(h, t)}, device_id_type=MESH,
        )

    def when(condition, *steps):
        @pl.when(condition)
        def _():
            for step in steps:
                step()

    half = rows // 2
    part = half // 2
    chunks = [(t, m, q) for t in crossing for m in range(2) for q in range(2)]
    thin_t, thin_m = chunks[-1][:2]
    chunks = chunks[:-2]
    w_refs = (wk_ref, wv_ref)
    z = lax.div(b, 2)
    upper = lax.rem(z, 2)
    mine = lax.rem(lax.div(lax.rem(z, 4) + 1, 2), 2)
    row_0 = b < 2
    row_1 = (b >= 2) & (b < 4)
    top = b + 2 >= n
    below_top = (b + 2 < n) & (b + 4 >= n)

    def held(t, m, q, side):
        return weights.at[t, m, pl.ds(side * half + q * part, part), :]

    def cross(t, m, q, j):
        return across(
            w_refs[m].at[pl.ds(partner(h, t) * rows + colour * half + q * part, part), :],
            held(t, m, q, colour), w_send.at[j], w_recv.at[j], t,
        )

    def cross_copy(j):
        return cross(*chunks[j], j)

    def cross_thin():
        return cross(thin_t, thin_m, mine, len(chunks))

    def hand_copy(ref, step, sent, received):
        if step:
            return along(ref, ref, sent, received, step)
        return pltpu.make_async_remote_copy(
            src_ref=ref, dst_ref=ref, send_sem=sent, recv_sem=received,
            device_id={"seq": partner(b, 1)}, device_id_type=MESH,
        )

    def chunk_copy(j, step, which):
        return hand_copy(held(*chunks[j], colour), step, f_send.at[j, which], f_recv.at[j])

    def hand(j, action):
        if j < 2:
            when(b >= 2, lambda: action(chunk_copy(j, -2, 0)))
            if j > 0:
                when(below_top, lambda: action(chunk_copy(j, 2, 1)))
        else:
            when(b + 2 < n, lambda: action(chunk_copy(j, 2, 1)))
            if j != 3:
                when(row_0, lambda: action(chunk_copy(j, 0, 0)))

    def hand_on(j):
        cross_copy(j).wait_recv()
        hand(j, lambda copy: copy.start())

    def hand_top(action):
        when(top, lambda: action(chunk_copy(0, 0, 1)))

    def hand_bottom(action):
        when(row_1, lambda: action(chunk_copy(3, -2, 0)))

    def thin_copy(which, step, sent, received, side=colour):
        return hand_copy(held(thin_t, thin_m, which, side), step, sent, received)

    def thin_up():
        return thin_copy(mine, 2, thin_send.at[0], thin_recv.at[0])

    def thin_down():
        return thin_copy(mine, -2, thin_send.at[0], thin_recv.at[0])

    def thin_side(which, at, side=colour):
        return thin_copy(which, 0, thin_send.at[at], thin_recv.at[at], side)

    def hand_thin():
        cross_thin().wait_recv()
        thin_side(mine, 1).start()
        when(upper == 1, lambda: thin_down().start())

    def raise_thin():
        when(upper == 0, lambda: thin_up().start())

    def share_thin():
        thin_copy(1 - mine, 2, thin_send.at[0], thin_recv.at[0], 1 - colour).wait_recv()
        thin_side(1 - mine, 2, 1 - colour).start()

    def await_weights():
        for j in range(len(chunks)):
            hand_copy(held(*chunks[j], 1 - colour), 0, f_send.at[j, 0], f_recv.at[j]).wait_recv()
        thin_side(mine, 1, 1 - colour).wait_recv()

    def await_thin():
        thin_side(1 - mine, 2).wait_recv()

    core_copies = [
        across(ref.at[pl.ds(partner(h, 1) * rows, rows), :], weights.at[1, m], c_send.at[m], c_recv.at[m], 1)
        for m, ref in enumerate(w_refs)
    ]
    own_copies = [
        pltpu.make_async_copy(ref.at[pl.ds(h * rows, rows), :], weights.at[0, m], w_own.at[m])
        for m, ref in enumerate(w_refs)
    ]

    def key_copy(g):
        return along(key_true.at[g], raw_far.at[g], kf_send.at[g], kf_recv.at[g], 2)

    piece = tokens // PIECES
    halo_refs = (value, smooth)

    def slot(kind, g, base, p):
        return halo_refs[kind].at[g, base + p * piece : base + (p + 1) * piece]

    def far_copy(kind, g, p):
        at = (kind, g, p, FAR)
        return along(slot(kind, g, own, p), slot(kind, g, 0, p), h_send.at[FAR], h_recv.at[at], 2)

    def near_copy(kind, g, p):
        at = (kind, g, p, NEAR)
        return along(slot(kind, g, own, p), slot(kind, g, tokens, p), h_send.at[NEAR], h_recv.at[at], 1)

    def relay_copy(kind, g, p):
        at = (kind, g, p, NEAR)
        return along(slot(kind, g, 0, p), slot(kind, g, tokens, p), h_send.at[NEAR], h_recv.at[at], -1)

    def send_far(kind, g):
        for p in range(PIECES):
            when(b + 2 < n, lambda: far_copy(kind, g, p).start())

    def send_near(kind, g):
        for p in range(PIECES):
            when(even, lambda: near_copy(kind, g, p).start())

    def relay(kind, g):
        for p in range(PIECES):
            @pl.when(odd & (b >= 2))
            def _():
                far_copy(kind, g, p).wait_recv()
                relay_copy(kind, g, p).start()

    def await_far(kind, g):
        for p in range(PIECES):
            when(even & (b >= 2), lambda: far_copy(kind, g, p).wait_recv())

    def await_near(kind, g):
        for p in range(PIECES):
            when(b >= 1, lambda: near_copy(kind, g, p).wait_recv())

    def near_sum():
        return along(total_own, total_near, t_send.at[0], t_recv.at[0], 1)

    def await_heads(g):
        for m, ref in enumerate((q_all, do_all)):
            pltpu.make_async_copy(ref.at[g], ref.at[g], qd_sem.at[g, m]).wait()

    def rows_of(p, base=0):
        return slice(base + p * piece, base + (p + 1) * piece)

    def grad_copy(m, g, over, p, step):
        at = (m, g, over, rows_of(p))
        return along(grad_out.at[at], grad_in.at[at], g_send.at[over], g_recv.at[m, g, over, p], step)

    def true_keys(g):
        for j in range(tiles):
            at = slice(j * TILE, (j + 1) * TILE)
            key_true[g, at] = (k_in[at, cols(g)].astype(F32) * power_of_two(ke_in[g : g + 1, j : j + 1])).astype(BF16)

    def true_values(g):
        for j in range(tiles):
            at = slice(j * TILE, (j + 1) * TILE)
            value[g, own + j * TILE : own + (j + 1) * TILE] = (
                v_in[at, cols(g)].astype(F32) * power_of_two(ve_in[g : g + 1, j : j + 1])
            ).astype(BF16)

    def sum_keys():
        for g in range(heads):
            total_own[:, cols(g)] = jnp.broadcast_to(
                jnp.sum(key_true[g].astype(F32), axis=0, keepdims=True), (8, D)
            )
        when(b + 1 < n, lambda: near_sum().start())

    def clear():
        @pl.when(b < 1)
        def _():
            total_near[...] = jnp.zeros_like(total_near)
            for g in range(heads):
                value[g, tokens:own, :] = jnp.zeros((tokens, D), BF16)
                smooth[g, tokens:own, :] = jnp.zeros((tokens, D), BF16)

        @pl.when(b < 2)
        def _():
            raw_far[...] = jnp.zeros_like(raw_far)
            for g in range(heads):
                value[g, 0:tokens, :] = jnp.zeros((tokens, D), BF16)
                smooth[g, 0:tokens, :] = jnp.zeros((tokens, D), BF16)
                for m in range(2):
                    grad_in[m, g, OVER_Y] = jnp.zeros((tokens, D), BF16)

        @pl.when(top)
        def _():
            for g in range(heads):
                for m in range(2):
                    grad_in[m, g, OVER_Z] = jnp.zeros((tokens, D), BF16)

        blank = jnp.zeros((TILE, width), BF16)
        for ref in (shares_all, score_all):
            for g in range(heads):
                for i in range(0, tiles, 2):
                    ref[g, i * TILE : (i + 1) * TILE, (i + 1) * width : (i + 2) * width] = blank
                    ref[g, own + (i + 1) * TILE : own + (i + 2) * TILE, i * width : (i + 1) * width] = blank

    row_at = lax.broadcasted_iota(jnp.int32, (tokens, tokens), 0)
    col_at = lax.broadcasted_iota(jnp.int32, (tokens, tokens), 1)
    lower = jnp.where(row_at >= col_at, 1.0, 0.0).astype(BF16)
    place = b * tokens + lax.broadcasted_iota(jnp.int32, (tokens, 1), 0)
    counts = jnp.clip(place + 1, 1, ATTEND_WINDOW).astype(F32)

    def running_keys(g):
        own_sum[g] = jnp.dot(lower, key_true[g], preferred_element_type=F32)

    def smooth_keys(g):
        when(b >= 2, lambda: key_copy(g).wait_recv())
        far = jnp.dot(lower, raw_far[g], preferred_element_type=F32)
        mean = (own_sum[g] - far + far[tokens - 1 :, :] + total_near[0:1, cols(g)]) / counts
        smooth[g, own : own + tokens, :] = (key_true[g].astype(F32) - mean).astype(BF16)
        send_far(S, g)
        send_near(S, g)

    row = lax.broadcasted_iota(jnp.int32, (TILE, width), 0)
    lane = lax.rem(lax.broadcasted_iota(jnp.int32, (1, width), 1), TILE)
    unit = jnp.where(
        lax.broadcasted_iota(jnp.int32, (TILE, TILE), 0) == lax.broadcasted_iota(jnp.int32, (TILE, TILE), 1), 1.0, 0.0
    )

    def lanes_of(i):
        return slice(i * width, (i + 1) * width)

    def keys_of(part, i):
        return (slice(i * TILE, tokens), slice(tokens, own), slice(own, own + (i + 1) * TILE))[part]

    def attend(g, part):
        for i in range(tiles):
            at, lanes = keys_of(part, i), lanes_of(i)
            scores = contract_last(smooth[g, at, :], q_all[g, lanes, :])
            if part == 0:
                edge = jnp.where(row > lane, scores[:TILE], -jnp.inf)
                scores = edge if i == tiles - 1 else jnp.concatenate([edge, scores[TILE:]], 0)
            if part == 2:
                edge = jnp.where(row <= lane, scores[i * TILE :], -jnp.inf)
                scores = edge if i == 0 else jnp.concatenate([scores[: i * TILE], edge], 0)
            highest = jnp.maximum(jnp.max(scores, axis=0, keepdims=True), LOWEST)
            powers = jnp.exp2((scores - highest) * (scale * LOG2_E))
            shares_all[g, at, lanes] = powers.astype(BF16)
            stats[g, part, 0:1, lanes] = highest
            stats[g, part, 1:2, lanes] = jnp.sum(powers, axis=0, keepdims=True)

    def combine(g):
        present = (b >= 2, b >= 1, b >= 0)
        tops = [jnp.where(here, stats[g, part, 0:1, :], LOWEST) for part, here in enumerate(present)]
        highest = jnp.maximum(jnp.maximum(tops[0], tops[1]), tops[2])
        powers = [
            jnp.where(here, jnp.exp2((top - highest) * (scale * LOG2_E)), 0.0) for top, here in zip(tops, present)
        ]
        total = sum(power * stats[g, part, 1:2, :] for part, power in enumerate(powers))
        inverse = 1.0 / total
        for part in range(3):
            factor = powers[part] * inverse
            stats[g, part, 0:1, :] = factor.astype(BF16).astype(F32)
            for k in range(group * tiles):
                at = slice(k * TILE, (k + 1) * TILE)
                spread = (unit * factor[:, at]).astype(BF16)
                do_part[g, part, at, :] = jnp.dot(
                    spread, do_all[g, at, :], preferred_element_type=F32
                ).astype(BF16)

    def differentiate(g):
        for i in range(tiles):
            lanes = lanes_of(i)
            row_dot, parts = 0.0, []
            for part in range(3):
                at = keys_of(part, i)
                share_grad = contract_last(value[g, at, :], do_part[g, part, lanes, :])
                shares = shares_all[g, at, lanes].astype(F32)
                row_dot = row_dot + jnp.sum(shares * share_grad, axis=0, keepdims=True)
                parts.append((at, shares, share_grad))
            for part, (at, shares, share_grad) in enumerate(parts):
                shift = row_dot * stats[g, part, 0:1, lanes]
                score_all[g, at, lanes] = (shares * (share_grad - shift)).astype(BF16)

    def key_grads(m, g, part, at, lanes):
        if m == 0:
            return jnp.dot(score_all[g, at, lanes], q_all[g, lanes, :], preferred_element_type=F32) * scale
        return jnp.dot(shares_all[g, at, lanes], do_part[g, part, lanes, :], preferred_element_type=F32)

    def near_grads(m, g):
        for p in range(PIECES):
            grads = key_grads(m, g, 1, rows_of(p, tokens), slice(0, group * tokens))
            grad_out[m, g, OVER_Y, rows_of(p)] = grads.astype(BF16)

    def send_near_grads(m, g):
        for p in range(PIECES):
            when(even & (b >= 2), lambda: grad_copy(m, g, OVER_Y, p, 1).start())
            when(odd, lambda: grad_copy(m, g, OVER_Y, p, -1).start())

    def far_grads(m, g):
        for p in range(PIECES):
            grads = key_grads(m, g, 0, rows_of(p), slice(0, (p + 1) * group * piece))
            far_grad[m, g, rows_of(p)] = grads

            @pl.when(even & (b >= 2))
            def _():
                grad_out[m, g, OVER_Z, rows_of(p)] = far_grad[m, g, rows_of(p)].astype(BF16)
                grad_copy(m, g, OVER_Z, p, -2).start()

    def join_grads(m, g):
        for p in range(PIECES):
            @pl.when(odd & (b >= 2))
            def _():
                grad_copy(m, g, OVER_Y, p, 1).wait_recv()
                both = far_grad[m, g, rows_of(p)] + grad_in[m, g, OVER_Y, rows_of(p)].astype(F32)
                grad_out[m, g, OVER_Z, rows_of(p)] = both.astype(BF16)
                grad_copy(m, g, OVER_Z, p, -2).start()

    def own_grads(m, g):
        for p in range(PIECES):
            own_grad[m, g, rows_of(p)] = key_grads(
                m, g, 2, rows_of(p, own), slice(p * group * piece, group * tokens)
            )

    def query_grads(g):
        smooth_t[...] = smooth[g].astype(F32).T.astype(BF16)
        for i in range(tiles):
            window = slice(i * TILE, i * TILE + SPAN)
            dq = jnp.dot(
                smooth_t[:, window], score_all[g, window, i * width : (i + 1) * width],
                preferred_element_type=F32,
            ) * scale
            dq = dq.T.astype(BF16)
            for u in range(group):
                dq_ref[i * TILE : (i + 1) * TILE, cols(g * group + u)] = dq[u * TILE : (u + 1) * TILE]

    def share_copy(m, g, p, t):
        at = (m, g) if p is None else (m, g, rows_of(p))
        return across(scaled.at[at], gathered.at[(t - 1,) + at], s_send.at[t - 1], s_recv.at[t - 1, m, g], t)

    def onward_copy(m, g, t):
        return across(gathered.at[t - 1, m, g], gathered.at[t, m, g], s_send.at[t], s_recv.at[t, m, g], 1)

    far_steps = list(range(2, nh, 2))

    def finish(m, g):
        exponent = (ke_in, ve_in)[m]
        for p in range(PIECES):
            when(even, lambda: grad_copy(m, g, OVER_Y, p, -1).wait_recv())
            when(b + 2 < n, lambda: grad_copy(m, g, OVER_Z, p, -2).wait_recv())
            for r in range(p * tiles // PIECES, (p + 1) * tiles // PIECES):
                at = slice(r * TILE, (r + 1) * TILE)
                whole = own_grad[m, g, at] + grad_in[m, g, OVER_Z, at].astype(F32)
                whole = whole + jnp.where(even, grad_in[m, g, OVER_Y, at].astype(F32), 0.0)
                scaled[m, g, at] = (whole * power_of_two(exponent[g : g + 1, r : r + 1])).astype(BF16)
            for t in far_steps + [1]:
                share_copy(m, g, p, t).start()

    def pass_on(m, g):
        for t in far_steps:
            share_copy(m, g, None, t).wait_recv()
            onward_copy(m, g, t).start()

    def await_core(g):
        for m in range(2):
            share_copy(m, g, None, 1).wait_recv()

    def await_onward(g):
        for m in range(2):
            for t in far_steps:
                onward_copy(m, g, t).wait_recv()

    chunk = rows // CHUNKS

    def product(ts, g, fresh, base=0, count=CHUNKS):
        def one_chunk(k, carry):
            c = base + k
            at = pl.ds(pl.multiple_of(c * chunk, 16), chunk)
            total = None if fresh else acc[at, :]
            for t in ts:
                left = jnp.concatenate([weights[t, 0, at, cols(g)], weights[t, 1, at, cols(g)]], 1)
                if t == 0:
                    right = jnp.concatenate([scaled[0, g], scaled[1, g]], 1)
                else:
                    right = jnp.concatenate([gathered[t - 1, 0, g], gathered[t - 1, 1, g]], 1)
                term = contract_last(left, right)
                total = term if total is None else total + term
            acc[at, :] = total
            return carry

        lax.fori_loop(0, count, one_chunk, 0)

    pl.semaphore_wait(barrier, greeted)
    for copy in loads: copy.wait()
    cross_thin().start()
    for j in range(len(chunks)): cross_copy(j).start()
    for g in range(heads): true_keys(g)
    sum_keys()
    for g in range(heads): when(b + 2 < n, lambda: key_copy(g).start())
    for g in range(heads):
        true_values(g)
        send_near(V, g)
    for copy in core_copies + own_copies: copy.start()
    clear()
    for g in range(heads): running_keys(g)
    when(b >= 1, lambda: near_sum().wait_recv())
    smooth_keys(0)
    hand_thin()
    smooth_keys(1)
    for g in range(heads): send_far(V, g)
    raise_thin()
    for g in range(heads): await_heads(g)
    attend(0, 2)
    attend(1, 2)
    relay(S, 0)
    hand_on(0)
    await_far(S, 0)
    attend(0, 0)
    when(row_0, share_thin)
    relay(S, 1)
    await_far(S, 1)
    attend(1, 0)
    hand_on(1)
    await_near(S, 0)
    attend(0, 1)
    combine(0)
    relay(V, 0)
    near_grads(1, 0)
    when(even, lambda: send_near_grads(1, 0))
    far_grads(1, 0)
    relay(V, 1)
    when(odd, lambda: send_near_grads(1, 0))
    await_near(S, 1)
    attend(1, 1)
    hand_on(2)
    combine(1)
    near_grads(1, 1)
    send_near_grads(1, 1)
    far_grads(1, 1)
    await_far(V, 0)
    await_near(V, 0)
    join_grads(1, 0)
    differentiate(0)
    near_grads(0, 0)
    send_near_grads(0, 0)
    hand_on(3)
    await_far(V, 1)
    await_near(V, 1)
    join_grads(1, 1)
    differentiate(1)
    near_grads(0, 1)
    send_near_grads(0, 1)
    hand_on(4)
    when(b >= 2, share_thin)
    hand_top(lambda copy: copy.start())
    far_grads(0, 0)
    far_grads(0, 1)
    for m in (1, 0): own_grads(m, 0)
    join_grads(0, 0)
    finish(1, 0)
    for m in (1, 0): own_grads(m, 1)
    hand_on(5)
    join_grads(0, 1)
    hand_bottom(lambda copy: copy.start())
    finish(1, 1)
    query_grads(0)
    finish(0, 0)
    query_grads(1)
    for copy in own_copies: copy.wait()
    for copy in core_copies: copy.wait_recv()
    await_core(0)
    product((0, 1), 0, True)
    finish(0, 1)
    await_core(1)
    product((0, 1), 1, False)
    for m in (1, 0): pass_on(m, 0)
    await_onward(0)
    await_thin()
    product(crossing, 0, False, 2 * colour, 2)
    for m in (1, 0): pass_on(m, 1)
    await_weights()
    product(crossing, 0, False, 2 - 2 * colour, 2)
    await_onward(1)

    when(b + 1 < n, lambda: near_sum().wait_send())
    for g in range(heads):
        when(b + 2 < n, lambda: key_copy(g).wait_send())
    halo = value.at[:, 0:own]
    when(b + 2 < n, lambda: along(halo, halo, h_send.at[FAR], h_recv.at[0, 0, 0, FAR], 2).wait_send())
    when(even | (b >= 2), lambda: along(halo, halo, h_send.at[NEAR], h_recv.at[0, 0, 0, FAR], 2).wait_send())
    for over, condition in ((OVER_Y, odd | (b >= 2)), (OVER_Z, b >= 2)):
        ref = grad_out.at[:, :, over]
        when(condition, lambda: along(ref, ref, g_send.at[over], g_recv.at[0, 0, 0, 0], 2).wait_send())
    for t in range(1, nh):
        across(scaled, scaled, s_send.at[t - 1], s_recv.at[0, 0, 0], 1).wait_send()
    cross_thin().wait_send()
    thin_up().wait_send()
    thin_side(mine, 1).wait_send()
    thin_side(1 - mine, 2, 1 - colour).wait_send()
    for j in range(len(chunks)):
        cross_copy(j).wait_send()
        hand(j, lambda copy: copy.wait_send())
    hand_top(lambda copy: copy.wait_send())
    hand_bottom(lambda copy: copy.wait_send())
    for copy in core_copies:
        copy.wait_send()


def last_product(nh, heads, dq_ref, gathered, weights, acc, dq_out, grad_rows, out_ref, sem):
    rows = acc.shape[0]
    chunk = rows // CHUNKS
    g = heads - 1
    cols = slice(g * D, (g + 1) * D)
    query_copy = pltpu.make_async_copy(dq_ref, dq_out, sem.at[CHUNKS])
    query_copy.start()
    copies = []
    for c in range(CHUNKS):
        at = slice(c * chunk, (c + 1) * chunk)
        total = acc[at, :]
        for t in range(2, nh):
            left = jnp.concatenate([weights[t, 0, at, cols], weights[t, 1, at, cols]], 1)
            right = jnp.concatenate([gathered[t - 1, 0, g], gathered[t - 1, 1, g]], 1)
            total = total + contract_last(left, right)
        out_ref[at, :] = total.astype(BF16)
        copies.append(pltpu.make_async_copy(out_ref.at[at, :], grad_rows.at[at, :], sem.at[c]))
        copies[-1].start()
    query_copy.wait()
    for copy in copies:
        copy.wait()


def solution(mesh):
    n, nh = mesh.shape["seq"], mesh.shape["head"]
    assert n % 8 == 0 and nh >= 4

    def local(q, k, v, do, ke, ve, wk, wv):
        tokens, width = k.shape
        heads = width // HEAD_SIZE
        group = q.shape[1] // width
        tiles = tokens // TILE
        assert ATTEND_WINDOW == 2 * tokens
        rows = wk.shape[0] // nh
        n_chunks = 4 * (nh - 2)
        hbm = pl.BlockSpec(memory_space=pltpu.HBM)
        dma = pltpu.SemaphoreType.DMA
        vmem = pl.BlockSpec(memory_space=pltpu.VMEM)
        parts = pl.pallas_call(
            functools.partial(kernel, n, nh),
            out_shape=(
                pltpu.VMEM(q.shape, BF16),
                pltpu.VMEM((nh - 1, 2, heads, tokens, D), BF16),
                pltpu.VMEM((nh, 2, rows, width), BF16),
                pltpu.VMEM((rows, tokens), F32),
            ),
            in_specs=[hbm] * 8,
            out_specs=(vmem,) * 4,
            scratch_shapes=[
                pltpu.VMEM((tokens, width), BF16),
                pltpu.VMEM((tokens, width), BF16),
                pltpu.VMEM((heads, tiles), jnp.int32),
                pltpu.VMEM((heads, tiles), jnp.int32),
                pltpu.VMEM((heads, group * tokens, D), BF16),
                pltpu.VMEM((heads, group * tokens, D), BF16),
                pltpu.VMEM((heads, tokens, D), BF16),
                pltpu.VMEM((heads, tokens, D), BF16),
                pltpu.VMEM((heads, tokens, D), F32),
                pltpu.VMEM((8, width), F32),
                pltpu.VMEM((8, width), F32),
                pltpu.VMEM((heads, 3 * tokens, D), BF16),
                pltpu.VMEM((heads, 3 * tokens, D), BF16),
                pltpu.VMEM((D, 3 * tokens), BF16),
                pltpu.VMEM((heads, 3 * tokens, group * tokens), BF16),
                pltpu.VMEM((heads, 3 * tokens, group * tokens), BF16),
                pltpu.VMEM((heads, 3, 2, group * tokens), F32),
                pltpu.VMEM((heads, 3, group * tokens, D), BF16),
                pltpu.VMEM((2, heads, tokens, D), F32),
                pltpu.VMEM((2, heads, tokens, D), F32),
                pltpu.VMEM((2, heads, 2, tokens, D), BF16),
                pltpu.VMEM((2, heads, 2, tokens, D), BF16),
                pltpu.VMEM((2, heads, tokens, D), BF16),
                dma((4,)), dma((heads, 2)), dma((2,)),
                dma((heads,)), dma((heads,)), dma((1,)), dma((1,)),
                dma((2,)), dma((2, heads, PIECES, 2)),
                dma((n_chunks - 1,)), dma((n_chunks - 1,)), dma((n_chunks - 2, 2)), dma((n_chunks - 2,)), dma((3,)), dma((3,)),
                dma((2,)), dma((2,)),
                dma((2,)), dma((2, heads, 2, PIECES)),
                dma((nh - 1,)), dma((nh - 1, 2, heads)),
            ],
            compiler_params=pltpu.CompilerParams(
                collective_id=0, has_side_effects=True, vmem_limit_bytes=48 * 2**20
            ),
        )(*[pltpu.with_memory_space_constraint(x, pltpu.HBM) for x in (q, k, v, do, ke.T, ve.T, wk, wv)])
        return pl.pallas_call(
            functools.partial(last_product, nh, heads),
            out_shape=(
                jax.ShapeDtypeStruct(q.shape, BF16),
                jax.ShapeDtypeStruct((rows, tokens), BF16),
            ),
            in_specs=[vmem] * 4,
            out_specs=(pl.BlockSpec(memory_space=pl.ANY),) * 2,
            scratch_shapes=[pltpu.VMEM((rows, tokens), BF16), dma((CHUNKS + 1,))],
            compiler_params=pltpu.CompilerParams(vmem_limit_bytes=24 * 2**20),
        )(*[pltpu.with_memory_space_constraint(x, pltpu.VMEM) for x in parts])

    in_specs = (P("seq", "head"),) * 6 + (P(None, "head"),) * 2
    out_specs = (P("seq", "head"), P("head", "seq"))
    return jax.shard_map(local, mesh=mesh, in_specs=in_specs, out_specs=out_specs, check_vma=False)
```

```python
import functools

import jax
import jax.numpy as jnp
from jax import lax
from jax.experimental import pallas as pl
from jax.experimental.pallas import tpu as pltpu
from jax.sharding import PartitionSpec as P

HEAD_SIZE = 128
QUERY_SCALE = 168
ATTEND_WINDOW = 1024
SCALE_BLOCK = 128
LOG2_E = 1.4426950408889634
LOWEST = -1e30
MESH = pl.DeviceIdType.MESH
F32 = jnp.float32
BF16 = jnp.bfloat16
D = HEAD_SIZE
TILE = SCALE_BLOCK
SPAN = ATTEND_WINDOW + TILE
PIECES = 2
CHUNKS = 2
LAST_CHUNKS = 4
V, S = 0, 1
FAR, NEAR = 0, 1
OVER_Y, OVER_Z = 0, 1


def power_of_two(exponent):
    return jnp.where(exponent > 0, 2.0, jnp.where(exponent < 0, 0.5, 1.0)).astype(F32)


def contract_last(a, b):
    return lax.dot_general(a, b, (((1,), (1,)), ((), ())), preferred_element_type=F32)


def partner(h, t):
    other, bit = h, 1
    while bit <= t:
        if t & bit:
            other = other + bit - 2 * bit * lax.rem(lax.div(h, bit), 2)
        bit *= 2
    return other


def kernel(
    n, nh, q_ref, k_ref, v_ref, do_ref, ke_ref, ve_ref, wk_ref, wv_ref, dq_ref, gathered, weights, acc,
    k_in, v_in, ke_in, ve_in, q_all, do_all, key_true, raw_far, own_sum, total_own, total_near, smooth, value, smooth_t,
    shares_all, score_all, stats, do_part, far_grad, own_grad, grad_out, grad_in, scaled,
    in_sem, qd_sem, w_own, kf_send, kf_recv, t_send, t_recv, h_send, h_recv,
    w_send, w_recv, f_send, f_recv, thin_send, thin_recv, c_send, c_recv, g_send, g_recv, s_send, s_recv,
):
    tokens = k_ref.shape[0]
    heads = k_ref.shape[1] // D
    group = q_ref.shape[1] // (heads * D)
    width = group * TILE
    tiles = tokens // TILE
    rows = acc.shape[0]
    own = 2 * tokens
    scale = QUERY_SCALE ** (-0.5)
    b = lax.axis_index("seq")
    h = lax.axis_index("head")
    odd = lax.rem(b, 2) == 1
    even = lax.rem(b, 2) == 0
    colour = lax.rem(lax.rem(b, 2) + lax.div(b, 2), 2)
    crossing = list(range(2, nh))

    def cols(g):
        return slice(g * D, (g + 1) * D)

    loads = [
        pltpu.make_async_copy(k_ref, k_in, in_sem.at[0]),
        pltpu.make_async_copy(v_ref, v_in, in_sem.at[1]),
        pltpu.make_async_copy(ke_ref, ke_in, in_sem.at[2]),
        pltpu.make_async_copy(ve_ref, ve_in, in_sem.at[3]),
    ]
    for copy in loads:
        copy.start()
    head_loads = []
    for g in range(heads):
        for m, (ref, dst) in enumerate(((q_ref, q_all), (do_ref, do_all))):
            for i in range(tiles):
                for u in range(group):
                    head_loads.append(
                        pltpu.make_async_copy(
                            ref.at[i * TILE : (i + 1) * TILE, cols(g * group + u)],
                            dst.at[g, (i * group + u) * TILE : (i * group + u + 1) * TILE, :],
                            qd_sem.at[g, m],
                        )
                    )
    for copy in head_loads:
        copy.start()

    barrier = pltpu.get_barrier_semaphore()

    def greet(step):
        pl.semaphore_signal(
            barrier, inc=1, device_id={"seq": lax.rem(b + n + step, n)}, device_id_type=MESH
        )

    for step in (1, 2):
        pl.when(b + step < n)(lambda: greet(step))
        pl.when(b >= step)(lambda: greet(-step))
    for t in range(1, nh):
        pl.semaphore_signal(barrier, inc=1, device_id={"head": partner(h, t)}, device_id_type=MESH)
    greeted = nh - 1 + jnp.minimum(b, 2) + jnp.minimum(n - 1 - b, 2)

    def when(condition, action):
        pl.when(condition)(action)

    def along(src, dst, send, recv, step):
        return pltpu.make_async_remote_copy(
            src_ref=src, dst_ref=dst, send_sem=send, recv_sem=recv,
            device_id={"seq": lax.rem(b + n + step, n)}, device_id_type=MESH,
        )

    def across(src, dst, send, recv, t):
        return pltpu.make_async_remote_copy(
            src_ref=src, dst_ref=dst, send_sem=send, recv_sem=recv,
            device_id={"head": partner(h, t)}, device_id_type=MESH,
        )

    def when(condition, *steps):
        @pl.when(condition)
        def _():
            for step in steps:
                step()

    half = rows // 2
    part = half // 2
    chunks = [(t, m, q) for t in crossing for m in range(2) for q in range(2)]
    thin_t, thin_m = chunks[-1][:2]
    chunks = chunks[:-2]
    w_refs = (wk_ref, wv_ref)
    z = lax.div(b, 2)
    upper = lax.rem(z, 2)
    mine = lax.rem(lax.div(lax.rem(z, 4) + 1, 2), 2)
    row_0 = b < 2
    row_1 = (b >= 2) & (b < 4)
    top = b + 2 >= n
    below_top = (b + 2 < n) & (b + 4 >= n)

    def held(t, m, q, side):
        return weights.at[t, m, pl.ds(side * half + q * part, part), :]

    def cross(t, m, q, j):
        return across(
            w_refs[m].at[pl.ds(partner(h, t) * rows + colour * half + q * part, part), :],
            held(t, m, q, colour), w_send.at[j], w_recv.at[j], t,
        )

    def cross_copy(j):
        return cross(*chunks[j], j)

    def cross_thin():
        return cross(thin_t, thin_m, mine, len(chunks))

    def hand_copy(ref, step, sent, received):
        if step:
            return along(ref, ref, sent, received, step)
        return pltpu.make_async_remote_copy(
            src_ref=ref, dst_ref=ref, send_sem=sent, recv_sem=received,
            device_id={"seq": partner(b, 1)}, device_id_type=MESH,
        )

    def chunk_copy(j, step, which):
        return hand_copy(held(*chunks[j], colour), step, f_send.at[j, which], f_recv.at[j])

    def hand(j, action):
        if j < 2:
            when(b >= 2, lambda: action(chunk_copy(j, -2, 0)))
            if j > 0:
                when(below_top, lambda: action(chunk_copy(j, 2, 1)))
        else:
            when(b + 2 < n, lambda: action(chunk_copy(j, 2, 1)))
            if j != 3:
                when(row_0, lambda: action(chunk_copy(j, 0, 0)))

    def hand_on(j):
        cross_copy(j).wait_recv()
        hand(j, lambda copy: copy.start())

    def hand_top(action):
        when(top, lambda: action(chunk_copy(0, 0, 1)))

    def hand_bottom(action):
        when(row_1, lambda: action(chunk_copy(3, -2, 0)))

    def thin_copy(which, step, sent, received, side=colour):
        return hand_copy(held(thin_t, thin_m, which, side), step, sent, received)

    def thin_up():
        return thin_copy(mine, 2, thin_send.at[0], thin_recv.at[0])

    def thin_down():
        return thin_copy(mine, -2, thin_send.at[0], thin_recv.at[0])

    def thin_side(which, at, side=colour):
        return thin_copy(which, 0, thin_send.at[at], thin_recv.at[at], side)

    def hand_thin():
        cross_thin().wait_recv()
        thin_side(mine, 1).start()
        when(upper == 1, lambda: thin_down().start())

    def raise_thin():
        when(upper == 0, lambda: thin_up().start())

    def share_thin():
        thin_copy(1 - mine, 2, thin_send.at[0], thin_recv.at[0], 1 - colour).wait_recv()
        thin_side(1 - mine, 2, 1 - colour).start()

    def await_weights():
        for j in range(len(chunks)):
            hand_copy(held(*chunks[j], 1 - colour), 0, f_send.at[j, 0], f_recv.at[j]).wait_recv()
        thin_side(mine, 1, 1 - colour).wait_recv()

    def await_thin():
        thin_side(1 - mine, 2).wait_recv()

    core_copies = [
        across(ref.at[pl.ds(partner(h, 1) * rows, rows), :], weights.at[1, m], c_send.at[m], c_recv.at[m], 1)
        for m, ref in enumerate(w_refs)
    ]
    own_copies = [
        pltpu.make_async_copy(ref.at[pl.ds(h * rows, rows), :], weights.at[0, m], w_own.at[m])
        for m, ref in enumerate(w_refs)
    ]

    def key_copy(g):
        return along(key_true.at[g], raw_far.at[g], kf_send.at[g], kf_recv.at[g], 2)

    piece = tokens // PIECES
    halo_refs = (value, smooth)

    def slot(kind, g, base, p):
        return halo_refs[kind].at[g, base + p * piece : base + (p + 1) * piece]

    def far_copy(kind, g, p):
        at = (kind, g, p, FAR)
        return along(slot(kind, g, own, p), slot(kind, g, 0, p), h_send.at[FAR], h_recv.at[at], 2)

    def near_copy(kind, g, p):
        at = (kind, g, p, NEAR)
        return along(slot(kind, g, own, p), slot(kind, g, tokens, p), h_send.at[NEAR], h_recv.at[at], 1)

    def relay_copy(kind, g, p):
        at = (kind, g, p, NEAR)
        return along(slot(kind, g, 0, p), slot(kind, g, tokens, p), h_send.at[NEAR], h_recv.at[at], -1)

    def send_far(kind, g):
        for p in range(PIECES):
            when(b + 2 < n, lambda: far_copy(kind, g, p).start())

    def send_near(kind, g):
        for p in range(PIECES):
            when(even, lambda: near_copy(kind, g, p).start())

    def relay(kind, g):
        for p in range(PIECES):
            @pl.when(odd & (b >= 2))
            def _():
                far_copy(kind, g, p).wait_recv()
                relay_copy(kind, g, p).start()

    def await_far(kind, g):
        for p in range(PIECES):
            when(even & (b >= 2), lambda: far_copy(kind, g, p).wait_recv())

    def await_near(kind, g):
        for p in range(PIECES):
            when(b >= 1, lambda: near_copy(kind, g, p).wait_recv())

    def near_sum():
        return along(total_own, total_near, t_send.at[0], t_recv.at[0], 1)

    def await_heads(g):
        for m, ref in enumerate((q_all, do_all)):
            pltpu.make_async_copy(ref.at[g], ref.at[g], qd_sem.at[g, m]).wait()

    def rows_of(p, base=0):
        return slice(base + p * piece, base + (p + 1) * piece)

    def grad_copy(m, g, over, p, step):
        at = (m, g, over, rows_of(p))
        return along(grad_out.at[at], grad_in.at[at], g_send.at[over], g_recv.at[m, g, over, p], step)

    def true_keys(g):
        for j in range(tiles):
            at = slice(j * TILE, (j + 1) * TILE)
            key_true[g, at] = (k_in[at, cols(g)].astype(F32) * power_of_two(ke_in[g : g + 1, j : j + 1])).astype(BF16)

    def true_values(g):
        for j in range(tiles):
            at = slice(j * TILE, (j + 1) * TILE)
            value[g, own + j * TILE : own + (j + 1) * TILE] = (
                v_in[at, cols(g)].astype(F32) * power_of_two(ve_in[g : g + 1, j : j + 1])
            ).astype(BF16)

    def sum_keys():
        for g in range(heads):
            total_own[:, cols(g)] = jnp.broadcast_to(
                jnp.sum(key_true[g].astype(F32), axis=0, keepdims=True), (8, D)
            )

    def clear():
        @pl.when(b < 1)
        def _():
            total_near[...] = jnp.zeros_like(total_near)
            for g in range(heads):
                value[g, tokens:own, :] = jnp.zeros((tokens, D), BF16)
                smooth[g, tokens:own, :] = jnp.zeros((tokens, D), BF16)

        @pl.when(b < 2)
        def _():
            raw_far[...] = jnp.zeros_like(raw_far)
            for g in range(heads):
                value[g, 0:tokens, :] = jnp.zeros((tokens, D), BF16)
                smooth[g, 0:tokens, :] = jnp.zeros((tokens, D), BF16)
                for m in range(2):
                    grad_in[m, g, OVER_Y] = jnp.zeros((tokens, D), BF16)

        @pl.when(top)
        def _():
            for g in range(heads):
                for m in range(2):
                    grad_in[m, g, OVER_Z] = jnp.zeros((tokens, D), BF16)

        blank = jnp.zeros((TILE, width), BF16)
        for ref in (shares_all, score_all):
            for g in range(heads):
                for i in range(0, tiles, 2):
                    ref[g, i * TILE : (i + 1) * TILE, (i + 1) * width : (i + 2) * width] = blank
                    ref[g, own + (i + 1) * TILE : own + (i + 2) * TILE, i * width : (i + 1) * width] = blank

    row_at = lax.broadcasted_iota(jnp.int32, (tokens, tokens), 0)
    col_at = lax.broadcasted_iota(jnp.int32, (tokens, tokens), 1)
    lower = jnp.where(row_at >= col_at, 1.0, 0.0).astype(BF16)
    place = b * tokens + lax.broadcasted_iota(jnp.int32, (tokens, 1), 0)
    counts = jnp.clip(place + 1, 1, ATTEND_WINDOW).astype(F32)

    def running_keys(g):
        own_sum[g] = jnp.dot(lower, key_true[g], preferred_element_type=F32)

    def smooth_keys(g):
        when(b >= 2, lambda: key_copy(g).wait_recv())
        far = jnp.dot(lower, raw_far[g], preferred_element_type=F32)
        mean = (own_sum[g] - far + far[tokens - 1 :, :] + total_near[0:1, cols(g)]) / counts
        smooth[g, own : own + tokens, :] = (key_true[g].astype(F32) - mean).astype(BF16)
        send_far(S, g)
        send_near(S, g)

    row = lax.broadcasted_iota(jnp.int32, (TILE, width), 0)
    lane = lax.rem(lax.broadcasted_iota(jnp.int32, (1, width), 1), TILE)
    unit = jnp.where(
        lax.broadcasted_iota(jnp.int32, (TILE, TILE), 0) == lax.broadcasted_iota(jnp.int32, (TILE, TILE), 1), 1.0, 0.0
    )

    def lanes_of(i):
        return slice(i * width, (i + 1) * width)

    def keys_of(part, i):
        return (slice(i * TILE, tokens), slice(tokens, own), slice(own, own + (i + 1) * TILE))[part]

    def attend(g, part):
        for i in range(tiles):
            at, lanes = keys_of(part, i), lanes_of(i)
            scores = contract_last(smooth[g, at, :], q_all[g, lanes, :])
            if part == 0:
                edge = jnp.where(row > lane, scores[:TILE], -jnp.inf)
                scores = edge if i == tiles - 1 else jnp.concatenate([edge, scores[TILE:]], 0)
            if part == 2:
                edge = jnp.where(row <= lane, scores[i * TILE :], -jnp.inf)
                scores = edge if i == 0 else jnp.concatenate([scores[: i * TILE], edge], 0)
            highest = jnp.maximum(jnp.max(scores, axis=0, keepdims=True), LOWEST)
            powers = jnp.exp2((scores - highest) * (scale * LOG2_E))
            shares_all[g, at, lanes] = powers.astype(BF16)
            stats[g, part, 0:1, lanes] = highest
            stats[g, part, 1:2, lanes] = jnp.sum(powers, axis=0, keepdims=True)

    def combine(g):
        present = (b >= 2, b >= 1, b >= 0)
        tops = [jnp.where(here, stats[g, part, 0:1, :], LOWEST) for part, here in enumerate(present)]
        highest = jnp.maximum(jnp.maximum(tops[0], tops[1]), tops[2])
        powers = [
            jnp.where(here, jnp.exp2((top - highest) * (scale * LOG2_E)), 0.0) for top, here in zip(tops, present)
        ]
        total = sum(power * stats[g, part, 1:2, :] for part, power in enumerate(powers))
        inverse = 1.0 / total
        for part in range(3):
            factor = powers[part] * inverse
            stats[g, part, 0:1, :] = factor.astype(BF16).astype(F32)
            for k in range(group * tiles):
                at = slice(k * TILE, (k + 1) * TILE)
                spread = (unit * factor[:, at]).astype(BF16)
                do_part[g, part, at, :] = jnp.dot(
                    spread, do_all[g, at, :], preferred_element_type=F32
                ).astype(BF16)

    def differentiate(g):
        for i in range(tiles):
            lanes = lanes_of(i)
            row_dot, parts = 0.0, []
            for part in range(3):
                at = keys_of(part, i)
                share_grad = contract_last(value[g, at, :], do_part[g, part, lanes, :])
                shares = shares_all[g, at, lanes].astype(F32)
                row_dot = row_dot + jnp.sum(shares * share_grad, axis=0, keepdims=True)
                parts.append((at, shares, share_grad))
            for part, (at, shares, share_grad) in enumerate(parts):
                shift = row_dot * stats[g, part, 0:1, lanes]
                score_all[g, at, lanes] = (shares * (share_grad - shift)).astype(BF16)

    def key_grads(m, g, part, at, lanes):
        if m == 0:
            return jnp.dot(score_all[g, at, lanes], q_all[g, lanes, :], preferred_element_type=F32) * scale
        return jnp.dot(shares_all[g, at, lanes], do_part[g, part, lanes, :], preferred_element_type=F32)

    def near_grads(m, g):
        for p in range(PIECES):
            grads = key_grads(m, g, 1, rows_of(p, tokens), slice(0, group * tokens))
            grad_out[m, g, OVER_Y, rows_of(p)] = grads.astype(BF16)

    def send_near_grads(m, g):
        for p in range(PIECES):
            when(even & (b >= 2), lambda: grad_copy(m, g, OVER_Y, p, 1).start())
            when(odd, lambda: grad_copy(m, g, OVER_Y, p, -1).start())

    def far_grads(m, g):
        for p in range(PIECES):
            grads = key_grads(m, g, 0, rows_of(p), slice(0, (p + 1) * group * piece))
            far_grad[m, g, rows_of(p)] = grads

            @pl.when(even & (b >= 2))
            def _():
                grad_out[m, g, OVER_Z, rows_of(p)] = far_grad[m, g, rows_of(p)].astype(BF16)
                grad_copy(m, g, OVER_Z, p, -2).start()

    def join_grads(m, g):
        for p in range(PIECES):
            @pl.when(odd & (b >= 2))
            def _():
                grad_copy(m, g, OVER_Y, p, 1).wait_recv()
                both = far_grad[m, g, rows_of(p)] + grad_in[m, g, OVER_Y, rows_of(p)].astype(F32)
                grad_out[m, g, OVER_Z, rows_of(p)] = both.astype(BF16)
                grad_copy(m, g, OVER_Z, p, -2).start()

    def own_grads(m, g):
        for p in range(PIECES):
            own_grad[m, g, rows_of(p)] = key_grads(
                m, g, 2, rows_of(p, own), slice(p * group * piece, group * tokens)
            )

    def query_grads(g):
        smooth_t[...] = smooth[g].astype(F32).T.astype(BF16)
        for i in range(tiles):
            window = slice(i * TILE, i * TILE + SPAN)
            dq = jnp.dot(
                smooth_t[:, window], score_all[g, window, i * width : (i + 1) * width],
                preferred_element_type=F32,
            ) * scale
            dq = dq.T.astype(BF16)
            for u in range(group):
                dq_ref[i * TILE : (i + 1) * TILE, cols(g * group + u)] = dq[u * TILE : (u + 1) * TILE]

    def share_copy(m, g, p, t):
        at = (m, g) if p is None else (m, g, rows_of(p))
        return across(scaled.at[at], gathered.at[(t - 1,) + at], s_send.at[t - 1], s_recv.at[t - 1, m, g], t)

    def onward_copy(m, g, t):
        return across(gathered.at[t - 1, m, g], gathered.at[t, m, g], s_send.at[t], s_recv.at[t, m, g], 1)

    far_steps = list(range(2, nh, 2))

    def finish(m, g):
        exponent = (ke_in, ve_in)[m]
        for p in range(PIECES):
            when(even, lambda: grad_copy(m, g, OVER_Y, p, -1).wait_recv())
            when(b + 2 < n, lambda: grad_copy(m, g, OVER_Z, p, -2).wait_recv())
            for r in range(p * tiles // PIECES, (p + 1) * tiles // PIECES):
                at = slice(r * TILE, (r + 1) * TILE)
                whole = own_grad[m, g, at] + grad_in[m, g, OVER_Z, at].astype(F32)
                whole = whole + jnp.where(even, grad_in[m, g, OVER_Y, at].astype(F32), 0.0)
                scaled[m, g, at] = (whole * power_of_two(exponent[g : g + 1, r : r + 1])).astype(BF16)
            for t in far_steps + [1]:
                share_copy(m, g, p, t).start()

    def pass_on(m, g):
        for t in far_steps:
            share_copy(m, g, None, t).wait_recv()
            onward_copy(m, g, t).start()

    def await_core(g):
        for m in range(2):
            share_copy(m, g, None, 1).wait_recv()

    def await_onward(g):
        for m in range(2):
            for t in far_steps:
                onward_copy(m, g, t).wait_recv()

    chunk = rows // CHUNKS

    def product(ts, g, fresh, base=0, count=CHUNKS):
        def one_chunk(k, carry):
            c = base + k
            at = pl.ds(pl.multiple_of(c * chunk, 16), chunk)
            total = None if fresh else acc[at, :]
            for t in ts:
                left = jnp.concatenate([weights[t, 0, at, cols(g)], weights[t, 1, at, cols(g)]], 1)
                if t == 0:
                    right = jnp.concatenate([scaled[0, g], scaled[1, g]], 1)
                else:
                    right = jnp.concatenate([gathered[t - 1, 0, g], gathered[t - 1, 1, g]], 1)
                term = contract_last(left, right)
                total = term if total is None else total + term
            acc[at, :] = total
            return carry

        lax.fori_loop(0, count, one_chunk, 0)

    for copy in loads: copy.wait()
    for g in range(heads): true_keys(g)
    sum_keys()
    for g in range(heads): true_values(g)
    pl.semaphore_wait(barrier, greeted)
    when(b + 1 < n, lambda: near_sum().start())
    cross_thin().start()
    for j in range(len(chunks)): cross_copy(j).start()
    for g in range(heads): when(b + 2 < n, lambda: key_copy(g).start())
    for g in range(heads): send_near(V, g)
    for copy in core_copies + own_copies: copy.start()
    clear()
    for g in range(heads): running_keys(g)
    when(b >= 1, lambda: near_sum().wait_recv())
    smooth_keys(0)
    hand_thin()
    smooth_keys(1)
    for g in range(heads): send_far(V, g)
    raise_thin()
    for g in range(heads): await_heads(g)
    attend(0, 2)
    attend(1, 2)
    relay(S, 0)
    hand_on(0)
    await_far(S, 0)
    attend(0, 0)
    when(row_0, share_thin)
    relay(S, 1)
    await_far(S, 1)
    attend(1, 0)
    hand_on(1)
    await_near(S, 0)
    attend(0, 1)
    combine(0)
    relay(V, 0)
    near_grads(1, 0)
    when(even, lambda: send_near_grads(1, 0))
    far_grads(1, 0)
    relay(V, 1)
    when(odd, lambda: send_near_grads(1, 0))
    await_near(S, 1)
    attend(1, 1)
    hand_on(2)
    combine(1)
    near_grads(1, 1)
    send_near_grads(1, 1)
    far_grads(1, 1)
    await_far(V, 0)
    await_near(V, 0)
    join_grads(1, 0)
    differentiate(0)
    near_grads(0, 0)
    send_near_grads(0, 0)
    hand_on(3)
    await_far(V, 1)
    await_near(V, 1)
    join_grads(1, 1)
    differentiate(1)
    near_grads(0, 1)
    send_near_grads(0, 1)
    hand_on(4)
    when(b >= 2, share_thin)
    hand_top(lambda copy: copy.start())
    far_grads(0, 0)
    far_grads(0, 1)
    for m in (1, 0): own_grads(m, 0)
    join_grads(0, 0)
    finish(1, 0)
    for m in (1, 0): own_grads(m, 1)
    hand_on(5)
    finish(1, 1)
    join_grads(0, 1)
    hand_bottom(lambda copy: copy.start())
    query_grads(0)
    finish(0, 0)
    query_grads(1)
    for copy in own_copies: copy.wait()
    for copy in core_copies: copy.wait_recv()
    await_core(0)
    product((0, 1), 0, True)
    finish(0, 1)
    await_core(1)
    product((0, 1), 1, False)
    for m in (1, 0): pass_on(m, 0)
    await_onward(0)
    await_thin()
    product(crossing, 0, False, colour, 1)
    for m in (1, 0): pass_on(m, 1)
    await_weights()
    product(crossing, 0, False, 1 - colour, 1)
    await_onward(1)

    when(b + 1 < n, lambda: near_sum().wait_send())
    for g in range(heads):
        when(b + 2 < n, lambda: key_copy(g).wait_send())
    halo = value.at[:, 0:own]
    when(b + 2 < n, lambda: along(halo, halo, h_send.at[FAR], h_recv.at[0, 0, 0, FAR], 2).wait_send())
    when(even | (b >= 2), lambda: along(halo, halo, h_send.at[NEAR], h_recv.at[0, 0, 0, FAR], 2).wait_send())
    for over, condition in ((OVER_Y, odd | (b >= 2)), (OVER_Z, b >= 2)):
        ref = grad_out.at[:, :, over]
        when(condition, lambda: along(ref, ref, g_send.at[over], g_recv.at[0, 0, 0, 0], 2).wait_send())
    for t in range(1, nh):
        across(scaled, scaled, s_send.at[t - 1], s_recv.at[0, 0, 0], 1).wait_send()
    cross_thin().wait_send()
    thin_up().wait_send()
    thin_side(mine, 1).wait_send()
    thin_side(1 - mine, 2, 1 - colour).wait_send()
    for j in range(len(chunks)):
        cross_copy(j).wait_send()
        hand(j, lambda copy: copy.wait_send())
    hand_top(lambda copy: copy.wait_send())
    hand_bottom(lambda copy: copy.wait_send())
    for copy in core_copies:
        copy.wait_send()


def last_product(nh, heads, dq_ref, gathered, weights, acc, dq_out, grad_rows, out_ref, sem):
    rows = acc.shape[0]
    chunk = rows // LAST_CHUNKS
    g = heads - 1
    cols = slice(g * D, (g + 1) * D)
    query_copy = pltpu.make_async_copy(dq_ref, dq_out, sem.at[LAST_CHUNKS])
    query_copy.start()
    copies = []
    for c in range(LAST_CHUNKS):
        at = slice(c * chunk, (c + 1) * chunk)
        total = acc[at, :]
        for t in range(2, nh):
            left = jnp.concatenate([weights[t, 0, at, cols], weights[t, 1, at, cols]], 1)
            right = jnp.concatenate([gathered[t - 1, 0, g], gathered[t - 1, 1, g]], 1)
            total = total + contract_last(left, right)
        out_ref[at, :] = total.astype(BF16)
        copies.append(pltpu.make_async_copy(out_ref.at[at, :], grad_rows.at[at, :], sem.at[c]))
        copies[-1].start()
    query_copy.wait()
    for copy in copies:
        copy.wait()


def solution(mesh):
    n, nh = mesh.shape["seq"], mesh.shape["head"]
    assert n % 8 == 0 and nh >= 4

    def local(q, k, v, do, ke, ve, wk, wv):
        tokens, width = k.shape
        heads = width // HEAD_SIZE
        group = q.shape[1] // width
        tiles = tokens // TILE
        assert ATTEND_WINDOW == 2 * tokens
        rows = wk.shape[0] // nh
        n_chunks = 4 * (nh - 2)
        hbm = pl.BlockSpec(memory_space=pltpu.HBM)
        dma = pltpu.SemaphoreType.DMA
        vmem = pl.BlockSpec(memory_space=pltpu.VMEM)
        parts = pl.pallas_call(
            functools.partial(kernel, n, nh),
            out_shape=(
                pltpu.VMEM(q.shape, BF16),
                pltpu.VMEM((nh - 1, 2, heads, tokens, D), BF16),
                pltpu.VMEM((nh, 2, rows, width), BF16),
                pltpu.VMEM((rows, tokens), F32),
            ),
            in_specs=[hbm] * 8,
            out_specs=(vmem,) * 4,
            scratch_shapes=[
                pltpu.VMEM((tokens, width), BF16),
                pltpu.VMEM((tokens, width), BF16),
                pltpu.VMEM((heads, tiles), jnp.int32),
                pltpu.VMEM((heads, tiles), jnp.int32),
                pltpu.VMEM((heads, group * tokens, D), BF16),
                pltpu.VMEM((heads, group * tokens, D), BF16),
                pltpu.VMEM((heads, tokens, D), BF16),
                pltpu.VMEM((heads, tokens, D), BF16),
                pltpu.VMEM((heads, tokens, D), F32),
                pltpu.VMEM((8, width), F32),
                pltpu.VMEM((8, width), F32),
                pltpu.VMEM((heads, 3 * tokens, D), BF16),
                pltpu.VMEM((heads, 3 * tokens, D), BF16),
                pltpu.VMEM((D, 3 * tokens), BF16),
                pltpu.VMEM((heads, 3 * tokens, group * tokens), BF16),
                pltpu.VMEM((heads, 3 * tokens, group * tokens), BF16),
                pltpu.VMEM((heads, 3, 2, group * tokens), F32),
                pltpu.VMEM((heads, 3, group * tokens, D), BF16),
                pltpu.VMEM((2, heads, tokens, D), F32),
                pltpu.VMEM((2, heads, tokens, D), F32),
                pltpu.VMEM((2, heads, 2, tokens, D), BF16),
                pltpu.VMEM((2, heads, 2, tokens, D), BF16),
                pltpu.VMEM((2, heads, tokens, D), BF16),
                dma((4,)), dma((heads, 2)), dma((2,)),
                dma((heads,)), dma((heads,)), dma((1,)), dma((1,)),
                dma((2,)), dma((2, heads, PIECES, 2)),
                dma((n_chunks - 1,)), dma((n_chunks - 1,)), dma((n_chunks - 2, 2)), dma((n_chunks - 2,)), dma((3,)), dma((3,)),
                dma((2,)), dma((2,)),
                dma((2,)), dma((2, heads, 2, PIECES)),
                dma((nh - 1,)), dma((nh - 1, 2, heads)),
            ],
            compiler_params=pltpu.CompilerParams(
                collective_id=0, has_side_effects=True, vmem_limit_bytes=48 * 2**20
            ),
        )(*[pltpu.with_memory_space_constraint(x, pltpu.HBM) for x in (q, k, v, do, ke.T, ve.T, wk, wv)])
        return pl.pallas_call(
            functools.partial(last_product, nh, heads),
            out_shape=(
                jax.ShapeDtypeStruct(q.shape, BF16),
                jax.ShapeDtypeStruct((rows, tokens), BF16),
            ),
            in_specs=[vmem] * 4,
            out_specs=(pl.BlockSpec(memory_space=pl.ANY),) * 2,
            scratch_shapes=[pltpu.VMEM((rows, tokens), BF16), dma((LAST_CHUNKS + 1,))],
            compiler_params=pltpu.CompilerParams(vmem_limit_bytes=24 * 2**20),
        )(*[pltpu.with_memory_space_constraint(x, pltpu.VMEM) for x in parts])

    in_specs = (P("seq", "head"),) * 6 + (P(None, "head"),) * 2
    out_specs = (P("seq", "head"), P("head", "seq"))
    return jax.shard_map(local, mesh=mesh, in_specs=in_specs, out_specs=out_specs, check_vma=False)
```

```python
import functools

import jax
import jax.numpy as jnp
from jax import lax
from jax.experimental import pallas as pl
from jax.experimental.pallas import tpu as pltpu
from jax.sharding import PartitionSpec as P

HEAD_SIZE = 128
QUERY_SCALE = 168
ATTEND_WINDOW = 1024
SCALE_BLOCK = 128
LOG2_E = 1.4426950408889634
LOWEST = -1e30
MESH = pl.DeviceIdType.MESH
F32 = jnp.float32
BF16 = jnp.bfloat16
D = HEAD_SIZE
TILE = SCALE_BLOCK
SPAN = ATTEND_WINDOW + TILE
PIECES = 2
CHUNKS = 2
LAST_CHUNKS = 4
V, S = 0, 1
FAR, NEAR = 0, 1
OVER_Y, OVER_Z = 0, 1


def power_of_two(exponent):
    return jnp.where(exponent > 0, 2.0, jnp.where(exponent < 0, 0.5, 1.0)).astype(F32)


def contract_last(a, b):
    return lax.dot_general(a, b, (((1,), (1,)), ((), ())), preferred_element_type=F32)


def partner(h, t):
    other, bit = h, 1
    while bit <= t:
        if t & bit:
            other = other + bit - 2 * bit * lax.rem(lax.div(h, bit), 2)
        bit *= 2
    return other


def kernel(
    n, nh, q_ref, k_ref, v_ref, do_ref, ke_ref, ve_ref, wk_ref, wv_ref, dq_ref, gathered, weights, acc,
    k_in, v_in, ke_in, ve_in, q_all, do_all, key_true, raw_far, own_sum, total_own, total_near, smooth, value, smooth_t,
    shares_all, score_all, stats, do_part, early_grad, far_grad, own_grad, grad_out, grad_in, scaled,
    in_sem, qd_sem, w_own, kf_send, kf_recv, t_send, t_recv, h_send, h_recv,
    w_send, w_recv, f_send, f_recv, thin_send, thin_recv, c_send, c_recv, g_send, g_recv, s_send, s_recv, s_last,
):
    tokens = k_ref.shape[0]
    heads = k_ref.shape[1] // D
    group = q_ref.shape[1] // (heads * D)
    width = group * TILE
    tiles = tokens // TILE
    rows = acc.shape[0]
    own = 2 * tokens
    scale = QUERY_SCALE ** (-0.5)
    b = lax.axis_index("seq")
    h = lax.axis_index("head")
    odd = lax.rem(b, 2) == 1
    even = lax.rem(b, 2) == 0
    colour = lax.rem(lax.rem(b, 2) + lax.div(b, 2), 2)
    crossing = list(range(2, nh))

    def cols(g):
        return slice(g * D, (g + 1) * D)

    loads = [
        pltpu.make_async_copy(k_ref, k_in, in_sem.at[0]),
        pltpu.make_async_copy(v_ref, v_in, in_sem.at[1]),
        pltpu.make_async_copy(ke_ref, ke_in, in_sem.at[2]),
        pltpu.make_async_copy(ve_ref, ve_in, in_sem.at[3]),
    ]
    barrier = pltpu.get_barrier_semaphore()

    def greet(step):
        pl.semaphore_signal(
            barrier, inc=1, device_id={"seq": lax.rem(b + n + step, n)}, device_id_type=MESH
        )

    for step in (1, 2):
        pl.when(b + step < n)(lambda: greet(step))
        pl.when(b >= step)(lambda: greet(-step))
    for t in range(1, nh):
        pl.semaphore_signal(barrier, inc=1, device_id={"head": partner(h, t)}, device_id_type=MESH)
    greeted = nh - 1 + jnp.minimum(b, 2) + jnp.minimum(n - 1 - b, 2)

    for copy in loads:
        copy.start()
    head_loads = []
    for g in range(heads):
        for m, (ref, dst) in enumerate(((q_ref, q_all), (do_ref, do_all))):
            for i in range(tiles):
                for u in range(group):
                    head_loads.append(
                        pltpu.make_async_copy(
                            ref.at[i * TILE : (i + 1) * TILE, cols(g * group + u)],
                            dst.at[g, (i * group + u) * TILE : (i * group + u + 1) * TILE, :],
                            qd_sem.at[g, m],
                        )
                    )


    def when(condition, action):
        pl.when(condition)(action)

    def along(src, dst, send, recv, step):
        return pltpu.make_async_remote_copy(
            src_ref=src, dst_ref=dst, send_sem=send, recv_sem=recv,
            device_id={"seq": lax.rem(b + n + step, n)}, device_id_type=MESH,
        )

    def across(src, dst, send, recv, t):
        return pltpu.make_async_remote_copy(
            src_ref=src, dst_ref=dst, send_sem=send, recv_sem=recv,
            device_id={"head": partner(h, t)}, device_id_type=MESH,
        )

    def when(condition, *steps):
        @pl.when(condition)
        def _():
            for step in steps:
                step()

    half = rows // 2
    part = half // 2
    chunks = [(t, m, q) for t in crossing for m in range(2) for q in range(2)]
    thin_t, thin_m = chunks[-1][:2]
    chunks = chunks[:-2]
    w_refs = (wk_ref, wv_ref)
    z = lax.div(b, 2)
    upper = lax.rem(z, 2)
    mine = lax.rem(lax.div(lax.rem(z, 4) + 1, 2), 2)
    row_0 = b < 2
    row_1 = (b >= 2) & (b < 4)
    top = b + 2 >= n
    below_top = (b + 2 < n) & (b + 4 >= n)

    def held(t, m, q, side):
        return weights.at[t, m, pl.ds(side * half + q * part, part), :]

    def cross(t, m, q, j):
        return across(
            w_refs[m].at[pl.ds(partner(h, t) * rows + colour * half + q * part, part), :],
            held(t, m, q, colour), w_send.at[j], w_recv.at[j], t,
        )

    def cross_copy(j):
        return cross(*chunks[j], j)

    def cross_thin():
        return cross(thin_t, thin_m, mine, len(chunks))

    def hand_copy(ref, step, sent, received):
        if step:
            return along(ref, ref, sent, received, step)
        return pltpu.make_async_remote_copy(
            src_ref=ref, dst_ref=ref, send_sem=sent, recv_sem=received,
            device_id={"seq": partner(b, 1)}, device_id_type=MESH,
        )

    def chunk_copy(j, step, which):
        return hand_copy(held(*chunks[j], colour), step, f_send.at[j, which], f_recv.at[j])

    def hand(j, action):
        if j < 2:
            when(b >= 2, lambda: action(chunk_copy(j, -2, 0)))
            if j > 0:
                when(below_top, lambda: action(chunk_copy(j, 2, 1)))
        else:
            when(b + 2 < n, lambda: action(chunk_copy(j, 2, 1)))
            if j != 3:
                when(row_0, lambda: action(chunk_copy(j, 0, 0)))

    def hand_on(j):
        cross_copy(j).wait_recv()
        hand(j, lambda copy: copy.start())

    def hand_top(action):
        when(top, lambda: action(chunk_copy(0, 0, 1)))

    def hand_bottom(action):
        when(row_1, lambda: action(chunk_copy(3, -2, 0)))

    def thin_copy(which, step, sent, received, side=colour):
        return hand_copy(held(thin_t, thin_m, which, side), step, sent, received)

    def thin_up():
        return thin_copy(mine, 2, thin_send.at[0], thin_recv.at[0])

    def thin_down():
        return thin_copy(mine, -2, thin_send.at[0], thin_recv.at[0])

    def thin_side(which, at, side=colour):
        return thin_copy(which, 0, thin_send.at[at], thin_recv.at[at], side)

    def hand_thin():
        cross_thin().wait_recv()
        thin_side(mine, 1).start()
        when(upper == 1, lambda: thin_down().start())

    def raise_thin():
        when(upper == 0, lambda: thin_up().start())

    def share_thin():
        thin_copy(1 - mine, 2, thin_send.at[0], thin_recv.at[0], 1 - colour).wait_recv()
        thin_side(1 - mine, 2, 1 - colour).start()

    def await_weights():
        for j in range(len(chunks)):
            hand_copy(held(*chunks[j], 1 - colour), 0, f_send.at[j, 0], f_recv.at[j]).wait_recv()
        thin_side(mine, 1, 1 - colour).wait_recv()

    def await_thin():
        thin_side(1 - mine, 2).wait_recv()

    core_copies = [
        across(ref.at[pl.ds(partner(h, 1) * rows, rows), :], weights.at[1, m], c_send.at[m], c_recv.at[m], 1)
        for m, ref in enumerate(w_refs)
    ]
    own_copies = [
        pltpu.make_async_copy(ref.at[pl.ds(h * rows, rows), :], weights.at[0, m], w_own.at[m])
        for m, ref in enumerate(w_refs)
    ]

    def key_copy(g):
        return along(key_true.at[g], raw_far.at[g], kf_send.at[g], kf_recv.at[g], 2)

    piece = tokens // PIECES
    halo_refs = (value, smooth)

    def slot(kind, g, base, p):
        return halo_refs[kind].at[g, base + p * piece : base + (p + 1) * piece]

    def far_copy(kind, g, p):
        at = (kind, g, p, FAR)
        return along(slot(kind, g, own, p), slot(kind, g, 0, p), h_send.at[FAR], h_recv.at[at], 2)

    def near_copy(kind, g, p):
        at = (kind, g, p, NEAR)
        return along(slot(kind, g, own, p), slot(kind, g, tokens, p), h_send.at[NEAR], h_recv.at[at], 1)

    def relay_copy(kind, g, p):
        at = (kind, g, p, NEAR)
        return along(slot(kind, g, 0, p), slot(kind, g, tokens, p), h_send.at[NEAR], h_recv.at[at], -1)

    def send_far(kind, g):
        for p in range(PIECES):
            when(b + 2 < n, lambda: far_copy(kind, g, p).start())

    def send_near(kind, g):
        for p in range(PIECES):
            when(even, lambda: near_copy(kind, g, p).start())

    def relay(kind, g):
        for p in range(PIECES):
            @pl.when(odd & (b >= 2))
            def _():
                far_copy(kind, g, p).wait_recv()
                relay_copy(kind, g, p).start()

    def await_far(kind, g):
        for p in range(PIECES):
            when(even & (b >= 2), lambda: far_copy(kind, g, p).wait_recv())

    def await_near(kind, g):
        for p in range(PIECES):
            when(b >= 1, lambda: near_copy(kind, g, p).wait_recv())

    def near_sum():
        return along(total_own, total_near, t_send.at[0], t_recv.at[0], 1)

    def await_heads(g):
        for m, ref in enumerate((q_all, do_all)):
            pltpu.make_async_copy(ref.at[g], ref.at[g], qd_sem.at[g, m]).wait()

    def rows_of(p, base=0):
        return slice(base + p * piece, base + (p + 1) * piece)

    def grad_copy(m, g, over, p, step):
        at = (m, g, over, rows_of(p))
        return along(grad_out.at[at], grad_in.at[at], g_send.at[over], g_recv.at[m, g, over, p], step)

    def true_keys(g):
        for j in range(tiles):
            at = slice(j * TILE, (j + 1) * TILE)
            key_true[g, at] = (k_in[at, cols(g)].astype(F32) * power_of_two(ke_in[g : g + 1, j : j + 1])).astype(BF16)

    def true_values(g):
        for j in range(tiles):
            at = slice(j * TILE, (j + 1) * TILE)
            value[g, own + j * TILE : own + (j + 1) * TILE] = (
                v_in[at, cols(g)].astype(F32) * power_of_two(ve_in[g : g + 1, j : j + 1])
            ).astype(BF16)

    def sum_keys():
        for g in range(heads):
            total_own[:, cols(g)] = jnp.broadcast_to(
                jnp.sum(key_true[g].astype(F32), axis=0, keepdims=True), (8, D)
            )

    def clear():
        @pl.when(b < 1)
        def _():
            total_near[...] = jnp.zeros_like(total_near)
            for g in range(heads):
                value[g, tokens:own, :] = jnp.zeros((tokens, D), BF16)
                smooth[g, tokens:own, :] = jnp.zeros((tokens, D), BF16)

        @pl.when(b < 2)
        def _():
            raw_far[...] = jnp.zeros_like(raw_far)
            for g in range(heads):
                value[g, 0:tokens, :] = jnp.zeros((tokens, D), BF16)
                smooth[g, 0:tokens, :] = jnp.zeros((tokens, D), BF16)
                for m in range(2):
                    grad_in[m, g, OVER_Y] = jnp.zeros((tokens, D), BF16)

        @pl.when(top)
        def _():
            for g in range(heads):
                for m in range(2):
                    grad_in[m, g, OVER_Z] = jnp.zeros((tokens, D), BF16)

        blank = jnp.zeros((TILE, width), BF16)
        for ref in (shares_all, score_all):
            for g in range(heads):
                for i in range(0, tiles, 2):
                    ref[g, i * TILE : (i + 1) * TILE, (i + 1) * width : (i + 2) * width] = blank
                    ref[g, own + (i + 1) * TILE : own + (i + 2) * TILE, i * width : (i + 1) * width] = blank

    row_at = lax.broadcasted_iota(jnp.int32, (tokens, tokens), 0)
    col_at = lax.broadcasted_iota(jnp.int32, (tokens, tokens), 1)
    lower = jnp.where(row_at >= col_at, 1.0, 0.0).astype(BF16)
    place = b * tokens + lax.broadcasted_iota(jnp.int32, (tokens, 1), 0)
    counts = jnp.clip(place + 1, 1, ATTEND_WINDOW).astype(F32)

    def running_keys(g):
        own_sum[g] = jnp.dot(lower, key_true[g], preferred_element_type=F32)

    def smooth_keys(g):
        when(b >= 2, lambda: key_copy(g).wait_recv())
        far = jnp.dot(lower, raw_far[g], preferred_element_type=F32)
        mean = (own_sum[g] - far + far[tokens - 1 :, :] + total_near[0:1, cols(g)]) / counts
        smooth[g, own : own + tokens, :] = (key_true[g].astype(F32) - mean).astype(BF16)
        send_far(S, g)
        send_near(S, g)

    row = lax.broadcasted_iota(jnp.int32, (TILE, width), 0)
    lane = lax.rem(lax.broadcasted_iota(jnp.int32, (1, width), 1), TILE)
    unit = jnp.where(
        lax.broadcasted_iota(jnp.int32, (TILE, TILE), 0) == lax.broadcasted_iota(jnp.int32, (TILE, TILE), 1), 1.0, 0.0
    )

    def lanes_of(i):
        return slice(i * width, (i + 1) * width)

    def keys_of(part, i):
        return (slice(i * TILE, tokens), slice(tokens, own), slice(own, own + (i + 1) * TILE))[part]

    def attend(g, part):
        for i in range(tiles):
            at, lanes = keys_of(part, i), lanes_of(i)
            scores = contract_last(smooth[g, at, :], q_all[g, lanes, :])
            if part == 0:
                edge = jnp.where(row > lane, scores[:TILE], -jnp.inf)
                scores = edge if i == tiles - 1 else jnp.concatenate([edge, scores[TILE:]], 0)
            if part == 2:
                edge = jnp.where(row <= lane, scores[i * TILE :], -jnp.inf)
                scores = edge if i == 0 else jnp.concatenate([scores[: i * TILE], edge], 0)
            highest = jnp.maximum(jnp.max(scores, axis=0, keepdims=True), LOWEST)
            powers = jnp.exp2((scores - highest) * (scale * LOG2_E))
            shares_all[g, at, lanes] = powers.astype(BF16)
            stats[g, part, 0:1, lanes] = highest
            stats[g, part, 1:2, lanes] = jnp.sum(powers, axis=0, keepdims=True)

    def combine(g):
        present = (b >= 2, b >= 1, b >= 0)
        tops = [jnp.where(here, stats[g, part, 0:1, :], LOWEST) for part, here in enumerate(present)]
        highest = jnp.maximum(jnp.maximum(tops[0], tops[1]), tops[2])
        powers = [
            jnp.where(here, jnp.exp2((top - highest) * (scale * LOG2_E)), 0.0) for top, here in zip(tops, present)
        ]
        total = sum(power * stats[g, part, 1:2, :] for part, power in enumerate(powers))
        inverse = 1.0 / total
        for part in range(3):
            factor = powers[part] * inverse
            stats[g, part, 0:1, :] = factor.astype(BF16).astype(F32)
            for k in range(group * tiles):
                at = slice(k * TILE, (k + 1) * TILE)
                spread = (unit * factor[:, at]).astype(BF16)
                do_part[g, part, at, :] = jnp.dot(
                    spread, do_all[g, at, :], preferred_element_type=F32
                ).astype(BF16)

    def local_of(part, i):
        return slice(i * TILE, tokens) if part == 0 else slice(0, (i + 1) * TILE)

    def differentiate_early(g):
        for i in range(tiles):
            lanes, row_dot = lanes_of(i), 0.0
            for part in (0, 2):
                at = keys_of(part, i)
                share_grad = contract_last(value[g, at, :], do_part[g, part, lanes, :])
                early_grad[g, part // 2, local_of(part, i), lanes] = share_grad
                row_dot = row_dot + jnp.sum(shares_all[g, at, lanes].astype(F32) * share_grad, axis=0, keepdims=True)
            stats[g, 0, 1:2, lanes] = row_dot

    def differentiate(g):
        for i in range(tiles):
            lanes = lanes_of(i)
            at = keys_of(1, i)
            near_grad = contract_last(value[g, at, :], do_part[g, 1, lanes, :])
            near_shares = shares_all[g, at, lanes].astype(F32)
            row_dot = stats[g, 0, 1:2, lanes] + jnp.sum(near_shares * near_grad, axis=0, keepdims=True)
            score_all[g, at, lanes] = (near_shares * (near_grad - row_dot * stats[g, 1, 0:1, lanes])).astype(BF16)
            for part in (0, 2):
                at = keys_of(part, i)
                share_grad = early_grad[g, part // 2, local_of(part, i), lanes]
                shift = row_dot * stats[g, part, 0:1, lanes]
                score_all[g, at, lanes] = (shares_all[g, at, lanes].astype(F32) * (share_grad - shift)).astype(BF16)

    def key_grads(m, g, part, at, lanes):
        if m == 0:
            return jnp.dot(score_all[g, at, lanes], q_all[g, lanes, :], preferred_element_type=F32) * scale
        return jnp.dot(shares_all[g, at, lanes], do_part[g, part, lanes, :], preferred_element_type=F32)

    def near_grads(m, g):
        for p in range(PIECES):
            grads = key_grads(m, g, 1, rows_of(p, tokens), slice(0, group * tokens))
            grad_out[m, g, OVER_Y, rows_of(p)] = grads.astype(BF16)

    def send_near_grads(m, g):
        for p in range(PIECES):
            when(even & (b >= 2), lambda: grad_copy(m, g, OVER_Y, p, 1).start())
            when(odd, lambda: grad_copy(m, g, OVER_Y, p, -1).start())

    def far_grads(m, g):
        for p in range(PIECES):
            grads = key_grads(m, g, 0, rows_of(p), slice(0, (p + 1) * group * piece))
            far_grad[m, g, rows_of(p)] = grads

            @pl.when(even & (b >= 2))
            def _():
                grad_out[m, g, OVER_Z, rows_of(p)] = far_grad[m, g, rows_of(p)].astype(BF16)
                grad_copy(m, g, OVER_Z, p, -2).start()

    def join_grads(m, g):
        for p in range(PIECES):
            @pl.when(odd & (b >= 2))
            def _():
                grad_copy(m, g, OVER_Y, p, 1).wait_recv()
                both = far_grad[m, g, rows_of(p)] + grad_in[m, g, OVER_Y, rows_of(p)].astype(F32)
                grad_out[m, g, OVER_Z, rows_of(p)] = both.astype(BF16)
                grad_copy(m, g, OVER_Z, p, -2).start()

    def own_grads(m, g):
        for p in range(PIECES):
            own_grad[m, g, rows_of(p)] = key_grads(
                m, g, 2, rows_of(p, own), slice(p * group * piece, group * tokens)
            )

    def query_grads(g):
        smooth_t[...] = smooth[g].astype(F32).T.astype(BF16)
        for i in range(tiles):
            window = slice(i * TILE, i * TILE + SPAN)
            dq = jnp.dot(
                smooth_t[:, window], score_all[g, window, i * width : (i + 1) * width],
                preferred_element_type=F32,
            ) * scale
            dq = dq.T.astype(BF16)
            for u in range(group):
                dq_ref[i * TILE : (i + 1) * TILE, cols(g * group + u)] = dq[u * TILE : (u + 1) * TILE]

    def share_copy(m, g, p, t):
        at = (m, g) if p is None else (m, g, rows_of(p))
        last = (m, g) == (0, heads - 1) and t > 1
        received = s_last.at[t - 1, p] if last else s_recv.at[t - 1, m, g]
        return across(scaled.at[at], gathered.at[(t - 1,) + at], s_send.at[t - 1], received, t)

    def onward_copy(m, g, t, p=None):
        at = (m, g) if p is None else (m, g, rows_of(p))
        received = s_recv.at[t, m, g] if p is None else s_last.at[t, p]
        return across(gathered.at[(t - 1,) + at], gathered.at[(t,) + at], s_send.at[t], received, 1)

    def hops_of(m, g):
        return range(PIECES) if (m, g) == (0, heads - 1) else (None,)

    far_steps = list(range(2, nh, 2))

    def finish(m, g):
        exponent = (ke_in, ve_in)[m]
        for p in range(PIECES):
            when(even, lambda: grad_copy(m, g, OVER_Y, p, -1).wait_recv())
            when(b + 2 < n, lambda: grad_copy(m, g, OVER_Z, p, -2).wait_recv())
            for r in range(p * tiles // PIECES, (p + 1) * tiles // PIECES):
                at = slice(r * TILE, (r + 1) * TILE)
                whole = own_grad[m, g, at] + grad_in[m, g, OVER_Z, at].astype(F32)
                whole = whole + jnp.where(even, grad_in[m, g, OVER_Y, at].astype(F32), 0.0)
                scaled[m, g, at] = (whole * power_of_two(exponent[g : g + 1, r : r + 1])).astype(BF16)
            for t in far_steps + [1]:
                share_copy(m, g, p, t).start()

    def pass_on(m, g):
        for t in far_steps:
            for p in hops_of(m, g):
                share_copy(m, g, p, t).wait_recv()
                onward_copy(m, g, t, p).start()

    def await_core(g):
        for m in range(2):
            share_copy(m, g, None, 1).wait_recv()

    def await_onward(m, g):
        for t in far_steps:
            for p in hops_of(m, g):
                onward_copy(m, g, t, p).wait_recv()

    chunk = rows // CHUNKS

    def product(terms, fresh, base=0, count=CHUNKS):
        def one_chunk(k, carry):
            at = pl.ds(pl.multiple_of((base + k) * chunk, 16), chunk)
            left = jnp.concatenate([weights[t, m, at, cols(g)] for t, m, g in terms], 1)
            right = [scaled[m, g] if t == 0 else gathered[t - 1, m, g] for t, m, g in terms]
            total = contract_last(left, jnp.concatenate(right, 1))
            if not fresh:
                total = total + acc[at, :]
            acc[at, :] = total
            return carry

        lax.fori_loop(0, count, one_chunk, 0)

    def terms_of(ts, g):
        return [(t, m, g) for t in ts for m in range(2)]

    crossed = terms_of(crossing, 0) + [(t, 1, 1) for t in crossing]

    for copy in loads: copy.wait()
    for g in range(heads): true_keys(g)
    sum_keys()
    for g in range(heads): true_values(g)
    pl.semaphore_wait(barrier, greeted)
    when(b + 1 < n, lambda: near_sum().start())
    cross_thin().start()
    for j in range(len(chunks)): cross_copy(j).start()
    for g in range(heads): when(b + 2 < n, lambda: key_copy(g).start())
    for g in range(heads): send_near(V, g)
    for copy in head_loads: copy.start()
    for copy in core_copies + own_copies: copy.start()
    clear()
    for g in range(heads): running_keys(g)
    when(b >= 1, lambda: near_sum().wait_recv())
    smooth_keys(0)
    hand_thin()
    smooth_keys(1)
    for g in range(heads): send_far(V, g)
    raise_thin()
    for g in range(heads): await_heads(g)
    attend(0, 2)
    attend(1, 2)
    relay(S, 0)
    hand_on(0)
    await_far(S, 0)
    attend(0, 0)
    when(row_0, share_thin)
    relay(S, 1)
    await_far(S, 1)
    attend(1, 0)
    hand_on(1)
    await_near(S, 0)
    attend(0, 1)
    combine(0)
    relay(V, 0)
    near_grads(1, 0)
    when(even, lambda: send_near_grads(1, 0))
    far_grads(1, 0)
    relay(V, 1)
    when(odd, lambda: send_near_grads(1, 0))
    await_near(S, 1)
    attend(1, 1)
    hand_on(2)
    combine(1)
    near_grads(1, 1)
    send_near_grads(1, 1)
    far_grads(1, 1)
    await_far(V, 0)
    differentiate_early(0)
    await_near(V, 0)
    join_grads(1, 0)
    differentiate(0)
    near_grads(0, 0)
    send_near_grads(0, 0)
    hand_on(3)
    await_far(V, 1)
    differentiate_early(1)
    await_near(V, 1)
    join_grads(1, 1)
    differentiate(1)
    near_grads(0, 1)
    send_near_grads(0, 1)
    hand_on(4)
    when(b >= 2, share_thin)
    hand_top(lambda copy: copy.start())
    far_grads(0, 0)
    far_grads(0, 1)
    for m in (1, 0): own_grads(m, 0)
    join_grads(0, 0)
    finish(1, 0)
    for m in (1, 0): own_grads(m, 1)
    hand_on(5)
    finish(1, 1)
    join_grads(0, 1)
    hand_bottom(lambda copy: copy.start())
    query_grads(0)
    finish(0, 0)
    query_grads(1)
    for copy in own_copies: copy.wait()
    for copy in core_copies: copy.wait_recv()
    finish(0, 1)
    await_core(0)
    product(terms_of((0, 1), 0), True)
    await_core(1)
    product(terms_of((0, 1), 1), False)
    for m, g in ((1, 0), (0, 0), (1, 1)): pass_on(m, g)
    for m, g in ((1, 0), (0, 0), (1, 1)): await_onward(m, g)
    await_thin()
    product(crossed, False, colour, 1)
    pass_on(0, 1)
    await_weights()
    product(crossed, False, 1 - colour, 1)
    await_onward(0, 1)

    when(b + 1 < n, lambda: near_sum().wait_send())
    for g in range(heads):
        when(b + 2 < n, lambda: key_copy(g).wait_send())
    halo = value.at[:, 0:own]
    when(b + 2 < n, lambda: along(halo, halo, h_send.at[FAR], h_recv.at[0, 0, 0, FAR], 2).wait_send())
    when(even | (b >= 2), lambda: along(halo, halo, h_send.at[NEAR], h_recv.at[0, 0, 0, FAR], 2).wait_send())
    for over, condition in ((OVER_Y, odd | (b >= 2)), (OVER_Z, b >= 2)):
        ref = grad_out.at[:, :, over]
        when(condition, lambda: along(ref, ref, g_send.at[over], g_recv.at[0, 0, 0, 0], 2).wait_send())
    for t in range(1, nh):
        across(scaled, scaled, s_send.at[t - 1], s_recv.at[0, 0, 0], 1).wait_send()
    cross_thin().wait_send()
    thin_up().wait_send()
    thin_side(mine, 1).wait_send()
    thin_side(1 - mine, 2, 1 - colour).wait_send()
    for j in range(len(chunks)):
        cross_copy(j).wait_send()
        hand(j, lambda copy: copy.wait_send())
    hand_top(lambda copy: copy.wait_send())
    hand_bottom(lambda copy: copy.wait_send())
    for copy in core_copies:
        copy.wait_send()


def last_product(nh, heads, dq_ref, gathered, weights, acc, dq_out, grad_rows, out_ref, sem):
    rows = acc.shape[0]
    chunk = rows // LAST_CHUNKS
    g = heads - 1
    cols = slice(g * D, (g + 1) * D)
    query_copy = pltpu.make_async_copy(dq_ref, dq_out, sem.at[LAST_CHUNKS])
    query_copy.start()
    copies = []
    for c in range(LAST_CHUNKS):
        at = slice(c * chunk, (c + 1) * chunk)
        left = jnp.concatenate([weights[t, 0, at, cols] for t in range(2, nh)], 1)
        right = jnp.concatenate([gathered[t - 1, 0, g] for t in range(2, nh)], 1)
        total = acc[at, :] + contract_last(left, right)
        out_ref[at, :] = total.astype(BF16)
        copies.append(pltpu.make_async_copy(out_ref.at[at, :], grad_rows.at[at, :], sem.at[c]))
        copies[-1].start()
    query_copy.wait()
    for copy in copies:
        copy.wait()


def solution(mesh):
    n, nh = mesh.shape["seq"], mesh.shape["head"]
    assert n % 8 == 0 and nh >= 4

    def local(q, k, v, do, ke, ve, wk, wv):
        tokens, width = k.shape
        heads = width // HEAD_SIZE
        assert heads == 2
        group = q.shape[1] // width
        tiles = tokens // TILE
        assert ATTEND_WINDOW == 2 * tokens
        rows = wk.shape[0] // nh
        n_chunks = 4 * (nh - 2)
        hbm = pl.BlockSpec(memory_space=pltpu.HBM)
        dma = pltpu.SemaphoreType.DMA
        vmem = pl.BlockSpec(memory_space=pltpu.VMEM)
        parts = pl.pallas_call(
            functools.partial(kernel, n, nh),
            out_shape=(
                pltpu.VMEM(q.shape, BF16),
                pltpu.VMEM((nh - 1, 2, heads, tokens, D), BF16),
                pltpu.VMEM((nh, 2, rows, width), BF16),
                pltpu.VMEM((rows, tokens), F32),
            ),
            in_specs=[hbm] * 8,
            out_specs=(vmem,) * 4,
            scratch_shapes=[
                pltpu.VMEM((tokens, width), BF16),
                pltpu.VMEM((tokens, width), BF16),
                pltpu.VMEM((heads, tiles), jnp.int32),
                pltpu.VMEM((heads, tiles), jnp.int32),
                pltpu.VMEM((heads, group * tokens, D), BF16),
                pltpu.VMEM((heads, group * tokens, D), BF16),
                pltpu.VMEM((heads, tokens, D), BF16),
                pltpu.VMEM((heads, tokens, D), BF16),
                pltpu.VMEM((heads, tokens, D), F32),
                pltpu.VMEM((8, width), F32),
                pltpu.VMEM((8, width), F32),
                pltpu.VMEM((heads, 3 * tokens, D), BF16),
                pltpu.VMEM((heads, 3 * tokens, D), BF16),
                pltpu.VMEM((D, 3 * tokens), BF16),
                pltpu.VMEM((heads, 3 * tokens, group * tokens), BF16),
                pltpu.VMEM((heads, 3 * tokens, group * tokens), BF16),
                pltpu.VMEM((heads, 3, 2, group * tokens), F32),
                pltpu.VMEM((heads, 3, group * tokens, D), BF16),
                pltpu.VMEM((heads, 2, tokens, group * tokens), F32),
                pltpu.VMEM((2, heads, tokens, D), F32),
                pltpu.VMEM((2, heads, tokens, D), F32),
                pltpu.VMEM((2, heads, 2, tokens, D), BF16),
                pltpu.VMEM((2, heads, 2, tokens, D), BF16),
                pltpu.VMEM((2, heads, tokens, D), BF16),
                dma((4,)), dma((heads, 2)), dma((2,)),
                dma((heads,)), dma((heads,)), dma((1,)), dma((1,)),
                dma((2,)), dma((2, heads, PIECES, 2)),
                dma((n_chunks - 1,)), dma((n_chunks - 1,)), dma((n_chunks - 2, 2)), dma((n_chunks - 2,)), dma((3,)), dma((3,)),
                dma((2,)), dma((2,)),
                dma((2,)), dma((2, heads, 2, PIECES)),
                dma((nh - 1,)), dma((nh - 1, 2, heads)), dma((nh - 1, PIECES)),
            ],
            compiler_params=pltpu.CompilerParams(
                collective_id=0, has_side_effects=True, vmem_limit_bytes=48 * 2**20
            ),
        )(*[pltpu.with_memory_space_constraint(x, pltpu.HBM) for x in (q, k, v, do, ke.T, ve.T, wk, wv)])
        return pl.pallas_call(
            functools.partial(last_product, nh, heads),
            out_shape=(
                jax.ShapeDtypeStruct(q.shape, BF16),
                jax.ShapeDtypeStruct((rows, tokens), BF16),
            ),
            in_specs=[vmem] * 4,
            out_specs=(pl.BlockSpec(memory_space=pl.ANY),) * 2,
            scratch_shapes=[pltpu.VMEM((rows, tokens), BF16), dma((LAST_CHUNKS + 1,))],
            compiler_params=pltpu.CompilerParams(vmem_limit_bytes=24 * 2**20),
        )(*[pltpu.with_memory_space_constraint(x, pltpu.VMEM) for x in parts])

    in_specs = (P("seq", "head"),) * 6 + (P(None, "head"),) * 2
    out_specs = (P("seq", "head"), P("head", "seq"))
    return jax.shard_map(local, mesh=mesh, in_specs=in_specs, out_specs=out_specs, check_vma=False)
```

```python
import functools

import jax
import jax.numpy as jnp
from jax import lax
from jax.experimental import pallas as pl
from jax.experimental.pallas import tpu as pltpu
from jax.sharding import PartitionSpec as P

HEAD_SIZE = 128
QUERY_SCALE = 168
ATTEND_WINDOW = 1024
SCALE_BLOCK = 128
LOG2_E = 1.4426950408889634
LOWEST = -1e30
MESH = pl.DeviceIdType.MESH
F32 = jnp.float32
BF16 = jnp.bfloat16
D = HEAD_SIZE
TILE = SCALE_BLOCK
SPAN = ATTEND_WINDOW + TILE
PIECES = 2
CHUNKS = 2
LAST_CHUNKS = 4
V, S = 0, 1
FAR, NEAR = 0, 1
OVER_Y, OVER_Z = 0, 1


def power_of_two(exponent):
    return jnp.where(exponent > 0, 2.0, jnp.where(exponent < 0, 0.5, 1.0)).astype(F32)


def contract_last(a, b):
    return lax.dot_general(a, b, (((1,), (1,)), ((), ())), preferred_element_type=F32)


def partner(h, t):
    other, bit = h, 1
    while bit <= t:
        if t & bit:
            other = other + bit - 2 * bit * lax.rem(lax.div(h, bit), 2)
        bit *= 2
    return other


def kernel(
    n, nh, q_ref, k_ref, v_ref, do_ref, ke_ref, ve_ref, wk_ref, wv_ref, dq_ref, gathered, weights, acc,
    k_in, v_in, ke_in, ve_in, q_all, do_all, key_true, raw_far, own_sum, total_own, total_near, smooth, value, smooth_t,
    shares_all, score_all, stats, do_part, early_grad, far_grad, own_grad, grad_out, grad_in, scaled,
    in_sem, qd_sem, w_own, kf_send, kf_recv, t_send, t_recv, h_send, h_recv,
    w_send, w_recv, f_send, f_recv, thin_send, thin_recv, c_send, c_recv, g_send, g_recv, s_send, s_recv, s_last,
):
    tokens = k_ref.shape[0]
    heads = k_ref.shape[1] // D
    group = q_ref.shape[1] // (heads * D)
    width = group * TILE
    tiles = tokens // TILE
    rows = acc.shape[0]
    own = 2 * tokens
    scale = QUERY_SCALE ** (-0.5)
    b = lax.axis_index("seq")
    h = lax.axis_index("head")
    odd = lax.rem(b, 2) == 1
    even = lax.rem(b, 2) == 0
    colour = lax.rem(lax.rem(b, 2) + lax.div(b, 2), 2)
    crossing = list(range(2, nh))

    def cols(g):
        return slice(g * D, (g + 1) * D)

    loads = [
        pltpu.make_async_copy(k_ref, k_in, in_sem.at[0]),
        pltpu.make_async_copy(v_ref, v_in, in_sem.at[1]),
        pltpu.make_async_copy(ke_ref, ke_in, in_sem.at[2]),
        pltpu.make_async_copy(ve_ref, ve_in, in_sem.at[3]),
    ]
    barrier = pltpu.get_barrier_semaphore()

    def greet(step):
        pl.semaphore_signal(
            barrier, inc=1, device_id={"seq": lax.rem(b + n + step, n)}, device_id_type=MESH
        )

    for step in (1, 2):
        pl.when(b + step < n)(lambda: greet(step))
        pl.when(b >= step)(lambda: greet(-step))
    for t in range(1, nh):
        pl.semaphore_signal(barrier, inc=1, device_id={"head": partner(h, t)}, device_id_type=MESH)
    greeted = nh - 1 + jnp.minimum(b, 2) + jnp.minimum(n - 1 - b, 2)

    for copy in loads:
        copy.start()
    head_loads = []
    for g in range(heads):
        for m, (ref, dst) in enumerate(((q_ref, q_all), (do_ref, do_all))):
            for i in range(tiles):
                for u in range(group):
                    head_loads.append(
                        pltpu.make_async_copy(
                            ref.at[i * TILE : (i + 1) * TILE, cols(g * group + u)],
                            dst.at[g, (i * group + u) * TILE : (i * group + u + 1) * TILE, :],
                            qd_sem.at[g, m],
                        )
                    )


    def when(condition, action):
        pl.when(condition)(action)

    def along(src, dst, send, recv, step):
        return pltpu.make_async_remote_copy(
            src_ref=src, dst_ref=dst, send_sem=send, recv_sem=recv,
            device_id={"seq": lax.rem(b + n + step, n)}, device_id_type=MESH,
        )

    def across(src, dst, send, recv, t):
        return pltpu.make_async_remote_copy(
            src_ref=src, dst_ref=dst, send_sem=send, recv_sem=recv,
            device_id={"head": partner(h, t)}, device_id_type=MESH,
        )

    def when(condition, *steps):
        @pl.when(condition)
        def _():
            for step in steps:
                step()

    half = rows // 2
    part = half // 2
    chunks = [(t, m, q) for t in crossing for m in range(2) for q in range(2)]
    thin_t, thin_m = chunks[-1][:2]
    chunks = chunks[:-2]
    w_refs = (wk_ref, wv_ref)
    z = lax.div(b, 2)
    upper = lax.rem(z, 2)
    mine = lax.rem(lax.div(lax.rem(z, 4) + 1, 2), 2)
    row_0 = b < 2
    row_1 = (b >= 2) & (b < 4)
    top = b + 2 >= n
    below_top = (b + 2 < n) & (b + 4 >= n)

    def held(t, m, q, side):
        return weights.at[t, m, pl.ds(side * half + q * part, part), :]

    def cross(t, m, q, j):
        return across(
            w_refs[m].at[pl.ds(partner(h, t) * rows + colour * half + q * part, part), :],
            held(t, m, q, colour), w_send.at[j // len(chunks)], w_recv.at[j], t,
        )

    def cross_copy(j):
        return cross(*chunks[j], j)

    def cross_thin():
        return cross(thin_t, thin_m, mine, len(chunks))

    def hand_copy(ref, step, sent, received):
        if step:
            return along(ref, ref, sent, received, step)
        return pltpu.make_async_remote_copy(
            src_ref=ref, dst_ref=ref, send_sem=sent, recv_sem=received,
            device_id={"seq": partner(b, 1)}, device_id_type=MESH,
        )

    def chunk_copy(j, step, sent):
        return hand_copy(held(*chunks[j], colour), step, f_send.at[sent], f_recv.at[j])

    def hand(j, action):
        if j < 2:
            when(b >= 2, lambda: action(chunk_copy(j, -2, 0)))
            if j > 0:
                when(below_top, lambda: action(chunk_copy(j, 2, 3)))
        else:
            when(b + 2 < n, lambda: action(chunk_copy(j, 2, 1)))
            if j != 3:
                when(row_0, lambda: action(chunk_copy(j, 0, 2)))

    def hand_on(j):
        cross_copy(j).wait_recv()
        hand(j, lambda copy: copy.start())

    def hand_top(action):
        when(top, lambda: action(chunk_copy(0, 0, 4)))

    def hand_bottom(action):
        when(row_1, lambda: action(chunk_copy(3, -2, 5)))

    def thin_copy(which, step, sent, received, side=colour):
        return hand_copy(held(thin_t, thin_m, which, side), step, sent, received)

    def thin_up():
        return thin_copy(mine, 2, thin_send.at[0], thin_recv.at[0])

    def thin_down():
        return thin_copy(mine, -2, thin_send.at[0], thin_recv.at[0])

    def thin_side(which, at, side=colour):
        return thin_copy(which, 0, thin_send.at[at], thin_recv.at[at], side)

    def hand_thin():
        cross_thin().wait_recv()
        thin_side(mine, 1).start()
        when(upper == 1, lambda: thin_down().start())

    def raise_thin():
        when(upper == 0, lambda: thin_up().start())

    def share_thin():
        thin_copy(1 - mine, 2, thin_send.at[0], thin_recv.at[0], 1 - colour).wait_recv()
        thin_side(1 - mine, 2, 1 - colour).start()

    def await_weights():
        for j in range(len(chunks)):
            hand_copy(held(*chunks[j], 1 - colour), 0, f_send.at[0], f_recv.at[j]).wait_recv()
        thin_side(mine, 1, 1 - colour).wait_recv()

    def await_thin():
        thin_side(1 - mine, 2).wait_recv()

    core_copies = [
        across(ref.at[pl.ds(partner(h, 1) * rows, rows), :], weights.at[1, m], c_send.at[0], c_recv.at[0], 1)
        for m, ref in enumerate(w_refs)
    ]
    own_copies = [
        pltpu.make_async_copy(ref.at[pl.ds(h * rows, rows), :], weights.at[0, m], w_own.at[0])
        for m, ref in enumerate(w_refs)
    ]

    def key_copy(g):
        return along(key_true.at[g], raw_far.at[g], kf_send.at[0], kf_recv.at[g], 2)

    piece = tokens // PIECES
    halo_refs = (value, smooth)

    def slot(kind, g, base, p):
        return halo_refs[kind].at[g, base + p * piece : base + (p + 1) * piece]

    def far_copy(kind, g, p):
        at = (kind, g, p, FAR)
        return along(slot(kind, g, own, p), slot(kind, g, 0, p), h_send.at[FAR], h_recv.at[at], 2)

    def near_copy(kind, g, p):
        at = (kind, g, p, NEAR)
        return along(slot(kind, g, own, p), slot(kind, g, tokens, p), h_send.at[NEAR], h_recv.at[at], 1)

    def relay_copy(kind, g, p):
        at = (kind, g, p, NEAR)
        return along(slot(kind, g, 0, p), slot(kind, g, tokens, p), h_send.at[NEAR], h_recv.at[at], -1)

    def send_far(kind, g):
        for p in range(PIECES):
            when(b + 2 < n, lambda: far_copy(kind, g, p).start())

    def send_near(kind, g):
        for p in range(PIECES):
            when(even, lambda: near_copy(kind, g, p).start())

    def relay(kind, g):
        for p in range(PIECES):
            @pl.when(odd & (b >= 2))
            def _():
                far_copy(kind, g, p).wait_recv()
                relay_copy(kind, g, p).start()

    def await_far(kind, g):
        for p in range(PIECES):
            when(even & (b >= 2), lambda: far_copy(kind, g, p).wait_recv())

    def await_near(kind, g):
        for p in range(PIECES):
            when(b >= 1, lambda: near_copy(kind, g, p).wait_recv())

    def near_sum():
        return along(total_own, total_near, t_send.at[0], t_recv.at[0], 1)

    def await_heads(g):
        for m, ref in enumerate((q_all, do_all)):
            pltpu.make_async_copy(ref.at[g], ref.at[g], qd_sem.at[g, m]).wait()

    def rows_of(p, base=0):
        return slice(base + p * piece, base + (p + 1) * piece)

    def grad_copy(m, g, over, p, step):
        at = (m, g, over, rows_of(p))
        return along(grad_out.at[at], grad_in.at[at], g_send.at[over], g_recv.at[m, g, over, p], step)

    def true_keys(g):
        for j in range(tiles):
            at = slice(j * TILE, (j + 1) * TILE)
            key_true[g, at] = (k_in[at, cols(g)].astype(F32) * power_of_two(ke_in[g : g + 1, j : j + 1])).astype(BF16)

    def true_values(g):
        for j in range(tiles):
            at = slice(j * TILE, (j + 1) * TILE)
            value[g, own + j * TILE : own + (j + 1) * TILE] = (
                v_in[at, cols(g)].astype(F32) * power_of_two(ve_in[g : g + 1, j : j + 1])
            ).astype(BF16)

    def sum_keys():
        for g in range(heads):
            total_own[:, cols(g)] = jnp.broadcast_to(
                jnp.sum(key_true[g].astype(F32), axis=0, keepdims=True), (8, D)
            )

    def clear():
        @pl.when(b < 1)
        def _():
            total_near[...] = jnp.zeros_like(total_near)
            for g in range(heads):
                value[g, tokens:own, :] = jnp.zeros((tokens, D), BF16)
                smooth[g, tokens:own, :] = jnp.zeros((tokens, D), BF16)

        @pl.when(b < 2)
        def _():
            raw_far[...] = jnp.zeros_like(raw_far)
            for g in range(heads):
                value[g, 0:tokens, :] = jnp.zeros((tokens, D), BF16)
                smooth[g, 0:tokens, :] = jnp.zeros((tokens, D), BF16)
                for m in range(2):
                    grad_in[m, g, OVER_Y] = jnp.zeros((tokens, D), BF16)

        @pl.when(top)
        def _():
            for g in range(heads):
                for m in range(2):
                    grad_in[m, g, OVER_Z] = jnp.zeros((tokens, D), BF16)

        blank = jnp.zeros((TILE, width), BF16)
        for ref in (shares_all, score_all):
            for g in range(heads):
                for i in range(0, tiles, 2):
                    ref[g, i * TILE : (i + 1) * TILE, (i + 1) * width : (i + 2) * width] = blank
                    ref[g, own + (i + 1) * TILE : own + (i + 2) * TILE, i * width : (i + 1) * width] = blank

    row_at = lax.broadcasted_iota(jnp.int32, (tokens, tokens), 0)
    col_at = lax.broadcasted_iota(jnp.int32, (tokens, tokens), 1)
    lower = jnp.where(row_at >= col_at, 1.0, 0.0).astype(BF16)
    place = b * tokens + lax.broadcasted_iota(jnp.int32, (tokens, 1), 0)
    counts = jnp.clip(place + 1, 1, ATTEND_WINDOW).astype(F32)

    def running_keys(g):
        own_sum[g] = jnp.dot(lower, key_true[g], preferred_element_type=F32)

    def smooth_keys(g):
        when(b >= 2, lambda: key_copy(g).wait_recv())
        far = jnp.dot(lower, raw_far[g], preferred_element_type=F32)
        mean = (own_sum[g] - far + far[tokens - 1 :, :] + total_near[0:1, cols(g)]) / counts
        smooth[g, own : own + tokens, :] = (key_true[g].astype(F32) - mean).astype(BF16)
        send_far(S, g)
        send_near(S, g)

    row = lax.broadcasted_iota(jnp.int32, (TILE, width), 0)
    lane = lax.rem(lax.broadcasted_iota(jnp.int32, (1, width), 1), TILE)
    unit = jnp.where(
        lax.broadcasted_iota(jnp.int32, (TILE, TILE), 0) == lax.broadcasted_iota(jnp.int32, (TILE, TILE), 1), 1.0, 0.0
    )

    def lanes_of(i):
        return slice(i * width, (i + 1) * width)

    def keys_of(part, i):
        return (slice(i * TILE, tokens), slice(tokens, own), slice(own, own + (i + 1) * TILE))[part]

    def attend(g, part):
        for i in range(tiles):
            at, lanes = keys_of(part, i), lanes_of(i)
            scores = contract_last(smooth[g, at, :], q_all[g, lanes, :])
            if part == 0:
                edge = jnp.where(row > lane, scores[:TILE], -jnp.inf)
                scores = edge if i == tiles - 1 else jnp.concatenate([edge, scores[TILE:]], 0)
            if part == 2:
                edge = jnp.where(row <= lane, scores[i * TILE :], -jnp.inf)
                scores = edge if i == 0 else jnp.concatenate([scores[: i * TILE], edge], 0)
            highest = jnp.maximum(jnp.max(scores, axis=0, keepdims=True), LOWEST)
            powers = jnp.exp2((scores - highest) * (scale * LOG2_E))
            shares_all[g, at, lanes] = powers.astype(BF16)
            stats[g, part, 0:1, lanes] = highest
            stats[g, part, 1:2, lanes] = jnp.sum(powers, axis=0, keepdims=True)

    def combine(g):
        present = (b >= 2, b >= 1, b >= 0)
        tops = [jnp.where(here, stats[g, part, 0:1, :], LOWEST) for part, here in enumerate(present)]
        highest = jnp.maximum(jnp.maximum(tops[0], tops[1]), tops[2])
        powers = [
            jnp.where(here, jnp.exp2((top - highest) * (scale * LOG2_E)), 0.0) for top, here in zip(tops, present)
        ]
        total = sum(power * stats[g, part, 1:2, :] for part, power in enumerate(powers))
        inverse = 1.0 / total
        for part in range(3):
            factor = powers[part] * inverse
            stats[g, part, 0:1, :] = factor.astype(BF16).astype(F32)
            for k in range(group * tiles):
                at = slice(k * TILE, (k + 1) * TILE)
                spread = (unit * factor[:, at]).astype(BF16)
                do_part[g, part, at, :] = jnp.dot(
                    spread, do_all[g, at, :], preferred_element_type=F32
                ).astype(BF16)

    def local_of(part, i):
        return slice(i * TILE, tokens) if part == 0 else slice(0, (i + 1) * TILE)

    def differentiate_early(g):
        for i in range(tiles):
            lanes, row_dot = lanes_of(i), 0.0
            for part in (0, 2):
                at = keys_of(part, i)
                share_grad = contract_last(value[g, at, :], do_part[g, part, lanes, :])
                early_grad[g, part // 2, local_of(part, i), lanes] = share_grad
                row_dot = row_dot + jnp.sum(shares_all[g, at, lanes].astype(F32) * share_grad, axis=0, keepdims=True)
            stats[g, 0, 1:2, lanes] = row_dot

    def differentiate(g):
        for i in range(tiles):
            lanes = lanes_of(i)
            at = keys_of(1, i)
            near_grad = contract_last(value[g, at, :], do_part[g, 1, lanes, :])
            near_shares = shares_all[g, at, lanes].astype(F32)
            row_dot = stats[g, 0, 1:2, lanes] + jnp.sum(near_shares * near_grad, axis=0, keepdims=True)
            score_all[g, at, lanes] = (near_shares * (near_grad - row_dot * stats[g, 1, 0:1, lanes])).astype(BF16)
            for part in (0, 2):
                at = keys_of(part, i)
                share_grad = early_grad[g, part // 2, local_of(part, i), lanes]
                shift = row_dot * stats[g, part, 0:1, lanes]
                score_all[g, at, lanes] = (shares_all[g, at, lanes].astype(F32) * (share_grad - shift)).astype(BF16)

    def key_grads(m, g, part, at, lanes):
        if m == 0:
            return jnp.dot(score_all[g, at, lanes], q_all[g, lanes, :], preferred_element_type=F32) * scale
        return jnp.dot(shares_all[g, at, lanes], do_part[g, part, lanes, :], preferred_element_type=F32)

    def near_grads(m, g):
        for p in range(PIECES):
            grads = key_grads(m, g, 1, rows_of(p, tokens), slice(0, group * tokens))
            grad_out[m, g, OVER_Y, rows_of(p)] = grads.astype(BF16)

    def send_near_grads(m, g):
        for p in range(PIECES):
            when(even & (b >= 2), lambda: grad_copy(m, g, OVER_Y, p, 1).start())
            when(odd, lambda: grad_copy(m, g, OVER_Y, p, -1).start())

    def far_grads(m, g):
        for p in range(PIECES):
            grads = key_grads(m, g, 0, rows_of(p), slice(0, (p + 1) * group * piece))
            far_grad[m, g, rows_of(p)] = grads

            @pl.when(even & (b >= 2))
            def _():
                grad_out[m, g, OVER_Z, rows_of(p)] = far_grad[m, g, rows_of(p)].astype(BF16)
                grad_copy(m, g, OVER_Z, p, -2).start()

    def join_grads(m, g):
        for p in range(PIECES):
            @pl.when(odd & (b >= 2))
            def _():
                grad_copy(m, g, OVER_Y, p, 1).wait_recv()
                both = far_grad[m, g, rows_of(p)] + grad_in[m, g, OVER_Y, rows_of(p)].astype(F32)
                grad_out[m, g, OVER_Z, rows_of(p)] = both.astype(BF16)
                grad_copy(m, g, OVER_Z, p, -2).start()

    def own_grads(m, g):
        for p in range(PIECES):
            own_grad[m, g, rows_of(p)] = key_grads(
                m, g, 2, rows_of(p, own), slice(p * group * piece, group * tokens)
            )

    def query_grads(g):
        smooth_t[...] = smooth[g].astype(F32).T.astype(BF16)
        for i in range(tiles):
            window = slice(i * TILE, i * TILE + SPAN)
            dq = jnp.dot(
                smooth_t[:, window], score_all[g, window, i * width : (i + 1) * width],
                preferred_element_type=F32,
            ) * scale
            dq = dq.T.astype(BF16)
            for u in range(group):
                dq_ref[i * TILE : (i + 1) * TILE, cols(g * group + u)] = dq[u * TILE : (u + 1) * TILE]

    def share_copy(m, g, p, t):
        at = (m, g) if p is None else (m, g, rows_of(p))
        last = (m, g) == (0, heads - 1) and t > 1
        received = s_last.at[t - 1, p] if last else s_recv.at[t - 1, m, g]
        return across(scaled.at[at], gathered.at[(t - 1,) + at], s_send.at[t - 1], received, t)

    def onward_copy(m, g, t, p=None):
        at = (m, g) if p is None else (m, g, rows_of(p))
        received = s_recv.at[t, m, g] if p is None else s_last.at[t, p]
        return across(gathered.at[(t - 1,) + at], gathered.at[(t,) + at], s_send.at[t], received, 1)

    def hops_of(m, g):
        return range(PIECES) if (m, g) == (0, heads - 1) else (None,)

    far_steps = list(range(2, nh, 2))

    def finish(m, g):
        exponent = (ke_in, ve_in)[m]
        for p in range(PIECES):
            when(even, lambda: grad_copy(m, g, OVER_Y, p, -1).wait_recv())
            when(b + 2 < n, lambda: grad_copy(m, g, OVER_Z, p, -2).wait_recv())
            for r in range(p * tiles // PIECES, (p + 1) * tiles // PIECES):
                at = slice(r * TILE, (r + 1) * TILE)
                whole = own_grad[m, g, at] + grad_in[m, g, OVER_Z, at].astype(F32)
                whole = whole + jnp.where(even, grad_in[m, g, OVER_Y, at].astype(F32), 0.0)
                scaled[m, g, at] = (whole * power_of_two(exponent[g : g + 1, r : r + 1])).astype(BF16)
            for t in far_steps + [1]:
                share_copy(m, g, p, t).start()

    def pass_on(m, g):
        for t in far_steps:
            for p in hops_of(m, g):
                share_copy(m, g, p, t).wait_recv()
                onward_copy(m, g, t, p).start()

    def await_core(g):
        for m in range(2):
            share_copy(m, g, None, 1).wait_recv()

    def await_onward(m, g):
        for t in far_steps:
            for p in hops_of(m, g):
                onward_copy(m, g, t, p).wait_recv()

    chunk = rows // CHUNKS

    def product(terms, fresh, base=0, count=CHUNKS):
        def one_chunk(k, carry):
            at = pl.ds(pl.multiple_of((base + k) * chunk, 16), chunk)
            left = jnp.concatenate([weights[t, m, at, cols(g)] for t, m, g in terms], 1)
            right = [scaled[m, g] if t == 0 else gathered[t - 1, m, g] for t, m, g in terms]
            total = contract_last(left, jnp.concatenate(right, 1))
            if not fresh:
                total = total + acc[at, :]
            acc[at, :] = total
            return carry

        lax.fori_loop(0, count, one_chunk, 0)

    def terms_of(ts, g):
        return [(t, m, g) for t in ts for m in range(2)]

    crossed = terms_of(crossing, 0) + [(t, 1, 1) for t in crossing]

    for copy in loads: copy.wait()
    for g in range(heads): true_keys(g)
    sum_keys()
    for g in range(heads): true_values(g)
    pl.semaphore_wait(barrier, greeted)
    when(b + 1 < n, lambda: near_sum().start())
    cross_thin().start()
    for j in range(len(chunks)): cross_copy(j).start()
    for g in range(heads): when(b + 2 < n, lambda: key_copy(g).start())
    for g in range(heads): send_near(V, g)
    for copy in head_loads: copy.start()
    for copy in core_copies + own_copies: copy.start()
    clear()
    for g in range(heads): running_keys(g)
    when(b >= 1, lambda: near_sum().wait_recv())
    smooth_keys(0)
    hand_thin()
    smooth_keys(1)
    for g in range(heads): send_far(V, g)
    raise_thin()
    for g in range(heads): await_heads(g)
    attend(0, 2)
    attend(1, 2)
    relay(S, 0)
    hand_on(0)
    await_far(S, 0)
    attend(0, 0)
    when(row_0, share_thin)
    relay(S, 1)
    await_far(S, 1)
    attend(1, 0)
    hand_on(1)
    await_near(S, 0)
    attend(0, 1)
    combine(0)
    relay(V, 0)
    near_grads(1, 0)
    when(even, lambda: send_near_grads(1, 0))
    far_grads(1, 0)
    relay(V, 1)
    when(odd, lambda: send_near_grads(1, 0))
    await_near(S, 1)
    attend(1, 1)
    hand_on(2)
    combine(1)
    near_grads(1, 1)
    send_near_grads(1, 1)
    far_grads(1, 1)
    await_far(V, 0)
    differentiate_early(0)
    await_near(V, 0)
    join_grads(1, 0)
    differentiate(0)
    near_grads(0, 0)
    send_near_grads(0, 0)
    hand_on(3)
    await_far(V, 1)
    differentiate_early(1)
    await_near(V, 1)
    join_grads(1, 1)
    differentiate(1)
    near_grads(0, 1)
    send_near_grads(0, 1)
    hand_on(4)
    when(b >= 2, share_thin)
    hand_top(lambda copy: copy.start())
    far_grads(0, 0)
    far_grads(0, 1)
    for m in (1, 0): own_grads(m, 0)
    join_grads(0, 0)
    finish(1, 0)
    for m in (1, 0): own_grads(m, 1)
    hand_on(5)
    finish(1, 1)
    join_grads(0, 1)
    hand_bottom(lambda copy: copy.start())
    query_grads(0)
    finish(0, 0)
    query_grads(1)
    pltpu.make_async_copy(weights.at[0], weights.at[0], w_own.at[0]).wait()
    across(weights.at[1], weights.at[1], c_send.at[0], c_recv.at[0], 1).wait_recv()
    finish(0, 1)
    await_core(0)
    product(terms_of((0, 1), 0), True)
    await_core(1)
    product(terms_of((0, 1), 1), False)
    for m, g in ((1, 0), (0, 0), (1, 1)): pass_on(m, g)
    for m, g in ((1, 0), (0, 0), (1, 1)): await_onward(m, g)
    await_thin()
    product(crossed, False, colour, 1)
    pass_on(0, 1)
    await_weights()
    product(crossed, False, 1 - colour, 1)
    await_onward(0, 1)

    when(b + 1 < n, lambda: near_sum().wait_send())
    when(b + 2 < n, lambda: along(key_true, key_true, kf_send.at[0], kf_recv.at[0], 2).wait_send())
    halo = value.at[:, 0:own]
    when(b + 2 < n, lambda: along(halo, halo, h_send.at[FAR], h_recv.at[0, 0, 0, FAR], 2).wait_send())
    when(even | (b >= 2), lambda: along(halo, halo, h_send.at[NEAR], h_recv.at[0, 0, 0, FAR], 2).wait_send())
    for over, condition in ((OVER_Y, odd | (b >= 2)), (OVER_Z, b >= 2)):
        ref = grad_out.at[:, :, over]
        when(condition, lambda: along(ref, ref, g_send.at[over], g_recv.at[0, 0, 0, 0], 2).wait_send())
    for t in range(1, nh):
        across(scaled, scaled, s_send.at[t - 1], s_recv.at[0, 0, 0], 1).wait_send()
    cross_thin().wait_send()
    thin_up().wait_send()
    thin_side(mine, 1).wait_send()
    thin_side(1 - mine, 2, 1 - colour).wait_send()
    sent = weights.at[0, :, 0 : len(chunks) * part // 2]
    across(sent, sent, w_send.at[0], w_recv.at[0], 1).wait_send()
    for at, condition, count in ((0, b >= 2, 2), (1, b + 2 < n, len(chunks) - 2), (2, row_0, len(chunks) - 3), (3, below_top, 1)):
        sent = weights.at[0, 0, 0 : count * part]
        when(condition, lambda: along(sent, sent, f_send.at[at], f_recv.at[0], 2).wait_send())
    hand_top(lambda copy: copy.wait_send())
    hand_bottom(lambda copy: copy.wait_send())
    across(weights.at[1], weights.at[1], c_send.at[0], c_recv.at[0], 1).wait_send()


def last_product(nh, heads, dq_ref, gathered, weights, acc, dq_out, grad_rows, out_ref, sem):
    rows = acc.shape[0]
    chunk = rows // LAST_CHUNKS
    g = heads - 1
    cols = slice(g * D, (g + 1) * D)
    query_copy = pltpu.make_async_copy(dq_ref, dq_out, sem.at[LAST_CHUNKS])
    query_copy.start()
    copies = []
    for c in range(LAST_CHUNKS):
        at = slice(c * chunk, (c + 1) * chunk)
        left = jnp.concatenate([weights[t, 0, at, cols] for t in range(2, nh)], 1)
        right = jnp.concatenate([gathered[t - 1, 0, g] for t in range(2, nh)], 1)
        total = acc[at, :] + contract_last(left, right)
        out_ref[at, :] = total.astype(BF16)
        copies.append(pltpu.make_async_copy(out_ref.at[at, :], grad_rows.at[at, :], sem.at[c]))
        copies[-1].start()
    query_copy.wait()
    for copy in copies:
        copy.wait()


def solution(mesh):
    n, nh = mesh.shape["seq"], mesh.shape["head"]
    assert n % 8 == 0 and nh == 4

    def local(q, k, v, do, ke, ve, wk, wv):
        tokens, width = k.shape
        heads = width // HEAD_SIZE
        assert heads == 2
        group = q.shape[1] // width
        tiles = tokens // TILE
        assert ATTEND_WINDOW == 2 * tokens
        rows = wk.shape[0] // nh
        n_chunks = 4 * (nh - 2)
        hbm = pl.BlockSpec(memory_space=pltpu.HBM)
        dma = pltpu.SemaphoreType.DMA
        vmem = pl.BlockSpec(memory_space=pltpu.VMEM)
        parts = pl.pallas_call(
            functools.partial(kernel, n, nh),
            out_shape=(
                pltpu.VMEM(q.shape, BF16),
                pltpu.VMEM((nh - 1, 2, heads, tokens, D), BF16),
                pltpu.VMEM((nh, 2, rows, width), BF16),
                pltpu.VMEM((rows, tokens), F32),
            ),
            in_specs=[hbm] * 8,
            out_specs=(vmem,) * 4,
            scratch_shapes=[
                pltpu.VMEM((tokens, width), BF16),
                pltpu.VMEM((tokens, width), BF16),
                pltpu.VMEM((heads, tiles), jnp.int32),
                pltpu.VMEM((heads, tiles), jnp.int32),
                pltpu.VMEM((heads, group * tokens, D), BF16),
                pltpu.VMEM((heads, group * tokens, D), BF16),
                pltpu.VMEM((heads, tokens, D), BF16),
                pltpu.VMEM((heads, tokens, D), BF16),
                pltpu.VMEM((heads, tokens, D), F32),
                pltpu.VMEM((8, width), F32),
                pltpu.VMEM((8, width), F32),
                pltpu.VMEM((heads, 3 * tokens, D), BF16),
                pltpu.VMEM((heads, 3 * tokens, D), BF16),
                pltpu.VMEM((D, 3 * tokens), BF16),
                pltpu.VMEM((heads, 3 * tokens, group * tokens), BF16),
                pltpu.VMEM((heads, 3 * tokens, group * tokens), BF16),
                pltpu.VMEM((heads, 3, 2, group * tokens), F32),
                pltpu.VMEM((heads, 3, group * tokens, D), BF16),
                pltpu.VMEM((heads, 2, tokens, group * tokens), F32),
                pltpu.VMEM((2, heads, tokens, D), F32),
                pltpu.VMEM((2, heads, tokens, D), F32),
                pltpu.VMEM((2, heads, 2, tokens, D), BF16),
                pltpu.VMEM((2, heads, 2, tokens, D), BF16),
                pltpu.VMEM((2, heads, tokens, D), BF16),
                dma((4,)), dma((heads, 2)), dma((1,)),
                dma((1,)), dma((heads,)), dma((1,)), dma((1,)),
                dma((2,)), dma((2, heads, PIECES, 2)),
                dma((2,)), dma((n_chunks - 1,)), dma((6,)), dma((n_chunks - 2,)), dma((3,)), dma((3,)),
                dma((1,)), dma((1,)),
                dma((2,)), dma((2, heads, 2, PIECES)),
                dma((nh - 1,)), dma((nh - 1, 2, heads)), dma((nh - 1, PIECES)),
            ],
            compiler_params=pltpu.CompilerParams(
                collective_id=0, has_side_effects=True, vmem_limit_bytes=48 * 2**20
            ),
        )(*[pltpu.with_memory_space_constraint(x, pltpu.HBM) for x in (q, k, v, do, ke.T, ve.T, wk, wv)])
        return pl.pallas_call(
            functools.partial(last_product, nh, heads),
            out_shape=(
                jax.ShapeDtypeStruct(q.shape, BF16),
                jax.ShapeDtypeStruct((rows, tokens), BF16),
            ),
            in_specs=[vmem] * 4,
            out_specs=(pl.BlockSpec(memory_space=pl.ANY),) * 2,
            scratch_shapes=[pltpu.VMEM((rows, tokens), BF16), dma((LAST_CHUNKS + 1,))],
            compiler_params=pltpu.CompilerParams(vmem_limit_bytes=24 * 2**20),
        )(*[pltpu.with_memory_space_constraint(x, pltpu.VMEM) for x in parts])

    in_specs = (P("seq", "head"),) * 6 + (P(None, "head"),) * 2
    out_specs = (P("seq", "head"), P("head", "seq"))
    return jax.shard_map(local, mesh=mesh, in_specs=in_specs, out_specs=out_specs, check_vma=False)
```
